32 devices in a mesh: grp: 2 (over y), user: 4 (over z), tm: 4 (over x, core).
Axes of the slice: x: 2, y: 2, z: 4, core: 2. Of those that a mesh axis runs over, the one named last changes fastest.
Arguments:
- history: bfloat16 [8, 1024, 512], P(('grp', 'user'), 'tm'), parts along dimension 0, may hold values from -6 to 6
- z_weight: bfloat16 [512, 1024], replicated, may hold values from -0.25 to 0.25
- xbc_weight: bfloat16 [512, 1280], replicated, may hold values from -0.25 to 0.25
- dt_weight: bfloat16 [512, 16], replicated, may hold values from -0.125 to 0.125
- dt_bias: float32 [16], replicated, may hold values from -1 to 0.5
- a_log: float32 [16], replicated
- conv_weight: float32 [4, 1280], replicated, may hold values from -3 to 3
- conv_bias: float32 [1280], replicated, may hold values from -3 to 3
- d_skip: float32 [16], replicated, may hold values from 0.5 to 1.5
- norm_gain: float32 [1024], replicated, may hold values from 0.1 to 1.9
- out_weight: bfloat16 [1024, 512], replicated, may hold values from -0.1875 to 0.1875
- label_pos: int32 [8, 2048], P(('grp', 'user'), 'tm'), parts along dimension 0, may hold values from 0 to 1023, as said below
- label_count: int32 [8, 4], P(('grp', 'user'), 'tm'), parts along dimension 0, may hold values from 1 to 511, as said below
- label_value: int32 [8, 2048], P(('grp', 'user'), 'tm'), parts along dimension 0, may hold values 0 or 1
- item_feat: bfloat16 [8, 2048, 512], P(('grp', 'user'), 'tm'), parts along dimension 0, may hold values from -6 to 6
- first_weight: bfloat16 [1024, 1024], replicated, may hold values from -0.1875 to 0.1875
- second_weight: bfloat16 [1024], replicated, may hold values from -0.1875 to 0.1875
Outputs:
- encoded: bfloat16 [8, 1024, 512], P(('grp', 'user'), 'tm'), parts along dimension 0
- row_logit: float32 [8, 2048], P(('grp', 'user'), 'tm'), parts along dimension 0
- grad_first: float32 [2048, 1024], P('grp'), parts along dimension 0
- grad_second: float32 [2048], P('grp'), parts along dimension 0
The draws below stay inside these ranges and needn't reach their ends.
There are 2 independent parts, one for each index of `grp`. The reference program is written for one: setup_inputs(seed, part) draws one part's arguments, and reference() takes and returns one part's arrays. A program takes and returns all parts, laid end to end along the dimension named above; an argument that names none is the same for every part. Nothing has to cross between parts.
Inputs may be any that keep to these rules, and one draw needn't show every extreme that they name: `label_pos`: positions in slots k * 512 to (k + 1) * 512 - 1 of a user lie in events k * 256 to (k + 1) * 256 - 1. label_count[u, k] slots are used in block k of user u's slots, and they are the block's first ones; the counts of blocks 2 * k and 2 * k + 1 of a user sum to 512.
All inputs are finite; a program needn't handle non-finite values. No bound on the sum of `label_value` on one device may be relied on, other than what follows from the above.
Results may differ from the reference program's by a relative error of at most 0.015.
Values may be sent and summed in bfloat16 or wider, within the bound.
No kernel may reach another device: no remote copies, remote signals or barrier semaphores. Data moves between devices by JAX's collectives and lax.ppermute only.
A program may use at most 64 MiB of HBM per device.

```python
import jax
import jax.numpy as jnp
from jax import lax

D = 512
HEADS = 16
HDIM = 64
DSTATE = 128
CONV = 4
BLOCK = 256
HID = 1024
L_DEV = 256
DINNER = 1024
XBC = 1280
LENGTH = 1024
USERS = 4
LAB_DEV = 512
SLOTS = 2048
N_TM = 4


def draw_a_log(key, part):
    pick_key, fast_key, slow_key = jax.random.split(key, 3)
    portion = 0.5
    slow_heads = jax.random.uniform(pick_key, (HEADS,)) < portion
    fast_rate = jax.random.uniform(fast_key, (HEADS,), minval=0.04, maxval=0.08)
    slow_rate = jax.random.uniform(slow_key, (HEADS,), minval=0.2, maxval=1.0) / LENGTH
    return jnp.log(jnp.where(slow_heads, slow_rate, fast_rate)).astype(jnp.float32)


def draw_label_pos(key, part):
    offsets = jax.random.randint(key, (USERS, SLOTS), 0, L_DEV)
    starts = jnp.arange(SLOTS, dtype=jnp.int32) // LAB_DEV * L_DEV
    places = offsets + starts[None, :]
    places = places.at[:, 0].set(0)
    places = places.at[:, SLOTS - 1].set(LENGTH - 1)
    return places.astype(jnp.int32)


def draw_label_count(key, part):
    pair_count = N_TM // 2
    first_key, forced_key, side_key = jax.random.split(jax.random.fold_in(key, 17), 3)
    first = jax.random.randint(first_key, (USERS, pair_count), 1, LAB_DEV)
    forced = jax.random.randint(forced_key, (USERS,), 0, pair_count)
    side = jax.random.randint(side_key, (USERS,), 0, 2)
    extreme = jnp.where(side == 1, LAB_DEV - 1, 1)
    pair_iota = jnp.arange(pair_count, dtype=jnp.int32)
    first = jnp.where(pair_iota[None, :] == forced[:, None], extreme[:, None], first)
    paired = jnp.stack([first, LAB_DEV - first], axis=2)
    return paired.reshape(USERS, N_TM).astype(jnp.int32)


def plant(drawn, stream_key, low, top_value):
    extent = drawn.shape
    index_at = [jax.random.randint(jax.random.fold_in(stream_key, axis), (), 0, extent[axis]) for axis in range(len(extent))]
    drawn = drawn.at[tuple(index_at)].set(low)
    longest = extent.index(max(extent))
    index_at[longest] = (index_at[longest] + 1) % extent[longest]
    return drawn.at[tuple(index_at)].set(top_value)


def shard_levels(own_key, extent, shards, low, top_value):
    def one(dim, parts):
        steps = jax.random.uniform(jax.random.fold_in(jax.random.fold_in(own_key, 6), dim), (parts,), jnp.float32, low / len(shards), top_value / len(shards))
        return jnp.repeat(jnp.exp(steps), extent[dim] // parts).reshape((-1,) + (1,) * (len(extent) - dim - 1))

    factor_of = one(*shards[0])
    for cut in shards[1:]:
        factor_of = factor_of * one(*cut)
    return factor_of


def gaussian(stream_key, dims, spread, most, cuts=(), held_as=jnp.bfloat16):
    loudness = shard_levels(stream_key, dims, cuts, -0.22, 0.18) if cuts else 1.0
    values = jax.random.normal(stream_key, dims, jnp.float32) * spread * loudness
    return jnp.minimum(jnp.maximum(values, -most), most).astype(held_as)


def setup_inputs(seed: int = 0, part: int = 0) -> dict:
    seeds = jax.random.split(jax.random.key(seed), 18)
    own_keys = jax.random.split(jax.random.fold_in(seeds[17], part), 18)
    return {
        "history": gaussian(own_keys[0], (USERS, LENGTH, D), 1.0, 6.0, ((0, 4), (1, 4))),
        "z_weight": gaussian(seeds[1], (D, DINNER), D ** -0.5, 0.25),
        "xbc_weight": gaussian(seeds[2], (D, XBC), D ** -0.5, 0.25),
        "dt_weight": gaussian(seeds[3], (D, HEADS), (4 * D) ** -0.5, 0.125),
        "dt_bias": jnp.clip(jax.random.uniform(seeds[4], (HEADS,), jnp.float32, -1.0, 0.5), -1.0, 0.5),
        "a_log": draw_a_log(jax.random.fold_in(seeds[17], 71), part),
        "conv_weight": gaussian(seeds[6], (CONV, XBC), 0.5, 3.0, (), jnp.float32),
        "conv_bias": gaussian(seeds[7], (XBC,), 0.5, 3.0, (), jnp.float32),
        "d_skip": jnp.clip(jax.random.uniform(seeds[8], (HEADS,), jnp.float32, 0.5, 1.5), 0.5, 1.5),
        "norm_gain": jnp.clip(1.0 + 0.18 * jax.random.normal(seeds[9], (DINNER,), jnp.float32), 0.1, 1.9),
        "out_weight": gaussian(seeds[10], (DINNER, D), DINNER ** -0.5, 0.1875),
        "label_pos": draw_label_pos(jax.random.fold_in(jax.random.fold_in(seeds[17], part), 71), part),
        "label_count": draw_label_count(jax.random.fold_in(jax.random.fold_in(seeds[17], part), 71), part),
        "label_value": plant((jax.random.randint(own_keys[13], (USERS, SLOTS), 0, 2) < 1).astype(jnp.int32), jax.random.fold_in(own_keys[13], 1), 0, 1),
        "item_feat": gaussian(own_keys[14], (USERS, SLOTS, D), 1.0, 6.0, ((0, 4), (1, 4))),
        "first_weight": gaussian(seeds[15], (2 * D, HID), (2 * D) ** -0.5, 0.1875),
        "second_weight": gaussian(seeds[16], (HID,), HID ** -0.5, 0.1875),
    }


def silu_grad(values):
    sig = jax.nn.sigmoid(values)
    return sig * (1.0 + values * (1.0 - sig))

def ranker(rank_rows, target, live_mask, first_weight, second_weight):
    pre_act = jnp.dot(rank_rows, first_weight, preferred_element_type=jnp.float32)
    hidden = jax.nn.silu(pre_act).astype(jnp.bfloat16)
    logit_vec = jnp.dot(hidden, second_weight, preferred_element_type=jnp.float32)
    dlogit = live_mask * (jax.nn.sigmoid(logit_vec) - target)
    grad_two = jnp.dot(dlogit, hidden.astype(jnp.float32), precision=lax.Precision.HIGHEST)
    grad_pre = (dlogit[:, None] * second_weight.astype(jnp.float32)[None, :] * silu_grad(pre_act)).astype(jnp.bfloat16)
    grad_one = jnp.dot(rank_rows.T, grad_pre, preferred_element_type=jnp.float32)
    return (live_mask * logit_vec, grad_one, grad_two)

def encode_user(history_user, z_weight, xbc_weight, dt_weight, dt_bias, a_log, conv_weight, conv_bias, d_skip, norm_gain, out_weight):
    z_gate = jnp.dot(history_user, z_weight, preferred_element_type=jnp.float32).astype(jnp.bfloat16)
    xbc_raw = jnp.dot(history_user, xbc_weight, preferred_element_type=jnp.float32).astype(jnp.bfloat16)
    step_size = jax.nn.softplus(jnp.dot(history_user, dt_weight, preferred_element_type=jnp.float32) + dt_bias)
    padded = jnp.concatenate([jnp.zeros((CONV - 1, XBC), jnp.bfloat16), xbc_raw], axis=0)
    conv_sum = jnp.zeros((LENGTH, XBC), jnp.float32) + conv_bias[None, :]
    for tap in range(CONV):
        conv_sum = conv_sum + conv_weight[tap][None, :] * padded[tap:tap + LENGTH].astype(jnp.float32)
    xbc = jax.nn.silu(conv_sum).astype(jnp.bfloat16)
    block_count = LENGTH // BLOCK
    x_part = xbc[:, :DINNER].reshape(block_count, BLOCK, HEADS, HDIM)
    b_part = xbc[:, DINNER:DINNER + DSTATE].reshape(block_count, BLOCK, DSTATE)
    c_part = xbc[:, DINNER + DSTATE:].reshape(block_count, BLOCK, DSTATE)
    log_decay = (-jnp.exp(a_log)[None, :] * step_size).reshape(block_count, BLOCK, HEADS)
    cumulated = jnp.cumsum(log_decay, axis=1)
    step_blocks = step_size.reshape(block_count, BLOCK, HEADS)
    rows_idx = lax.broadcasted_iota(jnp.int32, (BLOCK, BLOCK), 0)
    cols_idx = lax.broadcasted_iota(jnp.int32, (BLOCK, BLOCK), 1)
    causal = (cols_idx <= rows_idx)[None]

    def block_step(carry_state, inputs):
        x_block, b_block, c_block, cum_block, step_block = inputs
        scores = jnp.dot(c_block, b_block.T, preferred_element_type=jnp.float32)
        cum_heads = cum_block.T
        gaps = cum_heads[:, :, None] - cum_heads[:, None, :]
        decays = jnp.where(causal, jnp.exp(jnp.where(causal, gaps, 0.0)), 0.0)
        weights = (decays * step_block.T[:, None, :] * scores[None]).astype(jnp.bfloat16)
        within = jnp.einsum('hts,shp->thp', weights.astype(jnp.float32), x_block.astype(jnp.float32))
        last_cum = cum_block[-1]
        across = jnp.exp(cum_block)[:, :, None] * jnp.einsum('tn,hpn->thp', c_block.astype(jnp.float32), carry_state, precision=lax.Precision.HIGHEST)
        carried = ((jnp.exp(last_cum[None, :] - cum_block) * step_block)[:, :, None] * x_block.astype(jnp.float32)).astype(jnp.bfloat16)
        new_state = jnp.exp(last_cum)[:, None, None] * carry_state + jnp.einsum('shp,sn->hpn', carried.astype(jnp.float32), b_block.astype(jnp.float32))
        result = within + across + d_skip[None, :, None] * x_block.astype(jnp.float32)
        return (new_state, result)
    zero_state = jnp.zeros((HEADS, HDIM, DSTATE), jnp.float32)
    final_state, ssd_out = lax.scan(block_step, zero_state, (x_part, b_part, c_part, cumulated, step_blocks))
    ssd_out = ssd_out.reshape(LENGTH, DINNER)
    gated_out = ssd_out * jax.nn.silu(z_gate.astype(jnp.float32))
    normed = (gated_out * lax.rsqrt(lax.optimization_barrier(jnp.mean(gated_out * gated_out, axis=-1, keepdims=True)) + 1e-05) * norm_gain[None, :]).astype(jnp.bfloat16)
    return jnp.dot(normed, out_weight, preferred_element_type=jnp.float32).astype(jnp.bfloat16)

def reference(history, z_weight, xbc_weight, dt_weight, dt_bias, a_log, conv_weight, conv_bias, d_skip, norm_gain, out_weight, label_pos, label_count, label_value, item_feat, first_weight, second_weight):
    slot_ids = jnp.arange(SLOTS).astype(jnp.int32)

    def per_user(carry, inputs):
        history_user, pos_user, count_user, value_user, item_user = inputs
        encoded_user = encode_user(history_user, z_weight, xbc_weight, dt_weight, dt_bias, a_log, conv_weight, conv_bias, d_skip, norm_gain, out_weight)
        enc_rows = encoded_user[pos_user]
        rank_rows = jnp.concatenate([enc_rows, item_user], axis=-1)
        live_mask = (slot_ids % LAB_DEV < count_user[slot_ids // LAB_DEV]).astype(jnp.float32)
        logit_vec, grad_one, grad_two = ranker(rank_rows, value_user.astype(jnp.float32), live_mask, first_weight, second_weight)
        return ((carry[0] + grad_one, carry[1] + grad_two), (encoded_user, logit_vec))
    start = (jnp.zeros((2 * D, HID), jnp.float32), jnp.zeros((HID,), jnp.float32))
    grads, outputs = lax.scan(per_user, start, (history, label_pos, label_count, label_value, item_feat))
    return (outputs[0], outputs[1], grads[0], grads[1])
```

```python
import functools

import jax
import jax.numpy as jnp
from jax import lax
from jax.experimental import pallas as pl
from jax.experimental.pallas import tpu as pltpu
from jax.sharding import PartitionSpec as P

F32 = jnp.float32
BF16 = jnp.bfloat16
LANES = 128
ALIGN = 16
VMEM = pl.BlockSpec(memory_space=pltpu.VMEM)
SMEM = pl.BlockSpec(memory_space=pltpu.SMEM)
LIMIT = 56 * 1024 * 1024


def dot(a, b):
    return jnp.dot(a, b, preferred_element_type=F32)


def dot_nt(a, b):
    return lax.dot_general(a, b, (((1,), (1,)), ((), ())), preferred_element_type=F32)


def dot_tn(a, b):
    return lax.dot_general(a, b, (((0,), (0,)), ((), ())), preferred_element_type=F32)


def split3(v):
    high = v.astype(BF16)
    rest = v - high.astype(F32)
    mid = rest.astype(BF16)
    low = (rest - mid.astype(F32)).astype(BF16)
    return high, mid, low


def spread(cols, first_head, head_size, rows):
    lane = lax.broadcasted_iota(jnp.int32, (rows, LANES), 1)
    out = jnp.broadcast_to(cols[:, first_head : first_head + 1], (rows, LANES))
    for k in range(1, LANES // head_size):
        nxt = cols[:, first_head + k : first_head + k + 1]
        out = jnp.where(lane >= k * head_size, nxt, out)
    return out


def scan_kernel(
    heads, halo, hist, w, dtw, dtb, alog, cw, cb, xbc, dt_o, cum_o, dt_t, cum_t, pay, raw, carried
):
    length = hist.shape[0]
    edge = halo.shape[0]
    taps = cw.shape[0]
    width = xbc.shape[1]
    inner = carried.shape[1]
    state = (width - inner) // 2
    head_size = inner // heads
    per = LANES // head_size
    rows = jnp.concatenate([halo[...], hist[...]], axis=0)

    v = dot_nt(hist[...], dtw[...]) + dtb[...]
    dt = jnp.maximum(v, 0.0) + jnp.log1p(jnp.exp(-jnp.abs(v)))
    decay = -jnp.exp(alog[...]) * dt
    ri = lax.broadcasted_iota(jnp.int32, (length, length), 0)
    ci = lax.broadcasted_iota(jnp.int32, (length, length), 1)
    tri = jnp.where(ci <= ri, 1.0, 0.0).astype(BF16)
    parts = split3(decay)
    cum = dot(tri, parts[0]) + (dot(tri, parts[1]) + dot(tri, parts[2]))
    dt_o[...] = dt
    cum_o[...] = cum
    dt_t[...] = dt.T
    cum_t[...] = cum.T
    last = cum[length - 1 : length, :]
    weight = jnp.exp(last - cum) * dt

    step = 2 * LANES
    for start in list(range(inner, width, step)) + list(range(0, inner, step)):
        cols = slice(start, start + step)
        piece = dot(rows, w[:, cols]).astype(BF16).astype(F32)
        raw[:, cols] = piece
        acc = jnp.broadcast_to(cb[:, cols], (length, step))
        for k in range(taps):
            acc = acc + cw[k : k + 1, cols] * raw[pl.ds(edge - (taps - 1) + k, length), cols]
        xbc[:, cols] = (acc / (1.0 + jnp.exp(-acc))).astype(BF16)
    for start in range(0, inner, LANES):
        cols = slice(start, start + LANES)
        x = xbc[:, cols].astype(F32)
        carried[:, cols] = (
            spread(weight, start // LANES * per, head_size, length) * x
        ).astype(BF16)
    b = xbc[:, inner : inner + state]
    pay[:state, :] = dot_tn(b, carried[...]).astype(BF16)
    gain = jnp.broadcast_to(jnp.exp(last), (ALIGN, heads))
    pick = lax.broadcasted_iota(jnp.int32, (ALIGN, LANES), 0)
    for start in range(0, inner, LANES):
        g = spread(gain, start // LANES * per, head_size, ALIGN)
        high = g.astype(BF16).astype(F32)
        pay[state:, start : start + LANES] = jnp.where(
            pick == 0, high, jnp.where(pick == 1, g - high, 0.0)
        ).astype(BF16)


def gain_row(pay, state):
    tail = pay[state:, :].astype(F32)
    return tail[0:1, :] + tail[1:2, :]


def chip_kernel(where_am_i, mine, other, out, gain_out):
    state = out.shape[0]
    odd = where_am_i[0] == 1
    m = mine[:state, :].astype(F32)
    o = other[:state, :].astype(F32)
    gm = gain_row(mine, state)
    go = gain_row(other, state)
    out[...] = jnp.where(odd, o * gm + m, m * go + o).astype(BF16)
    gain_out[...] = jnp.broadcast_to(gm * go, gain_out.shape)


def within_kernel(heads, d_skip, hist, zw, xbc, cum, dt_t, cum_t, item, first_low, part, gate, pre):
    length = hist.shape[0]
    inner = zw.shape[1]
    state = (xbc.shape[1] - inner) // 2
    head_size = inner // heads
    per = LANES // head_size
    b = xbc[:, inner : inner + state]
    c = xbc[:, inner + state :]
    scores = dot_nt(c, b)
    half = length // 2
    tops = lax.broadcasted_iota(jnp.int32, (half, half), 0)
    lefts = lax.broadcasted_iota(jnp.int32, (half, half), 1)
    low_tri = lefts <= tops
    lane = lax.broadcasted_iota(jnp.int32, (length, LANES), 1)
    for start in range(0, inner, LANES):
        cols = slice(start, start + LANES)
        x = xbc[:, cols]
        out = None
        for k in range(per):
            h = start // LANES * per + k
            row = cum_t[h : h + 1, :]
            col = cum[:, h : h + 1]
            dts = dt_t[h : h + 1, :]

            def block(r, s, masked):
                gap = col[r : r + half] - row[:, s : s + half]
                if masked:
                    gap = jnp.where(low_tri, gap, 0.0)
                d = jnp.exp(gap)
                if masked:
                    d = jnp.where(low_tri, d, 0.0)
                return (d * dts[:, s : s + half] * scores[r : r + half, s : s + half]).astype(BF16)

            upper = dot(block(0, 0, True), x[:half])
            lower = dot(block(half, 0, False), x[:half]) + dot(block(half, half, True), x[half:])
            got = jnp.concatenate([upper, lower], axis=0)
            skip = d_skip[h]
            got = got + skip * x.astype(F32)
            out = got if out is None else jnp.where(lane >= k * head_size, got, out)
        part[:, cols] = out
    step = 2 * LANES
    for start in range(0, inner, step):
        cols = slice(start, start + step)
        z = dot(hist[...], zw[:, cols]).astype(BF16).astype(F32)
        gate[:, cols] = z / (1.0 + jnp.exp(-z))
    for start in range(0, pre.shape[1], step):
        cols = slice(start, start + step)
        pre[:, cols] = dot(item[...], first_low[:, cols])


def rank_kernel(
    heads,
    where_am_i,
    count,
    incoming,
    other,
    xbc,
    cum,
    part,
    gate,
    gain,
    ow,
    pos,
    value,
    item,
    pre,
    first_high,
    second,
    enc_o,
    logit_o,
    send_o,
    keep_o,
    gated_s,
    rank_s,
    slope_s,
    hid_s,
    gp_s,
):
    length, inner = part.shape
    state = incoming.shape[0]
    head_size = inner // heads
    per = LANES // head_size
    slots = pos.shape[1]
    odd = where_am_i[0] == 1
    base = where_am_i[1]
    arrived = incoming[...].astype(F32)
    enter = jnp.where(
        odd, arrived * gain_row(other, state) + other[:state, :].astype(F32), arrived
    )
    high = enter.astype(BF16)
    low = (enter - high.astype(F32)).astype(BF16)
    c = xbc[:, inner + state :]
    grow = jnp.exp(cum[...])
    total = jnp.zeros((length, LANES), F32)
    for start in range(0, inner, LANES):
        cols = slice(start, start + LANES)
        read = dot(c, high[:, cols]) + dot(c, low[:, cols])
        y = part[:, cols] + spread(grow, start // LANES * per, head_size, length) * read
        y = y * gate[:, cols]
        gated_s[:, cols] = y
        total = total + y * y
    mean = jnp.sum(total, axis=1, keepdims=True) * (1.0 / inner)
    scale = lax.rsqrt(mean + 1e-05)
    normed = (gated_s[...] * scale * gain[...]).astype(BF16)
    enc = dot(normed, ow[...]).astype(BF16)
    enc_o[...] = enc
    width = enc.shape[1]
    place = pos[...] - base
    hot = (lax.broadcasted_iota(jnp.int32, (length, slots), 0) == place).astype(F32).astype(BF16)
    rank_s[...] = dot_tn(hot, enc).astype(BF16)

    hidden_width = pre.shape[1]
    step = 2 * LANES
    logit = jnp.zeros((slots, LANES), F32)
    for start in range(0, hidden_width, step):
        cols = slice(start, start + step)
        v = pre[:, cols] + dot(rank_s[...], first_high[:, cols])
        sig = 1.0 / (1.0 + jnp.exp(-v))
        hid = (v * sig).astype(BF16)
        hid_s[:, cols] = hid
        w2 = second[:, cols].astype(F32)
        prod = hid.astype(F32) * w2
        for k in range(0, step, LANES):
            logit = logit + prod[:, k : k + LANES]
        slope_s[:, cols] = w2 * (sig * (1.0 + v * (1.0 - sig)))
    ones = jnp.ones((8, LANES), BF16)
    p = split3(logit)
    logit8 = dot_nt(ones, p[0]) + (dot_nt(ones, p[1]) + dot_nt(ones, p[2]))
    slot = lax.broadcasted_iota(jnp.int32, (8, slots), 1)
    live = jnp.where(slot < count[0, 0], 1.0, 0.0)
    logit_o[...] = (live * logit8)[0:1, :]
    target = value[...].astype(F32)
    dl = live * (1.0 / (1.0 + jnp.exp(-logit8)) - target)
    d0, d1, d2 = split3(dl)
    which = lax.broadcasted_iota(jnp.int32, (8, slots), 0)
    dl3 = jnp.where(
        which == 0,
        d0.astype(F32),
        jnp.where(which == 1, d1.astype(F32), jnp.where(which == 2, d2.astype(F32), 0.0)),
    ).astype(BF16)
    grad2 = jnp.sum(dot(dl3, hid_s[...]), axis=0, keepdims=True)
    dcol = dot_tn(dl3, jnp.ones((8, LANES), BF16))
    for start in range(0, hidden_width, LANES):
        cols = slice(start, start + LANES)
        gp_s[:, cols] = (dcol * slope_s[:, cols]).astype(BF16)
    rows = width
    pick = lax.broadcasted_iota(jnp.int32, (8, hidden_width), 0)
    extra = jnp.where(pick == 0, grad2, 0.0).astype(BF16)
    away = jnp.where(odd, rank_s[...], item[...])
    home = jnp.where(odd, item[...], rank_s[...])
    send_o[:rows, :] = dot_tn(away, gp_s[...]).astype(BF16)
    send_o[rows:, :] = extra
    keep_o[:rows, :] = dot_tn(home, gp_s[...]).astype(BF16)
    keep_o[rows:, :] = extra


def call(kernel, out_shape, in_specs, scratch, args, flops, moved):
    return pl.pallas_call(
        kernel,
        out_shape=out_shape,
        in_specs=in_specs,
        out_specs=jax.tree.map(lambda _: VMEM, out_shape),
        scratch_shapes=scratch,
        compiler_params=pltpu.CompilerParams(vmem_limit_bytes=LIMIT),
        cost_estimate=pl.CostEstimate(flops=flops, bytes_accessed=moved, transcendentals=0),
    )(*args)


def shape(dims, dtype):
    return jax.ShapeDtypeStruct(dims, dtype)


def bits_of(n):
    return max(n.bit_length() - 1, 0)


def body(
    history,
    z_weight,
    xbc_weight,
    dt_weight,
    dt_bias,
    a_log,
    conv_weight,
    conv_bias,
    d_skip,
    norm_gain,
    out_weight,
    label_pos,
    label_count,
    label_value,
    item_feat,
    first_weight,
    second_weight,
):
    hist = history[0]
    item = item_feat[0]
    length, width = hist.shape
    inner = z_weight.shape[1]
    heads = a_log.shape[0]
    channels = xbc_weight.shape[1]
    state = (channels - inner) // 2
    slots = label_pos.shape[1]
    hidden = first_weight.shape[1]
    n_tm = lax.axis_size("tm")
    n_user = lax.axis_size("user")
    chips = n_tm // 2
    tm = lax.axis_index("tm")
    user = lax.axis_index("user")
    odd = tm % 2
    where_am_i = jnp.stack([odd, tm * length]).astype(jnp.int32)

    halo = lax.ppermute(hist[length - ALIGN :], "tm", [(i, i + 1) for i in range(n_tm - 1)])
    xbc, dt, cum, dt_t, cum_t, pay = call(
        functools.partial(scan_kernel, heads),
        (
            shape((length, channels), BF16),
            shape((length, heads), F32),
            shape((length, heads), F32),
            shape((heads, length), F32),
            shape((heads, length), F32),
            shape((state + ALIGN, inner), BF16),
        ),
        [VMEM] * 8,
        [pltpu.VMEM((length + ALIGN, channels), F32), pltpu.VMEM((length, inner), BF16)],
        (
            halo,
            hist,
            xbc_weight,
            dt_weight.T,
            dt_bias.reshape(1, heads),
            a_log.reshape(1, heads),
            conv_weight,
            conv_bias.reshape(1, channels),
        ),
        2 * length * width * channels,
        4 * width * channels,
    )
    other = lax.ppermute(pay, "tm", [(i, i ^ 1) for i in range(n_tm)])
    chip_state, chip_gain = call(
        chip_kernel,
        (shape((state, inner), BF16), shape((8, inner), F32)),
        [SMEM, VMEM, VMEM],
        [],
        (where_am_i, pay, other),
        state * inner,
        6 * state * inner,
    )
    onward = [(i, i + 2) for i in range(n_tm - 2)]
    incoming = lax.ppermute(chip_state, "tm", onward)
    for _ in range(chips - 2):
        passed = chip_gain[0:1] * incoming.astype(F32) + chip_state.astype(F32)
        incoming = lax.ppermute(passed.astype(BF16), "tm", onward)
    part, gate, pre = call(
        functools.partial(within_kernel, heads),
        (
            shape((length, inner), F32),
            shape((length, inner), F32),
            shape((slots, hidden), F32),
        ),
        [SMEM] + [VMEM] * 8,
        [],
        (d_skip, hist, z_weight, xbc, cum, dt_t, cum_t, item, first_weight[width:]),
        2 * length * width * inner + 2 * slots * width * hidden + 4 * length * length * inner,
        16 * length * inner * 4,
    )
    enc, row_logit, send, keep = call(
        functools.partial(rank_kernel, heads),
        (
            shape((length, width), BF16),
            shape((1, slots), F32),
            shape((width + 8, hidden), BF16),
            shape((width + 8, hidden), BF16),
        ),
        [SMEM, SMEM] + [VMEM] * 14,
        [
            pltpu.VMEM((length, inner), F32),
            pltpu.VMEM((slots, width), BF16),
            pltpu.VMEM((slots, hidden), F32),
            pltpu.VMEM((slots, hidden), BF16),
            pltpu.VMEM((slots, hidden), BF16),
        ],
        (
            where_am_i,
            label_count,
            incoming,
            other,
            xbc,
            cum,
            part,
            gate,
            norm_gain.reshape(1, inner),
            out_weight,
            label_pos,
            label_value,
            item,
            pre,
            first_weight[:width],
            second_weight.reshape(1, hidden),
        ),
        4 * slots * width * hidden,
        8 * slots * hidden,
    )
    grad_first, grad_second = total_sum(send, keep, n_user, n_tm, user, tm)
    return (enc[None], row_logit, grad_first, grad_second)


def total_sum(send, keep, n_user, n_tm, user, tm):
    rows = keep.shape[0] - 8
    odd = tm % 2
    axes = ("user", "tm")
    every = [(u, t) for u in range(n_user) for t in range(n_tm)]

    def swap(value, partner):
        pairs = [(u * n_tm + t, partner(u, t)) for u, t in every]
        return lax.ppermute(value, axes, pairs)

    chip_bits = [("tm", k) for k in range(bits_of(n_tm // 2))]
    user_bits = [("user", k) for k in range(bits_of(n_user))]
    order_even = chip_bits + user_bits
    order_odd = user_bits + chip_bits

    def partner_of(level):
        def partner(u, t):
            axis, k = (order_even if t % 2 == 0 else order_odd)[level]
            if axis == "tm":
                return u * n_tm + (t ^ (2 << k))
            return (u ^ (1 << k)) * n_tm + t

        return partner

    def bit_of(level):
        def one(entry):
            axis, k = entry
            return (tm >> (k + 1)) & 1 if axis == "tm" else (user >> k) & 1

        return jnp.where(odd == 0, one(order_even[level]), one(order_odd[level])) == 1

    got = swap(send, lambda u, t: u * n_tm + (t ^ 1))
    levels = len(order_even)
    size = rows
    extra_a, extra_b = keep[rows:].astype(F32), got[rows:].astype(F32)
    main_a, main_b = keep[:rows], got[:rows]
    extra = (extra_a + extra_b).astype(BF16)
    for level in range(levels):
        size //= 2
        bit = bit_of(level)
        low = main_a[:size].astype(F32) + main_b[:size].astype(F32)
        high = main_a[size:].astype(F32) + main_b[size:].astype(F32)
        leave = jnp.where(bit, low, high).astype(BF16)
        main_a = jnp.where(bit, high, low).astype(BF16)
        got = swap(jnp.concatenate([leave, extra], axis=0), partner_of(level))
        main_b = got[:size]
        extra = (extra.astype(F32) + got[size:].astype(F32)).astype(BF16)
    whole = (main_a.astype(F32) + main_b.astype(F32)).astype(BF16)
    for level in reversed(range(levels)):
        got = swap(whole, partner_of(level))
        bit = bit_of(level)
        whole = jnp.concatenate([jnp.where(bit, got, whole), jnp.where(bit, whole, got)], axis=0)
    got = swap(jnp.concatenate([whole, extra], axis=0), lambda u, t: u * n_tm + (t ^ 1))
    bit = odd == 1
    grad_second = jnp.where(bit, got[rows:], extra)[0].astype(F32)
    got = got[:rows]
    grad_first = jnp.concatenate(
        [jnp.where(bit, got, whole), jnp.where(bit, whole, got)], axis=0
    ).astype(F32)
    return grad_first, grad_second


def solution(mesh):
    in_specs = (
        P(("grp", "user"), "tm", None),
        P(),
        P(),
        P(),
        P(),
        P(),
        P(),
        P(),
        P(),
        P(),
        P(),
        P(("grp", "user"), "tm"),
        P(("grp", "user"), "tm"),
        P(("grp", "user"), "tm"),
        P(("grp", "user"), "tm", None),
        P(),
        P(),
    )
    out_specs = (P(("grp", "user"), "tm", None), P(("grp", "user"), "tm"), P("grp", None), P("grp"))
    return jax.shard_map(body, mesh=mesh, in_specs=in_specs, out_specs=out_specs, check_vma=False)
```

```python
import functools

import jax
import jax.numpy as jnp
from jax import lax
from jax.experimental import pallas as pl
from jax.experimental.pallas import tpu as pltpu
from jax.sharding import PartitionSpec as P

F32 = jnp.float32
BF16 = jnp.bfloat16
LANES = 128
ALIGN = 16
VMEM = pl.BlockSpec(memory_space=pltpu.VMEM)
SMEM = pl.BlockSpec(memory_space=pltpu.SMEM)
HBM = pl.BlockSpec(memory_space=pltpu.HBM)


def dot(a, b):
    return jnp.dot(a, b, preferred_element_type=F32)


def dot_nt(a, b):
    return lax.dot_general(a, b, (((1,), (1,)), ((), ())), preferred_element_type=F32)


def dot_tn(a, b):
    return lax.dot_general(a, b, (((0,), (0,)), ((), ())), preferred_element_type=F32)


def split3(v):
    high = v.astype(BF16)
    rest = v - high.astype(F32)
    mid = rest.astype(BF16)
    low = (rest - mid.astype(F32)).astype(BF16)
    return high, mid, low


def spread(cols, first_head, head_size, rows):
    lane = lax.broadcasted_iota(jnp.int32, (rows, LANES), 1)
    out = jnp.broadcast_to(cols[:, first_head : first_head + 1], (rows, LANES))
    for k in range(1, LANES // head_size):
        nxt = cols[:, first_head + k : first_head + k + 1]
        out = jnp.where(lane >= k * head_size, nxt, out)
    return out


def scan_kernel(
    heads, take, halo, xbc, cum_o, dt_t, cum_t, pay, raw, carried
):
    hist = take(0)
    dtw, dtb, alog, cw, cb = take(1), take(2), take(3), take(4), take(5)
    length = hist.shape[0]
    edge = halo.shape[0]
    taps = cw.shape[0]
    width = xbc.shape[1]
    inner = carried.shape[1]
    state = (width - inner) // 2
    head_size = inner // heads
    per = LANES // head_size
    rows = jnp.concatenate([halo[...], hist[...]], axis=0)

    v = dot_nt(hist[...], dtw[...]) + dtb[...]
    dt = jnp.maximum(v, 0.0) + jnp.log1p(jnp.exp(-jnp.abs(v)))
    decay = -jnp.exp(alog[...]) * dt
    ri = lax.broadcasted_iota(jnp.int32, (length, length), 0)
    ci = lax.broadcasted_iota(jnp.int32, (length, length), 1)
    tri = jnp.where(ci <= ri, 1.0, 0.0).astype(BF16)
    parts = split3(decay)
    cum = dot(tri, parts[0]) + (dot(tri, parts[1]) + dot(tri, parts[2]))
    cum_o[...] = cum
    dt_t[...] = dt.T
    cum_t[...] = cum.T
    last = cum[length - 1 : length, :]
    weight = jnp.exp(last - cum) * dt

    step = 2 * LANES
    w = take(6)
    for start in list(range(inner, width, step)) + list(range(0, inner, step)):
        cols = slice(start, start + step)
        piece = dot(rows, w[:, cols]).astype(BF16).astype(F32)
        raw[:, cols] = piece
        first = start // LANES
        acc = jnp.concatenate(
            [jnp.broadcast_to(cb[k : k + 1, :], (length, LANES)) for k in (first, first + 1)], axis=1
        )
        for k in range(taps):
            acc = acc + cw[k : k + 1, cols] * raw[pl.ds(edge - (taps - 1) + k, length), cols]
        xbc[:, cols] = (acc / (1.0 + jnp.exp(-acc))).astype(BF16)
    for start in range(0, inner, LANES):
        cols = slice(start, start + LANES)
        x = xbc[:, cols].astype(F32)
        carried[:, cols] = (
            spread(weight, start // LANES * per, head_size, length) * x
        ).astype(BF16)
    b = xbc[:, inner : inner + state]
    pay[:state, :] = dot_tn(b, carried[...]).astype(BF16)
    gain = jnp.broadcast_to(jnp.exp(last), (ALIGN, heads))
    pick = lax.broadcasted_iota(jnp.int32, (ALIGN, LANES), 0)
    for start in range(0, inner, LANES):
        g = spread(gain, start // LANES * per, head_size, ALIGN)
        high = g.astype(BF16).astype(F32)
        pay[state:, start : start + LANES] = jnp.where(
            pick == 0, high, jnp.where(pick == 1, g - high, 0.0)
        ).astype(BF16)


def gain_row(pay, state):
    tail = pay[state:, :].astype(F32)
    return tail[0:1, :] + tail[1:2, :]


def chip_kernel(take, mine, other, out, gain_out):
    state = out.shape[0]
    odd = lax.rem(lax.axis_index("tm"), 2) == 1
    m = mine[:state, :].astype(F32)
    o = other[:state, :].astype(F32)
    gm = gain_row(mine, state)
    go = gain_row(other, state)
    out[...] = jnp.where(odd, o * gm + m, m * go + o).astype(BF16)
    gain_out[...] = jnp.broadcast_to(gm * go, gain_out.shape)


def within_kernel(heads, take, d_skip, xbc, cum, dt_t, cum_t, part, gate, pre):
    length, inner = part.shape
    state = (xbc.shape[1] - inner) // 2
    head_size = inner // heads
    per = LANES // head_size
    b = xbc[:, inner : inner + state]
    c = xbc[:, inner + state :]
    scores = dot_nt(c, b)
    half = length // 2
    tops = lax.broadcasted_iota(jnp.int32, (half, half), 0)
    lefts = lax.broadcasted_iota(jnp.int32, (half, half), 1)
    low_tri = lefts <= tops
    lane = lax.broadcasted_iota(jnp.int32, (length, LANES), 1)
    for start in range(0, inner, LANES):
        cols = slice(start, start + LANES)
        x = xbc[:, cols]
        out = None
        for k in range(per):
            h = start // LANES * per + k
            row = cum_t[h : h + 1, :]
            col = cum[:, h : h + 1]
            dts = dt_t[h : h + 1, :]

            def block(r, s, masked):
                gap = col[r : r + half] - row[:, s : s + half]
                if masked:
                    gap = jnp.where(low_tri, gap, 0.0)
                d = jnp.exp(gap)
                if masked:
                    d = jnp.where(low_tri, d, 0.0)
                return (d * dts[:, s : s + half] * scores[r : r + half, s : s + half]).astype(BF16)

            upper = dot(block(0, 0, True), x[:half])
            lower = dot(block(half, 0, False), x[:half]) + dot(block(half, half, True), x[half:])
            got = jnp.concatenate([upper, lower], axis=0)
            skip = d_skip[h]
            got = got + skip * x.astype(F32)
            out = got if out is None else jnp.where(lane >= k * head_size, got, out)
        part[:, cols] = out
    step = 2 * LANES
    hist, zw = take(0), take(1)
    for start in range(0, inner, step):
        cols = slice(start, start + step)
        z = dot(hist[...], zw[:, cols]).astype(BF16).astype(F32)
        gate[:, cols] = z / (1.0 + jnp.exp(-z))
    item, first = take(2), take(3)
    for start in range(0, pre.shape[1], step):
        cols = slice(start, start + step)
        pre[:, cols] = dot(item[...], first[:, cols])


def rank_kernel(
    heads,
    take,
    count,
    incoming,
    other,
    xbc,
    cum,
    part,
    gate,
    pre,
    enc_o,
    logit_o,
    send_o,
    keep_o,
    gated_s,
    rank_s,
    slope_s,
    hid_s,
    gp_s,
):
    length, inner = part.shape
    state = incoming.shape[0]
    head_size = inner // heads
    per = LANES // head_size
    slots = pre.shape[0]
    tm = lax.axis_index("tm")
    odd = lax.rem(tm, 2) == 1
    base = tm * length
    arrived = incoming[...].astype(F32)
    enter = jnp.where(
        odd, arrived * gain_row(other, state) + other[:state, :].astype(F32), arrived
    )
    high = enter.astype(BF16)
    low = (enter - high.astype(F32)).astype(BF16)
    c = xbc[:, inner + state :]
    grow = jnp.exp(cum[...])
    total = jnp.zeros((length, LANES), F32)
    for start in range(0, inner, LANES):
        cols = slice(start, start + LANES)
        read = dot(c, high[:, cols]) + dot(c, low[:, cols])
        y = part[:, cols] + spread(grow, start // LANES * per, head_size, length) * read
        y = y * gate[:, cols]
        gated_s[:, cols] = y
        total = total + y * y
    mean = jnp.sum(total, axis=1, keepdims=True) * (1.0 / inner)
    scale = lax.rsqrt(mean + 1e-05)
    gain, ow = take(0), take(1)
    normed = (gated_s[...] * scale * gain[...]).astype(BF16)
    enc = dot(normed, ow[...]).astype(BF16)
    enc_o[...] = enc
    width = enc.shape[1]
    pos = take(2)
    place = pos[...] - base
    hot = (lax.broadcasted_iota(jnp.int32, (length, slots), 0) == place).astype(F32).astype(BF16)
    rank_s[...] = dot_tn(hot, enc).astype(BF16)

    hidden_width = pre.shape[1]
    step = 2 * LANES
    logit = jnp.zeros((slots, LANES), F32)
    first, second = take(3), take(4)
    weights2 = second[...].astype(F32)
    for start in range(0, hidden_width, step):
        cols = slice(start, start + step)
        v = pre[:, cols] + dot(rank_s[...], first[:, cols])
        sig = 1.0 / (1.0 + jnp.exp(-v))
        hid = (v * sig).astype(BF16)
        hid_s[:, cols] = hid
        k = start // LANES
        w2 = jnp.concatenate([weights2[k : k + 1], weights2[k + 1 : k + 2]], axis=1)
        prod = hid.astype(F32) * w2
        for k in range(0, step, LANES):
            logit = logit + prod[:, k : k + LANES]
        slope_s[:, cols] = w2 * (sig * (1.0 + v * (1.0 - sig)))
    ones = jnp.ones((8, LANES), BF16)
    p = split3(logit)
    logit8 = dot_nt(ones, p[0]) + (dot_nt(ones, p[1]) + dot_nt(ones, p[2]))
    slot = lax.broadcasted_iota(jnp.int32, (8, slots), 1)
    live = jnp.where(slot < count[0, 0], 1.0, 0.0)
    logit_o[...] = (live * logit8)[0:1, :]
    value = take(5)
    target = value[...].astype(F32)
    dl = live * (1.0 / (1.0 + jnp.exp(-logit8)) - target)
    d0, d1, d2 = split3(dl)
    which = lax.broadcasted_iota(jnp.int32, (8, slots), 0)
    dl3 = jnp.where(
        which == 0,
        d0.astype(F32),
        jnp.where(which == 1, d1.astype(F32), jnp.where(which == 2, d2.astype(F32), 0.0)),
    ).astype(BF16)
    grad2 = jnp.sum(dot(dl3, hid_s[...]), axis=0, keepdims=True)
    dcol = dot_tn(dl3, jnp.ones((8, LANES), BF16))
    for start in range(0, hidden_width, LANES):
        cols = slice(start, start + LANES)
        gp_s[:, cols] = (dcol * slope_s[:, cols]).astype(BF16)
    rows = width
    item = take(6)
    pick = lax.broadcasted_iota(jnp.int32, (8, hidden_width), 0)
    extra = jnp.where(pick == 0, grad2, 0.0).astype(BF16)
    away = jnp.where(odd, rank_s[...], item[...])
    home = jnp.where(odd, item[...], rank_s[...])
    send_o[:rows, :] = dot_tn(away, gp_s[...]).astype(BF16)
    send_o[rows:, :] = extra
    keep_o[:rows, :] = dot_tn(home, gp_s[...]).astype(BF16)
    keep_o[rows:, :] = extra


def loading(kernel, n_loaded, n_given, n_out, windows):
    def wrapped(*refs):
        sources = refs[:n_loaded]
        given = refs[n_loaded : n_loaded + n_given + n_out]
        rest = refs[n_loaded + n_given + n_out :]
        places, sems, scratch = rest[:n_loaded], rest[n_loaded], rest[n_loaded + 1 :]
        copies = []
        for i, source in enumerate(sources):
            window = windows.get(i)
            view = source if window is None else source.at[pl.ds(*window)]
            copies.append(pltpu.make_async_copy(view, places[i], sems.at[i]))
            copies[i].start()

        def take(i):
            copies[i].wait()
            return places[i]

        kernel(take, *given, *scratch)

    return wrapped


def call(kernel, loaded, given, out_shape, scratch, flops, moved, mib, windows=None, smem=0):
    windows = windows or {}
    places = []
    for i, value in enumerate(loaded):
        dims = value.shape if i not in windows else (windows[i][1],) + value.shape[1:]
        places.append(pltpu.VMEM(dims, value.dtype))
    return pl.pallas_call(
        loading(kernel, len(loaded), len(given), len(out_shape), windows),
        out_shape=out_shape,
        in_specs=[HBM] * len(loaded) + [SMEM] * smem + [VMEM] * (len(given) - smem),
        out_specs=[VMEM] * len(out_shape),
        scratch_shapes=places + [pltpu.SemaphoreType.DMA((max(len(loaded), 1),))] + scratch,
        compiler_params=pltpu.CompilerParams(vmem_limit_bytes=mib * 1024 * 1024),
        cost_estimate=pl.CostEstimate(flops=flops, bytes_accessed=moved, transcendentals=0),
    )(*[pltpu.with_memory_space_constraint(value, pltpu.HBM) for value in loaded], *given)


def shape(dims, dtype):
    return jax.ShapeDtypeStruct(dims, dtype)


def bits_of(n):
    return max(n.bit_length() - 1, 0)


def body(
    history,
    z_weight,
    xbc_weight,
    dt_weight,
    dt_bias,
    a_log,
    conv_weight,
    conv_bias,
    d_skip,
    norm_gain,
    out_weight,
    label_pos,
    label_count,
    label_value,
    item_feat,
    first_weight,
    second_weight,
):
    hist = history[0]
    item = item_feat[0]
    length, width = hist.shape
    inner = z_weight.shape[1]
    heads = a_log.shape[0]
    channels = xbc_weight.shape[1]
    state = (channels - inner) // 2
    slots = label_pos.shape[1]
    hidden = first_weight.shape[1]
    n_tm = lax.axis_size("tm")
    n_user = lax.axis_size("user")
    chips = n_tm // 2
    tm = lax.axis_index("tm")
    user = lax.axis_index("user")

    halo = lax.ppermute(hist[length - ALIGN :], "tm", [(i, i + 1) for i in range(n_tm - 1)])
    xbc, cum, dt_t, cum_t, pay = call(
        functools.partial(scan_kernel, heads),
        (
            hist,
            dt_weight.T,
            dt_bias.reshape(1, heads),
            a_log.reshape(1, heads),
            conv_weight,
            conv_bias.reshape(channels // LANES, LANES),
            xbc_weight,
        ),
        (halo,),
        (
            shape((length, channels), BF16),
            shape((length, heads), F32),
            shape((heads, length), F32),
            shape((heads, length), F32),
            shape((state + ALIGN, inner), BF16),
        ),
        [pltpu.VMEM((length + ALIGN, channels), F32), pltpu.VMEM((length, inner), BF16)],
        2 * length * width * channels,
        4 * width * channels,
        16,
    )
    other = lax.ppermute(pay, "tm", [(i, i ^ 1) for i in range(n_tm)])
    chip_state, chip_gain = call(
        chip_kernel,
        (),
        (pay, other),
        (shape((state, inner), BF16), shape((8, inner), F32)),
        [],
        state * inner,
        6 * state * inner,
        6,
    )
    onward = [(i, i + 2) for i in range(n_tm - 2)]
    incoming = lax.ppermute(chip_state, "tm", onward)
    for _ in range(chips - 2):
        passed = chip_gain[0:1] * incoming.astype(F32) + chip_state.astype(F32)
        incoming = lax.ppermute(passed.astype(BF16), "tm", onward)
    part, gate, pre = call(
        functools.partial(within_kernel, heads),
        (hist, z_weight, item, first_weight),
        (d_skip, xbc, cum, dt_t, cum_t),
        (
            shape((length, inner), F32),
            shape((length, inner), F32),
            shape((slots, hidden), F32),
        ),
        [],
        2 * length * width * inner + 2 * slots * width * hidden + 4 * length * length * inner,
        16 * length * inner * 4,
        20,
        {3: (width, width)},
        1,
    )
    enc, row_logit, send, keep = call(
        functools.partial(rank_kernel, heads),
        (
            norm_gain.reshape(1, inner),
            out_weight,
            label_pos,
            first_weight,
            second_weight.reshape(hidden // LANES, LANES),
            label_value,
            item,
        ),
        (label_count, incoming, other, xbc, cum, part, gate, pre),
        (
            shape((length, width), BF16),
            shape((1, slots), F32),
            shape((width + 8, hidden), BF16),
            shape((width + 8, hidden), BF16),
        ),
        [
            pltpu.VMEM((length, inner), F32),
            pltpu.VMEM((slots, width), BF16),
            pltpu.VMEM((slots, hidden), F32),
            pltpu.VMEM((slots, hidden), BF16),
            pltpu.VMEM((slots, hidden), BF16),
        ],
        4 * slots * width * hidden,
        8 * slots * hidden,
        24,
        {3: (0, width)},
        1,
    )
    grad_first, grad_second = total_sum(send, keep, n_user, n_tm, user, tm)
    return (enc[None], row_logit, grad_first, grad_second)


def total_sum(send, keep, n_user, n_tm, user, tm):
    rows = keep.shape[0] - 8
    odd = tm % 2
    axes = ("user", "tm")
    every = [(u, t) for u in range(n_user) for t in range(n_tm)]

    def swap(value, partner):
        pairs = [(u * n_tm + t, partner(u, t)) for u, t in every]
        return lax.ppermute(value, axes, pairs)

    chip_bits = [("tm", k) for k in range(bits_of(n_tm // 2))]
    user_bits = [("user", k) for k in range(bits_of(n_user))]
    order_even = chip_bits + user_bits
    order_odd = user_bits + chip_bits

    def partner_of(level):
        def partner(u, t):
            axis, k = (order_even if t % 2 == 0 else order_odd)[level]
            if axis == "tm":
                return u * n_tm + (t ^ (2 << k))
            return (u ^ (1 << k)) * n_tm + t

        return partner

    def bit_of(level):
        def one(entry):
            axis, k = entry
            return (tm >> (k + 1)) & 1 if axis == "tm" else (user >> k) & 1

        return jnp.where(odd == 0, one(order_even[level]), one(order_odd[level])) == 1

    got = swap(send, lambda u, t: u * n_tm + (t ^ 1))
    levels = len(order_even)
    size = rows
    extra_a, extra_b = keep[rows:].astype(F32), got[rows:].astype(F32)
    main_a, main_b = keep[:rows], got[:rows]
    extra = (extra_a + extra_b).astype(BF16)
    for level in range(levels):
        size //= 2
        bit = bit_of(level)
        low = main_a[:size].astype(F32) + main_b[:size].astype(F32)
        high = main_a[size:].astype(F32) + main_b[size:].astype(F32)
        leave = jnp.where(bit, low, high).astype(BF16)
        main_a = jnp.where(bit, high, low).astype(BF16)
        got = swap(jnp.concatenate([leave, extra], axis=0), partner_of(level))
        main_b = got[:size]
        extra = (extra.astype(F32) + got[size:].astype(F32)).astype(BF16)
    whole = (main_a.astype(F32) + main_b.astype(F32)).astype(BF16)
    for level in reversed(range(levels)):
        got = swap(whole, partner_of(level))
        bit = bit_of(level)
        whole = jnp.concatenate([jnp.where(bit, got, whole), jnp.where(bit, whole, got)], axis=0)
    got = swap(jnp.concatenate([whole, extra], axis=0), lambda u, t: u * n_tm + (t ^ 1))
    bit = odd == 1
    grad_second = jnp.where(bit, got[rows:], extra)[0].astype(F32)
    got = got[:rows]
    grad_first = jnp.concatenate(
        [jnp.where(bit, got, whole), jnp.where(bit, whole, got)], axis=0
    ).astype(F32)
    return grad_first, grad_second


def solution(mesh):
    in_specs = (
        P(("grp", "user"), "tm", None),
        P(),
        P(),
        P(),
        P(),
        P(),
        P(),
        P(),
        P(),
        P(),
        P(),
        P(("grp", "user"), "tm"),
        P(("grp", "user"), "tm"),
        P(("grp", "user"), "tm"),
        P(("grp", "user"), "tm", None),
        P(),
        P(),
    )
    out_specs = (P(("grp", "user"), "tm", None), P(("grp", "user"), "tm"), P("grp", None), P("grp"))
    return jax.shard_map(body, mesh=mesh, in_specs=in_specs, out_specs=out_specs, check_vma=False)
```

```python
import functools

import jax
import jax.numpy as jnp
from jax import lax
from jax.experimental import pallas as pl
from jax.experimental.pallas import tpu as pltpu
from jax.sharding import PartitionSpec as P

F32 = jnp.float32
BF16 = jnp.bfloat16
LANES = 128
ALIGN = 16
VMEM = pl.BlockSpec(memory_space=pltpu.VMEM)
SMEM = pl.BlockSpec(memory_space=pltpu.SMEM)
HBM = pl.BlockSpec(memory_space=pltpu.HBM)


def dot(a, b):
    return jnp.dot(a, b, preferred_element_type=F32)


def dot_nt(a, b):
    return lax.dot_general(a, b, (((1,), (1,)), ((), ())), preferred_element_type=F32)


def dot_tn(a, b):
    return lax.dot_general(a, b, (((0,), (0,)), ((), ())), preferred_element_type=F32)


def split3(v):
    high = v.astype(BF16)
    rest = v - high.astype(F32)
    mid = rest.astype(BF16)
    low = (rest - mid.astype(F32)).astype(BF16)
    return high, mid, low


def spread(cols, first_head, head_size, rows):
    lane = lax.broadcasted_iota(jnp.int32, (rows, LANES), 1)
    out = jnp.broadcast_to(cols[:, first_head : first_head + 1], (rows, LANES))
    for k in range(1, LANES // head_size):
        nxt = cols[:, first_head + k : first_head + k + 1]
        out = jnp.where(lane >= k * head_size, nxt, out)
    return out


def scan_kernel(
    heads, take, halo, xbc, cum_o, dt_t, cum_t, pay, raw, carried
):
    hist = take(0)
    dtw, dtb, alog, cw, cb = take(1), take(2), take(3), take(4), take(5)
    length = hist.shape[0]
    edge = halo.shape[0]
    taps = cw.shape[0]
    width = xbc.shape[1]
    inner = carried.shape[1]
    state = (width - inner) // 2
    head_size = inner // heads
    per = LANES // head_size
    rows = jnp.concatenate([halo[...], hist[...]], axis=0)

    v = dot_nt(hist[...], dtw[...]) + dtb[...]
    dt = jnp.maximum(v, 0.0) + jnp.log1p(jnp.exp(-jnp.abs(v)))
    decay = -jnp.exp(alog[...]) * dt
    ri = lax.broadcasted_iota(jnp.int32, (length, length), 0)
    ci = lax.broadcasted_iota(jnp.int32, (length, length), 1)
    tri = jnp.where(ci <= ri, 1.0, 0.0).astype(BF16)
    parts = split3(decay)
    cum = dot(tri, parts[0]) + (dot(tri, parts[1]) + dot(tri, parts[2]))
    cum_o[...] = cum
    dt_t[...] = dt.T
    cum_t[...] = cum.T
    last = cum[length - 1 : length, :]
    weight = jnp.exp(last - cum) * dt

    step = 2 * LANES
    w = take(6)
    for start in list(range(inner, width, step)) + list(range(0, inner, step)):
        cols = slice(start, start + step)
        piece = dot(rows, w[:, cols]).astype(BF16).astype(F32)
        raw[:, cols] = piece
        first = start // LANES
        acc = jnp.concatenate(
            [jnp.broadcast_to(cb[k : k + 1, :], (length, LANES)) for k in (first, first + 1)], axis=1
        )
        for k in range(taps):
            acc = acc + cw[k : k + 1, cols] * raw[pl.ds(edge - (taps - 1) + k, length), cols]
        xbc[:, cols] = (acc / (1.0 + jnp.exp(-acc))).astype(BF16)
    for start in range(0, inner, LANES):
        cols = slice(start, start + LANES)
        x = xbc[:, cols].astype(F32)
        carried[:, cols] = (
            spread(weight, start // LANES * per, head_size, length) * x
        ).astype(BF16)
    b = xbc[:, inner : inner + state]
    pay[:state, :] = dot_tn(b, carried[...]).astype(BF16)
    gain = jnp.broadcast_to(jnp.exp(last), (ALIGN, heads))
    pick = lax.broadcasted_iota(jnp.int32, (ALIGN, LANES), 0)
    for start in range(0, inner, LANES):
        g = spread(gain, start // LANES * per, head_size, ALIGN)
        high = g.astype(BF16).astype(F32)
        pay[state:, start : start + LANES] = jnp.where(
            pick == 0, high, jnp.where(pick == 1, g - high, 0.0)
        ).astype(BF16)


def gain_row(pay, state):
    tail = pay[state:, :].astype(F32)
    return tail[0:1, :] + tail[1:2, :]


def chip_kernel(take, mine, other, out, gain_out):
    state = out.shape[0]
    odd = lax.rem(lax.axis_index("tm"), 2) == 1
    m = mine[:state, :].astype(F32)
    o = other[:state, :].astype(F32)
    gm = gain_row(mine, state)
    go = gain_row(other, state)
    out[...] = jnp.where(odd, o * gm + m, m * go + o).astype(BF16)
    gain_out[...] = jnp.broadcast_to(gm * go, gain_out.shape)


def within_kernel(heads, take, d_skip, xbc, cum, dt_t, cum_t, part, gate, pre):
    length, inner = part.shape
    state = (xbc.shape[1] - inner) // 2
    head_size = inner // heads
    per = LANES // head_size
    b = xbc[:, inner : inner + state]
    c = xbc[:, inner + state :]
    scores = dot_nt(c, b)
    half = length // 2
    tops = lax.broadcasted_iota(jnp.int32, (half, half), 0)
    lefts = lax.broadcasted_iota(jnp.int32, (half, half), 1)
    low_tri = lefts <= tops
    lane = lax.broadcasted_iota(jnp.int32, (length, LANES), 1)
    for start in range(0, inner, LANES):
        cols = slice(start, start + LANES)
        x = xbc[:, cols]
        out = None
        for k in range(per):
            h = start // LANES * per + k
            row = cum_t[h : h + 1, :]
            col = cum[:, h : h + 1]
            dts = dt_t[h : h + 1, :]

            def block(r, s, masked):
                gap = col[r : r + half] - row[:, s : s + half]
                if masked:
                    gap = jnp.where(low_tri, gap, 0.0)
                d = jnp.exp(gap)
                if masked:
                    d = jnp.where(low_tri, d, 0.0)
                return (d * dts[:, s : s + half] * scores[r : r + half, s : s + half]).astype(BF16)

            upper = dot(block(0, 0, True), x[:half])
            lower = dot(block(half, 0, False), x[:half]) + dot(block(half, half, True), x[half:])
            got = jnp.concatenate([upper, lower], axis=0)
            skip = d_skip[h]
            got = got + skip * x.astype(F32)
            out = got if out is None else jnp.where(lane >= k * head_size, got, out)
        part[:, cols] = out
    step = 2 * LANES
    hist, zw = take(0), take(1)
    for start in range(0, inner, step):
        cols = slice(start, start + step)
        z = dot(hist[...], zw[:, cols]).astype(BF16).astype(F32)
        gate[:, cols] = z / (1.0 + jnp.exp(-z))
    item, first = take(2), take(3)
    for start in range(0, pre.shape[1], step):
        cols = slice(start, start + step)
        pre[:, cols] = dot(item[...], first[:, cols])


def rank_kernel(
    heads,
    take,
    count,
    incoming,
    other,
    xbc,
    cum,
    part,
    gate,
    pre,
    enc_o,
    logit_o,
    send_o,
    keep_o,
    gated_s,
    rank_s,
    slope_s,
    hid_s,
    gp_s,
):
    length, inner = part.shape
    state = incoming.shape[0]
    head_size = inner // heads
    per = LANES // head_size
    slots = pre.shape[0]
    tm = lax.axis_index("tm")
    odd = lax.rem(tm, 2) == 1
    base = tm * length
    arrived = incoming[...].astype(F32)
    enter = jnp.where(
        odd, arrived * gain_row(other, state) + other[:state, :].astype(F32), arrived
    )
    high = enter.astype(BF16)
    low = (enter - high.astype(F32)).astype(BF16)
    c = xbc[:, inner + state :]
    grow = jnp.exp(cum[...])
    total = jnp.zeros((length, LANES), F32)
    for start in range(0, inner, LANES):
        cols = slice(start, start + LANES)
        read = dot(c, high[:, cols]) + dot(c, low[:, cols])
        y = part[:, cols] + spread(grow, start // LANES * per, head_size, length) * read
        y = y * gate[:, cols]
        gated_s[:, cols] = y
        total = total + y * y
    mean = jnp.sum(total, axis=1, keepdims=True) * (1.0 / inner)
    scale = lax.rsqrt(mean + 1e-05)
    gain, ow = take(0), take(1)
    normed = (gated_s[...] * scale * gain[...]).astype(BF16)
    enc = dot(normed, ow[...]).astype(BF16)
    enc_o[...] = enc
    width = enc.shape[1]
    pos = take(2)
    place = pos[...] - base
    hot = (lax.broadcasted_iota(jnp.int32, (length, slots), 0) == place).astype(F32).astype(BF16)
    rank_s[...] = dot_tn(hot, enc).astype(BF16)

    hidden_width = pre.shape[1]
    step = 2 * LANES
    logit = jnp.zeros((slots, LANES), F32)
    first, second = take(3), take(4)
    weights2 = second[...].astype(F32)
    for start in range(0, hidden_width, step):
        cols = slice(start, start + step)
        v = pre[:, cols] + dot(rank_s[...], first[:, cols])
        sig = 1.0 / (1.0 + jnp.exp(-v))
        hid = (v * sig).astype(BF16)
        hid_s[:, cols] = hid
        k = start // LANES
        w2 = jnp.concatenate([weights2[k : k + 1], weights2[k + 1 : k + 2]], axis=1)
        prod = hid.astype(F32) * w2
        for k in range(0, step, LANES):
            logit = logit + prod[:, k : k + LANES]
        slope_s[:, cols] = w2 * (sig * (1.0 + v * (1.0 - sig)))
    ones = jnp.ones((8, LANES), BF16)
    p = split3(logit)
    logit8 = dot_nt(ones, p[0]) + (dot_nt(ones, p[1]) + dot_nt(ones, p[2]))
    slot = lax.broadcasted_iota(jnp.int32, (8, slots), 1)
    live = jnp.where(slot < count[0, 0], 1.0, 0.0)
    logit_o[...] = (live * logit8)[0:1, :]
    value = take(5)
    target = value[...].astype(F32)
    dl = live * (1.0 / (1.0 + jnp.exp(-logit8)) - target)
    d0, d1, d2 = split3(dl)
    which = lax.broadcasted_iota(jnp.int32, (8, slots), 0)
    dl3 = jnp.where(
        which == 0,
        d0.astype(F32),
        jnp.where(which == 1, d1.astype(F32), jnp.where(which == 2, d2.astype(F32), 0.0)),
    ).astype(BF16)
    grad2 = jnp.sum(dot(dl3, hid_s[...]), axis=0, keepdims=True)
    dcol = dot_tn(dl3, jnp.ones((8, LANES), BF16))
    for start in range(0, hidden_width, LANES):
        cols = slice(start, start + LANES)
        gp_s[:, cols] = (dcol * slope_s[:, cols]).astype(BF16)
    rows = width
    item = take(6)
    pick = lax.broadcasted_iota(jnp.int32, (8, hidden_width), 0)
    extra = jnp.where(pick == 0, grad2, 0.0).astype(BF16)
    away = jnp.where(odd, rank_s[...], item[...])
    home = jnp.where(odd, item[...], rank_s[...])
    send_o[:rows, :] = dot_tn(away, gp_s[...]).astype(BF16)
    send_o[rows:, :] = extra
    keep_o[:rows, :] = dot_tn(home, gp_s[...]).astype(BF16)
    keep_o[rows:, :] = extra


def loading(kernel, n_loaded, n_given, n_out, windows):
    def wrapped(*refs):
        sources = refs[:n_loaded]
        given = refs[n_loaded : n_loaded + n_given + n_out]
        rest = refs[n_loaded + n_given + n_out :]
        places, sems, scratch = rest[:n_loaded], rest[n_loaded], rest[n_loaded + 1 :]
        copies = []
        for i, source in enumerate(sources):
            window = windows.get(i)
            view = source if window is None else source.at[pl.ds(*window)]
            copies.append(pltpu.make_async_copy(view, places[i], sems.at[i]))
            copies[i].start()

        def take(i):
            copies[i].wait()
            return places[i]

        kernel(take, *given, *scratch)

    return wrapped


def call(kernel, loaded, given, out_shape, scratch, flops, moved, mib, windows=None, smem=0):
    windows = windows or {}
    places = []
    for i, value in enumerate(loaded):
        dims = value.shape if i not in windows else (windows[i][1],) + value.shape[1:]
        places.append(pltpu.VMEM(dims, value.dtype))
    return pl.pallas_call(
        loading(kernel, len(loaded), len(given), len(out_shape), windows),
        out_shape=out_shape,
        in_specs=[HBM] * len(loaded) + [SMEM] * smem + [VMEM] * (len(given) - smem),
        out_specs=[VMEM] * len(out_shape),
        scratch_shapes=places + [pltpu.SemaphoreType.DMA((max(len(loaded), 1),))] + scratch,
        compiler_params=pltpu.CompilerParams(vmem_limit_bytes=mib * 1024 * 1024),
        cost_estimate=pl.CostEstimate(flops=flops, bytes_accessed=moved, transcendentals=0),
    )(*[pltpu.with_memory_space_constraint(value, pltpu.HBM) for value in loaded], *given)


def shape(dims, dtype):
    return jax.ShapeDtypeStruct(dims, dtype)


def bits_of(n):
    return max(n.bit_length() - 1, 0)


def body(
    history,
    z_weight,
    xbc_weight,
    dt_weight,
    dt_bias,
    a_log,
    conv_weight,
    conv_bias,
    d_skip,
    norm_gain,
    out_weight,
    label_pos,
    label_count,
    label_value,
    item_feat,
    first_weight,
    second_weight,
):
    hist = history[0]
    item = item_feat[0]
    length, width = hist.shape
    inner = z_weight.shape[1]
    heads = a_log.shape[0]
    channels = xbc_weight.shape[1]
    state = (channels - inner) // 2
    slots = label_pos.shape[1]
    hidden = first_weight.shape[1]
    n_tm = lax.axis_size("tm")
    n_user = lax.axis_size("user")
    chips = n_tm // 2
    tm = lax.axis_index("tm")
    user = lax.axis_index("user")

    halo = lax.ppermute(hist[length - ALIGN :], "tm", [(i, i + 1) for i in range(n_tm - 1)])
    xbc, cum, dt_t, cum_t, pay = call(
        functools.partial(scan_kernel, heads),
        (
            hist,
            dt_weight.T,
            dt_bias.reshape(1, heads),
            a_log.reshape(1, heads),
            conv_weight,
            conv_bias.reshape(channels // LANES, LANES),
            xbc_weight,
        ),
        (halo,),
        (
            shape((length, channels), BF16),
            shape((length, heads), F32),
            shape((heads, length), F32),
            shape((heads, length), F32),
            shape((state + ALIGN, inner), BF16),
        ),
        [pltpu.VMEM((length + ALIGN, channels), F32), pltpu.VMEM((length, inner), BF16)],
        2 * length * width * channels,
        4 * width * channels,
        16,
    )
    other = lax.ppermute(pay, "tm", [(i, i ^ 1) for i in range(n_tm)])
    chip_state, chip_gain = call(
        chip_kernel,
        (),
        (pay, other),
        (shape((state, inner), BF16), shape((8, inner), F32)),
        [],
        state * inner,
        6 * state * inner,
        6,
    )
    onward = [(i, i + 2) for i in range(n_tm - 2)]
    incoming = lax.ppermute(chip_state, "tm", onward)
    for _ in range(chips - 2):
        passed = chip_gain[0:1] * incoming.astype(F32) + chip_state.astype(F32)
        incoming = lax.ppermute(passed.astype(BF16), "tm", onward)
    part, gate, pre = call(
        functools.partial(within_kernel, heads),
        (hist, z_weight, item, first_weight),
        (d_skip, xbc, cum, dt_t, cum_t),
        (
            shape((length, inner), F32),
            shape((length, inner), F32),
            shape((slots, hidden), F32),
        ),
        [],
        2 * length * width * inner + 2 * slots * width * hidden + 4 * length * length * inner,
        16 * length * inner * 4,
        20,
        {3: (width, width)},
        1,
    )
    enc, row_logit, send, keep = call(
        functools.partial(rank_kernel, heads),
        (
            norm_gain.reshape(1, inner),
            out_weight,
            label_pos,
            first_weight,
            second_weight.reshape(hidden // LANES, LANES),
            label_value,
            item,
        ),
        (label_count, incoming, other, xbc, cum, part, gate, pre),
        (
            shape((length, width), BF16),
            shape((1, slots), F32),
            shape((width + 8, hidden), BF16),
            shape((width + 8, hidden), BF16),
        ),
        [
            pltpu.VMEM((length, inner), F32),
            pltpu.VMEM((slots, width), BF16),
            pltpu.VMEM((slots, hidden), F32),
            pltpu.VMEM((slots, hidden), BF16),
            pltpu.VMEM((slots, hidden), BF16),
        ],
        4 * slots * width * hidden,
        8 * slots * hidden,
        24,
        {3: (0, width)},
        1,
    )
    grad_first, grad_second = total_sum(send, keep, n_user, n_tm, user, tm)
    return (enc[None], row_logit, grad_first, grad_second)


def total_sum(send, keep, n_user, n_tm, user, tm):
    rows = keep.shape[0] - 8
    odd = tm % 2
    axes = ("user", "tm")
    every = [(u, t) for u in range(n_user) for t in range(n_tm)]
    chunks = 2

    def swap(value, partner):
        pairs = [(u * n_tm + t, partner(u, t)) for u, t in every]
        return lax.ppermute(value, axes, pairs)

    def across(u, t):
        return u * n_tm + (t ^ 1)

    chip_bits = [("tm", k) for k in range(bits_of(n_tm // 2))]
    user_bits = [("user", k) for k in range(bits_of(n_user))]
    order_even = chip_bits + user_bits
    order_odd = user_bits + chip_bits

    def partner_of(level):
        def partner(u, t):
            axis, k = (order_even if t % 2 == 0 else order_odd)[level]
            if axis == "tm":
                return u * n_tm + (t ^ (2 << k))
            return (u ^ (1 << k)) * n_tm + t

        return partner

    def bit_of(level):
        def one(entry):
            axis, k = entry
            return (tm >> (k + 1)) & 1 if axis == "tm" else (user >> k) & 1

        return jnp.where(odd == 0, one(order_even[level]), one(order_odd[level])) == 1

    levels = len(order_even)
    bits = [bit_of(level) for level in range(levels)]
    bit = odd == 1
    edges = [rows * k // chunks for k in range(chunks + 1)]
    pieces = []
    for k in range(chunks):
        last = k == chunks - 1
        stop = edges[k + 1] + (8 if last else 0)
        pieces.append((send[edges[k] : stop], keep[edges[k] : stop], last))
    size = rows // chunks
    state = []
    for leave, stay, has_extra in pieces:
        got = swap(leave, across)
        extra = None
        if has_extra:
            extra = (stay[size:].astype(F32) + got[size:].astype(F32)).astype(BF16)
        state.append((stay[:size], got[:size], extra))
    for level in range(levels):
        size //= 2
        after = []
        for a, b, extra in state:
            low = a[:size].astype(F32) + b[:size].astype(F32)
            high = a[size:].astype(F32) + b[size:].astype(F32)
            leave = jnp.where(bits[level], low, high).astype(BF16)
            stay = jnp.where(bits[level], high, low).astype(BF16)
            if extra is not None:
                leave = jnp.concatenate([leave, extra], axis=0)
            got = swap(leave, partner_of(level))
            if extra is not None:
                extra = (extra.astype(F32) + got[size:].astype(F32)).astype(BF16)
            after.append((stay, got[:size], extra))
        state = after
    wholes = [((a.astype(F32) + b.astype(F32)).astype(BF16), extra) for a, b, extra in state]
    for level in reversed(range(levels)):
        after = []
        for whole, extra in wholes:
            got = swap(whole, partner_of(level))
            first = jnp.where(bits[level], got, whole)
            second = jnp.where(bits[level], whole, got)
            after.append((jnp.concatenate([first, second], axis=0), extra))
        wholes = after
    tops, bottoms = [], []
    for whole, extra in wholes:
        n = whole.shape[0]
        if extra is None:
            got = swap(whole, across)
        else:
            got = swap(jnp.concatenate([whole, extra], axis=0), across)
            grad_second = jnp.where(bit, got[n:], extra)[0].astype(F32)
            got = got[:n]
        tops.append(jnp.where(bit, got, whole).astype(F32))
        bottoms.append(jnp.where(bit, whole, got).astype(F32))
    return jnp.concatenate(tops + bottoms, axis=0), grad_second


def solution(mesh):
    in_specs = (
        P(("grp", "user"), "tm", None),
        P(),
        P(),
        P(),
        P(),
        P(),
        P(),
        P(),
        P(),
        P(),
        P(),
        P(("grp", "user"), "tm"),
        P(("grp", "user"), "tm"),
        P(("grp", "user"), "tm"),
        P(("grp", "user"), "tm", None),
        P(),
        P(),
    )
    out_specs = (P(("grp", "user"), "tm", None), P(("grp", "user"), "tm"), P("grp", None), P("grp"))
    return jax.shard_map(body, mesh=mesh, in_specs=in_specs, out_specs=out_specs, check_vma=False)
```

```python
import functools

import jax
import jax.numpy as jnp
from jax import lax
from jax.experimental import pallas as pl
from jax.experimental.pallas import tpu as pltpu
from jax.sharding import PartitionSpec as P

F32 = jnp.float32
BF16 = jnp.bfloat16
LANES = 128
ALIGN = 16
VMEM = pl.BlockSpec(memory_space=pltpu.VMEM)
SMEM = pl.BlockSpec(memory_space=pltpu.SMEM)
HBM = pl.BlockSpec(memory_space=pltpu.HBM)


def dot(a, b):
    return jnp.dot(a, b, preferred_element_type=F32)


def dot_nt(a, b):
    return lax.dot_general(a, b, (((1,), (1,)), ((), ())), preferred_element_type=F32)


def dot_tn(a, b):
    return lax.dot_general(a, b, (((0,), (0,)), ((), ())), preferred_element_type=F32)


def split3(v):
    high = v.astype(BF16)
    rest = v - high.astype(F32)
    mid = rest.astype(BF16)
    low = (rest - mid.astype(F32)).astype(BF16)
    return high, mid, low


def spread(cols, first_head, head_size, rows):
    lane = lax.broadcasted_iota(jnp.int32, (rows, LANES), 1)
    out = jnp.broadcast_to(cols[:, first_head : first_head + 1], (rows, LANES))
    for k in range(1, LANES // head_size):
        nxt = cols[:, first_head + k : first_head + k + 1]
        out = jnp.where(lane >= k * head_size, nxt, out)
    return out


def scan_kernel(
    heads, take, halo, xbc, cum_o, dt_t, cum_t, pay, raw, carried
):
    hist = take(0)
    dtw, dtb, alog, cw, cb = take(1), take(2), take(3), take(4), take(5)
    length = hist.shape[0]
    edge = halo.shape[0]
    taps = cw.shape[0]
    width = xbc.shape[1]
    inner = carried.shape[1]
    state = (width - inner) // 2
    head_size = inner // heads
    per = LANES // head_size
    before = jnp.where(lax.axis_index("tm") == 0, 0.0, halo[...].astype(F32)).astype(BF16)
    rows = jnp.concatenate([before, hist[...]], axis=0)

    v = dot_nt(hist[...], dtw[...]) + dtb[...]
    dt = jnp.maximum(v, 0.0) + jnp.log1p(jnp.exp(-jnp.abs(v)))
    decay = -jnp.exp(alog[...]) * dt
    ri = lax.broadcasted_iota(jnp.int32, (length, length), 0)
    ci = lax.broadcasted_iota(jnp.int32, (length, length), 1)
    tri = jnp.where(ci <= ri, 1.0, 0.0).astype(BF16)
    parts = split3(decay)
    cum = dot(tri, parts[0]) + (dot(tri, parts[1]) + dot(tri, parts[2]))
    cum_o[...] = cum
    dt_t[...] = dt.T
    cum_t[...] = cum.T
    last = cum[length - 1 : length, :]
    weight = jnp.exp(last - cum) * dt

    step = 2 * LANES
    w = take(6)
    for start in list(range(inner, width, step)) + list(range(0, inner, step)):
        cols = slice(start, start + step)
        piece = dot(rows, w[:, cols]).astype(BF16).astype(F32)
        raw[:, cols] = piece
        first = start // LANES
        acc = jnp.concatenate(
            [jnp.broadcast_to(cb[k : k + 1, :], (length, LANES)) for k in (first, first + 1)], axis=1
        )
        for k in range(taps):
            acc = acc + cw[k : k + 1, cols] * raw[pl.ds(edge - (taps - 1) + k, length), cols]
        xbc[:, cols] = (acc / (1.0 + jnp.exp(-acc))).astype(BF16)
    for start in range(0, inner, LANES):
        cols = slice(start, start + LANES)
        x = xbc[:, cols].astype(F32)
        carried[:, cols] = (
            spread(weight, start // LANES * per, head_size, length) * x
        ).astype(BF16)
    b = xbc[:, inner : inner + state]
    pay[:state, :] = dot_tn(b, carried[...]).astype(BF16)
    gain = jnp.broadcast_to(jnp.exp(last), (ALIGN, heads))
    pick = lax.broadcasted_iota(jnp.int32, (ALIGN, LANES), 0)
    for start in range(0, inner, LANES):
        g = spread(gain, start // LANES * per, head_size, ALIGN)
        high = g.astype(BF16).astype(F32)
        pay[state:, start : start + LANES] = jnp.where(
            pick == 0, high, jnp.where(pick == 1, g - high, 0.0)
        ).astype(BF16)


def gain_row(pay, state):
    tail = pay[state:, :].astype(F32)
    return tail[0:1, :] + tail[1:2, :]


def chip_kernel(take, mine, other, out, gain_out):
    state = out.shape[0]
    odd = lax.rem(lax.axis_index("tm"), 2) == 1
    m = mine[:state, :].astype(F32)
    o = other[:state, :].astype(F32)
    gm = gain_row(mine, state)
    go = gain_row(other, state)
    out[...] = jnp.where(odd, o * gm + m, m * go + o).astype(BF16)
    gain_out[...] = jnp.broadcast_to(gm * go, gain_out.shape)


def within_kernel(heads, take, d_skip, xbc, cum, dt_t, cum_t, part, gate, pre):
    length, inner = part.shape
    state = (xbc.shape[1] - inner) // 2
    head_size = inner // heads
    per = LANES // head_size
    b = xbc[:, inner : inner + state]
    c = xbc[:, inner + state :]
    scores = dot_nt(c, b)
    half = length // 2
    tops = lax.broadcasted_iota(jnp.int32, (half, half), 0)
    lefts = lax.broadcasted_iota(jnp.int32, (half, half), 1)
    low_tri = lefts <= tops
    lane = lax.broadcasted_iota(jnp.int32, (length, LANES), 1)
    for start in range(0, inner, LANES):
        cols = slice(start, start + LANES)
        x = xbc[:, cols]
        out = None
        for k in range(per):
            h = start // LANES * per + k
            row = cum_t[h : h + 1, :]
            col = cum[:, h : h + 1]
            dts = dt_t[h : h + 1, :]

            def block(r, s, masked):
                gap = col[r : r + half] - row[:, s : s + half]
                if masked:
                    gap = jnp.where(low_tri, gap, 0.0)
                d = jnp.exp(gap)
                if masked:
                    d = jnp.where(low_tri, d, 0.0)
                return (d * dts[:, s : s + half] * scores[r : r + half, s : s + half]).astype(BF16)

            upper = dot(block(0, 0, True), x[:half])
            lower = dot(block(half, 0, False), x[:half]) + dot(block(half, half, True), x[half:])
            got = jnp.concatenate([upper, lower], axis=0)
            skip = d_skip[h]
            got = got + skip * x.astype(F32)
            out = got if out is None else jnp.where(lane >= k * head_size, got, out)
        part[:, cols] = out
    step = 2 * LANES
    hist, zw = take(0), take(1)
    for start in range(0, inner, step):
        cols = slice(start, start + step)
        z = dot(hist[...], zw[:, cols]).astype(BF16).astype(F32)
        gate[:, cols] = z / (1.0 + jnp.exp(-z))
    item, first = take(2), take(3)
    for start in range(0, pre.shape[1], step):
        cols = slice(start, start + step)
        pre[:, cols] = dot(item[...], first[:, cols])


def rank_kernel(
    heads,
    take,
    count,
    incoming,
    other,
    xbc,
    cum,
    part,
    gate,
    pre,
    enc_o,
    logit_o,
    send_o,
    keep_o,
    gated_s,
    rank_s,
    slope_s,
    hid_s,
    gp_s,
):
    length, inner = part.shape
    state = incoming.shape[0]
    head_size = inner // heads
    per = LANES // head_size
    slots = pre.shape[0]
    tm = lax.axis_index("tm")
    odd = lax.rem(tm, 2) == 1
    base = tm * length
    arrived = jnp.where(tm < 2, 0.0, incoming[...].astype(F32))
    enter = jnp.where(
        odd, arrived * gain_row(other, state) + other[:state, :].astype(F32), arrived
    )
    high = enter.astype(BF16)
    low = (enter - high.astype(F32)).astype(BF16)
    c = xbc[:, inner + state :]
    grow = jnp.exp(cum[...])
    total = jnp.zeros((length, LANES), F32)
    for start in range(0, inner, LANES):
        cols = slice(start, start + LANES)
        read = dot(c, high[:, cols]) + dot(c, low[:, cols])
        y = part[:, cols] + spread(grow, start // LANES * per, head_size, length) * read
        y = y * gate[:, cols]
        gated_s[:, cols] = y
        total = total + y * y
    mean = jnp.sum(total, axis=1, keepdims=True) * (1.0 / inner)
    scale = lax.rsqrt(mean + 1e-05)
    gain, ow = take(0), take(1)
    normed = (gated_s[...] * scale * gain[...]).astype(BF16)
    enc = dot(normed, ow[...]).astype(BF16)
    enc_o[...] = enc
    width = enc.shape[1]
    pos = take(2)
    place = pos[...] - base
    hot = (lax.broadcasted_iota(jnp.int32, (length, slots), 0) == place).astype(F32).astype(BF16)
    rank_s[...] = dot_tn(hot, enc).astype(BF16)

    hidden_width = pre.shape[1]
    step = 2 * LANES
    logit = jnp.zeros((slots, LANES), F32)
    first, second = take(3), take(4)
    weights2 = second[...].astype(F32)
    for start in range(0, hidden_width, step):
        cols = slice(start, start + step)
        v = pre[:, cols] + dot(rank_s[...], first[:, cols])
        sig = 1.0 / (1.0 + jnp.exp(-v))
        hid = (v * sig).astype(BF16)
        hid_s[:, cols] = hid
        k = start // LANES
        w2 = jnp.concatenate([weights2[k : k + 1], weights2[k + 1 : k + 2]], axis=1)
        prod = hid.astype(F32) * w2
        for k in range(0, step, LANES):
            logit = logit + prod[:, k : k + LANES]
        slope_s[:, cols] = w2 * (sig * (1.0 + v * (1.0 - sig)))
    ones = jnp.ones((8, LANES), BF16)
    p = split3(logit)
    logit8 = dot_nt(ones, p[0]) + (dot_nt(ones, p[1]) + dot_nt(ones, p[2]))
    slot = lax.broadcasted_iota(jnp.int32, (8, slots), 1)
    live = jnp.where(slot < count[0, 0], 1.0, 0.0)
    logit_o[...] = (live * logit8)[0:1, :]
    value = take(5)
    target = value[...].astype(F32)
    dl = live * (1.0 / (1.0 + jnp.exp(-logit8)) - target)
    d0, d1, d2 = split3(dl)
    which = lax.broadcasted_iota(jnp.int32, (8, slots), 0)
    dl3 = jnp.where(
        which == 0,
        d0.astype(F32),
        jnp.where(which == 1, d1.astype(F32), jnp.where(which == 2, d2.astype(F32), 0.0)),
    ).astype(BF16)
    grad2 = jnp.sum(dot(dl3, hid_s[...]), axis=0, keepdims=True)
    dcol = dot_tn(dl3, jnp.ones((8, LANES), BF16))
    for start in range(0, hidden_width, LANES):
        cols = slice(start, start + LANES)
        gp_s[:, cols] = (dcol * slope_s[:, cols]).astype(BF16)
    rows = width
    item = take(6)
    pick = lax.broadcasted_iota(jnp.int32, (8, hidden_width), 0)
    extra = jnp.where(pick == 0, grad2, 0.0).astype(BF16)
    away = jnp.where(odd, rank_s[...], item[...])
    home = jnp.where(odd, item[...], rank_s[...])
    send_o[:rows, :] = dot_tn(away, gp_s[...]).astype(BF16)
    send_o[rows:, :] = extra
    keep_o[:rows, :] = dot_tn(home, gp_s[...]).astype(BF16)
    keep_o[rows:, :] = extra


def loading(kernel, n_loaded, n_given, n_out, windows):
    def wrapped(*refs):
        sources = refs[:n_loaded]
        given = refs[n_loaded : n_loaded + n_given + n_out]
        rest = refs[n_loaded + n_given + n_out :]
        places, sems, scratch = rest[:n_loaded], rest[n_loaded], rest[n_loaded + 1 :]
        copies = []
        for i, source in enumerate(sources):
            window = windows.get(i)
            view = source if window is None else source.at[pl.ds(*window)]
            copies.append(pltpu.make_async_copy(view, places[i], sems.at[i]))
            copies[i].start()

        def take(i):
            copies[i].wait()
            return places[i]

        kernel(take, *given, *scratch)

    return wrapped


def call(kernel, loaded, given, out_shape, scratch, flops, moved, mib, windows=None, smem=0):
    windows = windows or {}
    places = []
    for i, value in enumerate(loaded):
        dims = value.shape if i not in windows else (windows[i][1],) + value.shape[1:]
        places.append(pltpu.VMEM(dims, value.dtype))
    return pl.pallas_call(
        loading(kernel, len(loaded), len(given), len(out_shape), windows),
        out_shape=out_shape,
        in_specs=[HBM] * len(loaded) + [SMEM] * smem + [VMEM] * (len(given) - smem),
        out_specs=[VMEM] * len(out_shape),
        scratch_shapes=places + [pltpu.SemaphoreType.DMA((max(len(loaded), 1),))] + scratch,
        compiler_params=pltpu.CompilerParams(vmem_limit_bytes=mib * 1024 * 1024),
        cost_estimate=pl.CostEstimate(flops=flops, bytes_accessed=moved, transcendentals=0),
    )(*[pltpu.with_memory_space_constraint(value, pltpu.HBM) for value in loaded], *given)


def shape(dims, dtype):
    return jax.ShapeDtypeStruct(dims, dtype)


def bits_of(n):
    return max(n.bit_length() - 1, 0)


def body(
    history,
    z_weight,
    xbc_weight,
    dt_weight,
    dt_bias,
    a_log,
    conv_weight,
    conv_bias,
    d_skip,
    norm_gain,
    out_weight,
    label_pos,
    label_count,
    label_value,
    item_feat,
    first_weight,
    second_weight,
):
    hist = history[0]
    item = item_feat[0]
    length, width = hist.shape
    inner = z_weight.shape[1]
    heads = a_log.shape[0]
    channels = xbc_weight.shape[1]
    state = (channels - inner) // 2
    slots = label_pos.shape[1]
    hidden = first_weight.shape[1]
    n_tm = lax.axis_size("tm")
    n_user = lax.axis_size("user")
    chips = n_tm // 2
    tm = lax.axis_index("tm")
    user = lax.axis_index("user")

    halo = lax.ppermute(hist[length - ALIGN :], "tm", [(i, (i + 1) % n_tm) for i in range(n_tm)])
    xbc, cum, dt_t, cum_t, pay = call(
        functools.partial(scan_kernel, heads),
        (
            hist,
            dt_weight.T,
            dt_bias.reshape(1, heads),
            a_log.reshape(1, heads),
            conv_weight,
            conv_bias.reshape(channels // LANES, LANES),
            xbc_weight,
        ),
        (halo,),
        (
            shape((length, channels), BF16),
            shape((length, heads), F32),
            shape((heads, length), F32),
            shape((heads, length), F32),
            shape((state + ALIGN, inner), BF16),
        ),
        [pltpu.VMEM((length + ALIGN, channels), F32), pltpu.VMEM((length, inner), BF16)],
        2 * length * width * channels,
        4 * width * channels,
        16,
    )
    other = lax.ppermute(pay, "tm", [(i, i ^ 1) for i in range(n_tm)])
    chip_state, chip_gain = call(
        chip_kernel,
        (),
        (pay, other),
        (shape((state, inner), BF16), shape((8, inner), F32)),
        [],
        state * inner,
        6 * state * inner,
        6,
    )
    onward = [(i, (i + 2) % n_tm) for i in range(n_tm)]
    incoming = lax.ppermute(chip_state, "tm", onward)
    for _ in range(chips - 2):
        incoming = jnp.where(tm < 2, 0.0, incoming.astype(F32))
        passed = chip_gain[0:1] * incoming + chip_state.astype(F32)
        incoming = lax.ppermute(passed.astype(BF16), "tm", onward)
    part, gate, pre = call(
        functools.partial(within_kernel, heads),
        (hist, z_weight, item, first_weight),
        (d_skip, xbc, cum, dt_t, cum_t),
        (
            shape((length, inner), F32),
            shape((length, inner), F32),
            shape((slots, hidden), F32),
        ),
        [],
        2 * length * width * inner + 2 * slots * width * hidden + 4 * length * length * inner,
        16 * length * inner * 4,
        20,
        {3: (width, width)},
        1,
    )
    enc, row_logit, send, keep = call(
        functools.partial(rank_kernel, heads),
        (
            norm_gain.reshape(1, inner),
            out_weight,
            label_pos,
            first_weight,
            second_weight.reshape(hidden // LANES, LANES),
            label_value,
            item,
        ),
        (label_count, incoming, other, xbc, cum, part, gate, pre),
        (
            shape((length, width), BF16),
            shape((1, slots), F32),
            shape((width + 8, hidden), BF16),
            shape((width + 8, hidden), BF16),
        ),
        [
            pltpu.VMEM((length, inner), F32),
            pltpu.VMEM((slots, width), BF16),
            pltpu.VMEM((slots, hidden), F32),
            pltpu.VMEM((slots, hidden), BF16),
            pltpu.VMEM((slots, hidden), BF16),
        ],
        4 * slots * width * hidden,
        8 * slots * hidden,
        24,
        {3: (0, width)},
        1,
    )
    grad_first, grad_second = total_sum(send, keep, n_user, n_tm, user, tm)
    return (enc[None], row_logit, grad_first, grad_second)


def total_sum(send, keep, n_user, n_tm, user, tm):
    rows = keep.shape[0] - 8
    odd = tm % 2
    axes = ("user", "tm")
    every = [(u, t) for u in range(n_user) for t in range(n_tm)]
    chunks = 2

    def swap(value, partner):
        pairs = [(u * n_tm + t, partner(u, t)) for u, t in every]
        return lax.ppermute(value, axes, pairs)

    def across(u, t):
        return u * n_tm + (t ^ 1)

    chip_bits = [("tm", k) for k in range(bits_of(n_tm // 2))]
    user_bits = [("user", k) for k in range(bits_of(n_user))]
    order_even = chip_bits + user_bits
    order_odd = user_bits + chip_bits

    def partner_of(level):
        def partner(u, t):
            axis, k = (order_even if t % 2 == 0 else order_odd)[level]
            if axis == "tm":
                return u * n_tm + (t ^ (2 << k))
            return (u ^ (1 << k)) * n_tm + t

        return partner

    def bit_of(level):
        def one(entry):
            axis, k = entry
            return (tm >> (k + 1)) & 1 if axis == "tm" else (user >> k) & 1

        return jnp.where(odd == 0, one(order_even[level]), one(order_odd[level])) == 1

    levels = len(order_even)
    bits = [bit_of(level) for level in range(levels)]
    bit = odd == 1
    edges = [rows * k // chunks for k in range(chunks + 1)]
    pieces = []
    for k in range(chunks):
        last = k == chunks - 1
        stop = edges[k + 1] + (8 if last else 0)
        pieces.append((send[edges[k] : stop], keep[edges[k] : stop], last))
    size = rows // chunks
    state = []
    for leave, stay, has_extra in pieces:
        got = swap(leave, across)
        extra = None
        if has_extra:
            extra = (stay[size:].astype(F32) + got[size:].astype(F32)).astype(BF16)
        state.append((stay[:size], got[:size], extra))
    for level in range(levels - 1):
        size //= 2
        after = []
        for a, b, extra in state:
            low = a[:size].astype(F32) + b[:size].astype(F32)
            high = a[size:].astype(F32) + b[size:].astype(F32)
            leave = jnp.where(bits[level], low, high).astype(BF16)
            stay = jnp.where(bits[level], high, low).astype(BF16)
            if extra is not None:
                leave = jnp.concatenate([leave, extra], axis=0)
            got = swap(leave, partner_of(level))
            if extra is not None:
                extra = (extra.astype(F32) + got[size:].astype(F32)).astype(BF16)
            after.append((stay, got[:size], extra))
        state = after
    wholes = []
    for a, b, extra in state:
        whole = (a.astype(F32) + b.astype(F32)).astype(BF16)
        if levels:
            leave = whole if extra is None else jnp.concatenate([whole, extra], axis=0)
            got = swap(leave, partner_of(levels - 1))
            whole = (whole.astype(F32) + got[:size].astype(F32)).astype(BF16)
            if extra is not None:
                extra = (extra.astype(F32) + got[size:].astype(F32)).astype(BF16)
        wholes.append((whole, extra))
    for level in reversed(range(levels - 1)):
        after = []
        for whole, extra in wholes:
            got = swap(whole, partner_of(level))
            first = jnp.where(bits[level], got, whole)
            second = jnp.where(bits[level], whole, got)
            after.append((jnp.concatenate([first, second], axis=0), extra))
        wholes = after
    tops, bottoms = [], []
    for whole, extra in wholes:
        n = whole.shape[0]
        if extra is None:
            got = swap(whole, across)
        else:
            got = swap(jnp.concatenate([whole, extra], axis=0), across)
            grad_second = jnp.where(bit, got[n:], extra)[0].astype(F32)
            got = got[:n]
        tops.append(jnp.where(bit, got, whole).astype(F32))
        bottoms.append(jnp.where(bit, whole, got).astype(F32))
    return jnp.concatenate(tops + bottoms, axis=0), grad_second


def solution(mesh):
    in_specs = (
        P(("grp", "user"), "tm", None),
        P(),
        P(),
        P(),
        P(),
        P(),
        P(),
        P(),
        P(),
        P(),
        P(),
        P(("grp", "user"), "tm"),
        P(("grp", "user"), "tm"),
        P(("grp", "user"), "tm"),
        P(("grp", "user"), "tm", None),
        P(),
        P(),
    )
    out_specs = (P(("grp", "user"), "tm", None), P(("grp", "user"), "tm"), P("grp", None), P("grp"))
    return jax.shard_map(body, mesh=mesh, in_specs=in_specs, out_specs=out_specs, check_vma=False)
```

```python
import functools

import jax
import jax.numpy as jnp
from jax import lax
from jax.experimental import pallas as pl
from jax.experimental.pallas import tpu as pltpu
from jax.sharding import PartitionSpec as P

F32 = jnp.float32
BF16 = jnp.bfloat16
LANES = 128
ALIGN = 16
VMEM = pl.BlockSpec(memory_space=pltpu.VMEM)
SMEM = pl.BlockSpec(memory_space=pltpu.SMEM)
HBM = pl.BlockSpec(memory_space=pltpu.HBM)


def dot(a, b):
    return jnp.dot(a, b, preferred_element_type=F32)


def dot_nt(a, b):
    return lax.dot_general(a, b, (((1,), (1,)), ((), ())), preferred_element_type=F32)


def dot_tn(a, b):
    return lax.dot_general(a, b, (((0,), (0,)), ((), ())), preferred_element_type=F32)


def split3(v):
    high = v.astype(BF16)
    rest = v - high.astype(F32)
    mid = rest.astype(BF16)
    low = (rest - mid.astype(F32)).astype(BF16)
    return high, mid, low


def spread(cols, first_head, head_size, rows):
    lane = lax.broadcasted_iota(jnp.int32, (rows, LANES), 1)
    out = jnp.broadcast_to(cols[:, first_head : first_head + 1], (rows, LANES))
    for k in range(1, LANES // head_size):
        nxt = cols[:, first_head + k : first_head + k + 1]
        out = jnp.where(lane >= k * head_size, nxt, out)
    return out


def scan_kernel(
    heads, take, halo, xbc, cum_o, dt_t, cum_t, pay, raw, carried
):
    hist = take(0)
    dtw, dtb, alog, cw, cb = take(1), take(2), take(3), take(4), take(5)
    length = hist.shape[0]
    edge = halo.shape[0]
    taps = cw.shape[0]
    width = xbc.shape[1]
    inner = carried.shape[1]
    state = (width - inner) // 2
    head_size = inner // heads
    per = LANES // head_size
    before = jnp.where(lax.axis_index("tm") == 0, 0.0, halo[...].astype(F32)).astype(BF16)
    rows = jnp.concatenate([before, hist[...]], axis=0)

    v = dot_nt(hist[...], dtw[...]) + dtb[...]
    dt = jnp.maximum(v, 0.0) + jnp.log1p(jnp.exp(-jnp.abs(v)))
    decay = -jnp.exp(alog[...]) * dt
    ri = lax.broadcasted_iota(jnp.int32, (length, length), 0)
    ci = lax.broadcasted_iota(jnp.int32, (length, length), 1)
    tri = jnp.where(ci <= ri, 1.0, 0.0).astype(BF16)
    parts = split3(decay)
    cum = dot(tri, parts[0]) + (dot(tri, parts[1]) + dot(tri, parts[2]))
    cum_o[...] = cum
    dt_t[...] = dt.T
    cum_t[...] = cum.T
    last = cum[length - 1 : length, :]
    weight = jnp.exp(last - cum) * dt

    step = 2 * LANES
    w = take(6)
    for start in list(range(inner, width, step)) + list(range(0, inner, step)):
        cols = slice(start, start + step)
        piece = dot(rows, w[:, cols]).astype(BF16).astype(F32)
        raw[:, cols] = piece
        first = start // LANES
        acc = jnp.concatenate(
            [jnp.broadcast_to(cb[k : k + 1, :], (length, LANES)) for k in (first, first + 1)], axis=1
        )
        for k in range(taps):
            acc = acc + cw[k : k + 1, cols] * raw[pl.ds(edge - (taps - 1) + k, length), cols]
        xbc[:, cols] = (acc / (1.0 + jnp.exp(-acc))).astype(BF16)
    for start in range(0, inner, LANES):
        cols = slice(start, start + LANES)
        x = xbc[:, cols].astype(F32)
        carried[:, cols] = (
            spread(weight, start // LANES * per, head_size, length) * x
        ).astype(BF16)
    b = xbc[:, inner : inner + state]
    pay[:state, :] = dot_tn(b, carried[...]).astype(BF16)
    gain = jnp.broadcast_to(jnp.exp(last), (ALIGN, heads))
    pick = lax.broadcasted_iota(jnp.int32, (ALIGN, LANES), 0)
    for start in range(0, inner, LANES):
        g = spread(gain, start // LANES * per, head_size, ALIGN)
        high = g.astype(BF16).astype(F32)
        pay[state:, start : start + LANES] = jnp.where(
            pick == 0, high, jnp.where(pick == 1, g - high, 0.0)
        ).astype(BF16)


def gain_row(pay, state):
    tail = pay[state:, :].astype(F32)
    return tail[0:1, :] + tail[1:2, :]


def chip_kernel(take, mine, other, out, gain_out):
    state = out.shape[0]
    odd = lax.rem(lax.axis_index("tm"), 2) == 1
    m = mine[:state, :].astype(F32)
    o = other[:state, :].astype(F32)
    gm = gain_row(mine, state)
    go = gain_row(other, state)
    out[...] = jnp.where(odd, o * gm + m, m * go + o).astype(BF16)
    gain_out[...] = jnp.broadcast_to(gm * go, gain_out.shape)


def within_kernel(heads, take, d_skip, xbc, cum, dt_t, cum_t, part, gate, pre):
    length, inner = part.shape
    state = (xbc.shape[1] - inner) // 2
    head_size = inner // heads
    per = LANES // head_size
    b = xbc[:, inner : inner + state]
    c = xbc[:, inner + state :]
    scores = dot_nt(c, b)
    half = length // 2
    tops = lax.broadcasted_iota(jnp.int32, (half, half), 0)
    lefts = lax.broadcasted_iota(jnp.int32, (half, half), 1)
    low_tri = lefts <= tops
    lane = lax.broadcasted_iota(jnp.int32, (length, LANES), 1)
    for start in range(0, inner, LANES):
        cols = slice(start, start + LANES)
        x = xbc[:, cols]
        out = None
        for k in range(per):
            h = start // LANES * per + k
            row = cum_t[h : h + 1, :]
            col = cum[:, h : h + 1]
            dts = dt_t[h : h + 1, :]

            def block(r, s, masked):
                gap = col[r : r + half] - row[:, s : s + half]
                if masked:
                    gap = jnp.where(low_tri, gap, 0.0)
                d = jnp.exp(gap)
                if masked:
                    d = jnp.where(low_tri, d, 0.0)
                return (d * dts[:, s : s + half] * scores[r : r + half, s : s + half]).astype(BF16)

            upper = dot(block(0, 0, True), x[:half])
            lower = dot(block(half, 0, False), x[:half]) + dot(block(half, half, True), x[half:])
            got = jnp.concatenate([upper, lower], axis=0)
            skip = d_skip[h]
            got = got + skip * x.astype(F32)
            out = got if out is None else jnp.where(lane >= k * head_size, got, out)
        part[:, cols] = out
    step = 2 * LANES
    hist, zw = take(0), take(1)
    for start in range(0, inner, step):
        cols = slice(start, start + step)
        z = dot(hist[...], zw[:, cols]).astype(BF16).astype(F32)
        gate[:, cols] = z / (1.0 + jnp.exp(-z))
    item, first = take(2), take(3)
    for start in range(0, pre.shape[1], step):
        cols = slice(start, start + step)
        pre[:, cols] = dot(item[...], first[:, cols])


def rank_kernel(
    heads,
    take,
    count,
    incoming,
    other,
    xbc,
    cum,
    part,
    gate,
    pre,
    enc_o,
    logit_o,
    send_o,
    keep_o,
    gated_s,
    rank_s,
    slope_s,
    hid_s,
    gp_s,
):
    length, inner = part.shape
    state = incoming.shape[0]
    head_size = inner // heads
    per = LANES // head_size
    slots = pre.shape[0]
    tm = lax.axis_index("tm")
    odd = lax.rem(tm, 2) == 1
    base = tm * length
    arrived = jnp.where(tm < 2, 0.0, incoming[...].astype(F32))
    enter = jnp.where(
        odd, arrived * gain_row(other, state) + other[:state, :].astype(F32), arrived
    )
    high = enter.astype(BF16)
    low = (enter - high.astype(F32)).astype(BF16)
    c = xbc[:, inner + state :]
    grow = jnp.exp(cum[...])
    total = jnp.zeros((length, LANES), F32)
    for start in range(0, inner, LANES):
        cols = slice(start, start + LANES)
        read = dot(c, high[:, cols]) + dot(c, low[:, cols])
        y = part[:, cols] + spread(grow, start // LANES * per, head_size, length) * read
        y = y * gate[:, cols]
        gated_s[:, cols] = y
        total = total + y * y
    mean = jnp.sum(total, axis=1, keepdims=True) * (1.0 / inner)
    scale = lax.rsqrt(mean + 1e-05)
    gain, ow = take(0), take(1)
    normed = (gated_s[...] * scale * gain[...]).astype(BF16)
    enc = dot(normed, ow[...]).astype(BF16)
    enc_o[...] = enc
    width = enc.shape[1]
    pos = take(2)
    place = pos[...] - base
    hot = (lax.broadcasted_iota(jnp.int32, (length, slots), 0) == place).astype(F32).astype(BF16)
    rank_s[...] = dot_tn(hot, enc).astype(BF16)

    hidden_width = pre.shape[1]
    step = 2 * LANES
    logit = jnp.zeros((slots, LANES), F32)
    first, second = take(3), take(4)
    weights2 = second[...].astype(F32)
    for start in range(0, hidden_width, step):
        cols = slice(start, start + step)
        v = pre[:, cols] + dot(rank_s[...], first[:, cols])
        sig = 1.0 / (1.0 + jnp.exp(-v))
        hid = (v * sig).astype(BF16)
        hid_s[:, cols] = hid
        k = start // LANES
        w2 = jnp.concatenate([weights2[k : k + 1], weights2[k + 1 : k + 2]], axis=1)
        prod = hid.astype(F32) * w2
        for k in range(0, step, LANES):
            logit = logit + prod[:, k : k + LANES]
        slope_s[:, cols] = w2 * (sig * (1.0 + v * (1.0 - sig)))
    ones = jnp.ones((8, LANES), BF16)
    p = split3(logit)
    logit8 = dot_nt(ones, p[0]) + (dot_nt(ones, p[1]) + dot_nt(ones, p[2]))
    slot = lax.broadcasted_iota(jnp.int32, (8, slots), 1)
    live = jnp.where(slot < count[0, 0], 1.0, 0.0)
    logit_o[...] = (live * logit8)[0:1, :]
    value = take(5)
    target = value[...].astype(F32)
    dl = live * (1.0 / (1.0 + jnp.exp(-logit8)) - target)
    d0, d1, d2 = split3(dl)
    which = lax.broadcasted_iota(jnp.int32, (8, slots), 0)
    dl3 = jnp.where(
        which == 0,
        d0.astype(F32),
        jnp.where(which == 1, d1.astype(F32), jnp.where(which == 2, d2.astype(F32), 0.0)),
    ).astype(BF16)
    grad2 = jnp.sum(dot(dl3, hid_s[...]), axis=0, keepdims=True)
    dcol = dot_tn(dl3, jnp.ones((8, LANES), BF16))
    for start in range(0, hidden_width, LANES):
        cols = slice(start, start + LANES)
        gp_s[:, cols] = (dcol * slope_s[:, cols]).astype(BF16)
    rows = width
    item = take(6)
    pick = lax.broadcasted_iota(jnp.int32, (8, hidden_width), 0)
    extra = jnp.where(pick == 0, grad2, 0.0).astype(BF16)
    away = jnp.where(odd, rank_s[...], item[...])
    home = jnp.where(odd, item[...], rank_s[...])
    send_o[:rows, :] = dot_tn(away, gp_s[...]).astype(BF16)
    send_o[rows:, :] = extra
    keep_o[:rows, :] = dot_tn(home, gp_s[...]).astype(BF16)
    keep_o[rows:, :] = extra


def loading(kernel, n_loaded, n_given, n_out, windows):
    def wrapped(*refs):
        sources = refs[:n_loaded]
        given = refs[n_loaded : n_loaded + n_given + n_out]
        rest = refs[n_loaded + n_given + n_out :]
        places, sems, scratch = rest[:n_loaded], rest[n_loaded], rest[n_loaded + 1 :]
        copies = []
        for i, source in enumerate(sources):
            window = windows.get(i)
            view = source if window is None else source.at[pl.ds(*window)]
            copies.append(pltpu.make_async_copy(view, places[i], sems.at[i]))
            copies[i].start()

        def take(i):
            copies[i].wait()
            return places[i]

        kernel(take, *given, *scratch)

    return wrapped


def call(kernel, loaded, given, out_shape, scratch, flops, moved, mib, windows=None, smem=0):
    windows = windows or {}
    places = []
    for i, value in enumerate(loaded):
        dims = value.shape if i not in windows else (windows[i][1],) + value.shape[1:]
        places.append(pltpu.VMEM(dims, value.dtype))
    return pl.pallas_call(
        loading(kernel, len(loaded), len(given), len(out_shape), windows),
        out_shape=out_shape,
        in_specs=[HBM] * len(loaded) + [SMEM] * smem + [VMEM] * (len(given) - smem),
        out_specs=[VMEM] * len(out_shape),
        scratch_shapes=places + [pltpu.SemaphoreType.DMA((max(len(loaded), 1),))] + scratch,
        compiler_params=pltpu.CompilerParams(vmem_limit_bytes=mib * 1024 * 1024),
        cost_estimate=pl.CostEstimate(flops=flops, bytes_accessed=moved, transcendentals=0),
    )(*[pltpu.with_memory_space_constraint(value, pltpu.HBM) for value in loaded], *given)


def shape(dims, dtype):
    return jax.ShapeDtypeStruct(dims, dtype)


def bits_of(n):
    return max(n.bit_length() - 1, 0)


def body(
    history,
    z_weight,
    xbc_weight,
    dt_weight,
    dt_bias,
    a_log,
    conv_weight,
    conv_bias,
    d_skip,
    norm_gain,
    out_weight,
    label_pos,
    label_count,
    label_value,
    item_feat,
    first_weight,
    second_weight,
):
    hist = history[0]
    item = item_feat[0]
    length, width = hist.shape
    inner = z_weight.shape[1]
    heads = a_log.shape[0]
    channels = xbc_weight.shape[1]
    state = (channels - inner) // 2
    slots = label_pos.shape[1]
    hidden = first_weight.shape[1]
    n_tm = lax.axis_size("tm")
    n_user = lax.axis_size("user")
    chips = n_tm // 2
    tm = lax.axis_index("tm")
    user = lax.axis_index("user")

    halo = lax.ppermute(hist[length - ALIGN :], "tm", [(i, (i + 1) % n_tm) for i in range(n_tm)])
    xbc, cum, dt_t, cum_t, pay = call(
        functools.partial(scan_kernel, heads),
        (
            hist,
            dt_weight.T,
            dt_bias.reshape(1, heads),
            a_log.reshape(1, heads),
            conv_weight,
            conv_bias.reshape(channels // LANES, LANES),
            xbc_weight,
        ),
        (halo,),
        (
            shape((length, channels), BF16),
            shape((length, heads), F32),
            shape((heads, length), F32),
            shape((heads, length), F32),
            shape((state + ALIGN, inner), BF16),
        ),
        [pltpu.VMEM((length + ALIGN, channels), F32), pltpu.VMEM((length, inner), BF16)],
        2 * length * width * channels,
        4 * width * channels,
        16,
    )
    other = lax.ppermute(pay, "tm", [(i, i ^ 1) for i in range(n_tm)])
    chip_state, chip_gain = call(
        chip_kernel,
        (),
        (pay, other),
        (shape((state, inner), BF16), shape((8, inner), F32)),
        [],
        state * inner,
        6 * state * inner,
        6,
    )
    onward = [(i, (i + 2) % n_tm) for i in range(n_tm)]
    incoming = lax.ppermute(chip_state, "tm", onward)
    for _ in range(chips - 2):
        incoming = jnp.where(tm < 2, 0.0, incoming.astype(F32))
        passed = chip_gain[0:1] * incoming + chip_state.astype(F32)
        incoming = lax.ppermute(passed.astype(BF16), "tm", onward)
    part, gate, pre = call(
        functools.partial(within_kernel, heads),
        (hist, z_weight, item, first_weight),
        (d_skip, xbc, cum, dt_t, cum_t),
        (
            shape((length, inner), F32),
            shape((length, inner), F32),
            shape((slots, hidden), F32),
        ),
        [],
        2 * length * width * inner + 2 * slots * width * hidden + 4 * length * length * inner,
        16 * length * inner * 4,
        20,
        {3: (width, width)},
        1,
    )
    enc, row_logit, send, keep = call(
        functools.partial(rank_kernel, heads),
        (
            norm_gain.reshape(1, inner),
            out_weight,
            label_pos,
            first_weight,
            second_weight.reshape(hidden // LANES, LANES),
            label_value,
            item,
        ),
        (label_count, incoming, other, xbc, cum, part, gate, pre),
        (
            shape((length, width), BF16),
            shape((1, slots), F32),
            shape((width + 8, hidden), BF16),
            shape((width + 8, hidden), BF16),
        ),
        [
            pltpu.VMEM((length, inner), F32),
            pltpu.VMEM((slots, width), BF16),
            pltpu.VMEM((slots, hidden), F32),
            pltpu.VMEM((slots, hidden), BF16),
            pltpu.VMEM((slots, hidden), BF16),
        ],
        4 * slots * width * hidden,
        8 * slots * hidden,
        24,
        {3: (0, width)},
        1,
    )
    grad_first, grad_second = total_sum(send, keep, n_user, n_tm, user, tm)
    return (enc[None], row_logit, grad_first, grad_second)


def total_sum(send, keep, n_user, n_tm, user, tm):
    rows = keep.shape[0] - 8
    odd = tm % 2
    axes = ("user", "tm")
    every = [(u, t) for u in range(n_user) for t in range(n_tm)]
    chunks = len((1, 1, 1, 1))

    def swap(value, partner):
        pairs = [(u * n_tm + t, partner(u, t)) for u, t in every]
        return lax.ppermute(value, axes, pairs)

    def across(u, t):
        return u * n_tm + (t ^ 1)

    chip_bits = [("tm", k) for k in range(bits_of(n_tm // 2))]
    user_bits = [("user", k) for k in range(bits_of(n_user))]
    order_even = chip_bits + user_bits
    order_odd = user_bits + chip_bits

    def partner_of(level):
        def partner(u, t):
            axis, k = (order_even if t % 2 == 0 else order_odd)[level]
            if axis == "tm":
                return u * n_tm + (t ^ (2 << k))
            return (u ^ (1 << k)) * n_tm + t

        return partner

    def bit_of(level):
        def one(entry):
            axis, k = entry
            return (tm >> (k + 1)) & 1 if axis == "tm" else (user >> k) & 1

        return jnp.where(odd == 0, one(order_even[level]), one(order_odd[level])) == 1

    levels = len(order_even)
    bits = [bit_of(level) for level in range(levels)]
    bit = odd == 1
    edges = [rows * sum((1, 1, 1, 1)[:k]) // sum((1, 1, 1, 1)) for k in range(chunks + 1)]
    pieces = []
    for k in range(chunks):
        last = k == chunks - 1
        stop = edges[k + 1] + (8 if last else 0)
        pieces.append((send[edges[k] : stop], keep[edges[k] : stop], last))
    state = []
    for leave, stay, has_extra in pieces:
        size = stay.shape[0] - (8 if has_extra else 0)
        got = swap(leave, across)
        extra = None
        if has_extra:
            extra = (stay[size:].astype(F32) + got[size:].astype(F32)).astype(BF16)
        state.append((stay[:size], got[:size], extra))
    for level in range(levels - 1):
        after = []
        for a, b, extra in state:
            size = a.shape[0] // 2
            low = a[:size].astype(F32) + b[:size].astype(F32)
            high = a[size:].astype(F32) + b[size:].astype(F32)
            leave = jnp.where(bits[level], low, high).astype(BF16)
            stay = jnp.where(bits[level], high, low).astype(BF16)
            if extra is not None:
                leave = jnp.concatenate([leave, extra], axis=0)
            got = swap(leave, partner_of(level))
            if extra is not None:
                extra = (extra.astype(F32) + got[size:].astype(F32)).astype(BF16)
            after.append((stay, got[:size], extra))
        state = after
    wholes = []
    for a, b, extra in state:
        size = a.shape[0]
        whole = (a.astype(F32) + b.astype(F32)).astype(BF16)
        if levels:
            leave = whole if extra is None else jnp.concatenate([whole, extra], axis=0)
            got = swap(leave, partner_of(levels - 1))
            whole = (whole.astype(F32) + got[:size].astype(F32)).astype(BF16)
            if extra is not None:
                extra = (extra.astype(F32) + got[size:].astype(F32)).astype(BF16)
        wholes.append((whole, extra))
    for level in reversed(range(levels - 1)):
        after = []
        for whole, extra in wholes:
            got = swap(whole, partner_of(level))
            first = jnp.where(bits[level], got, whole)
            second = jnp.where(bits[level], whole, got)
            after.append((jnp.concatenate([first, second], axis=0), extra))
        wholes = after
    tops, bottoms = [], []
    for whole, extra in wholes:
        n = whole.shape[0]
        if extra is None:
            got = swap(whole, across)
        else:
            got = swap(jnp.concatenate([whole, extra], axis=0), across)
            grad_second = jnp.where(bit, got[n:], extra)[0].astype(F32)
            got = got[:n]
        tops.append(jnp.where(bit, got, whole).astype(F32))
        bottoms.append(jnp.where(bit, whole, got).astype(F32))
    return jnp.concatenate(tops + bottoms, axis=0), grad_second


def solution(mesh):
    in_specs = (
        P(("grp", "user"), "tm", None),
        P(),
        P(),
        P(),
        P(),
        P(),
        P(),
        P(),
        P(),
        P(),
        P(),
        P(("grp", "user"), "tm"),
        P(("grp", "user"), "tm"),
        P(("grp", "user"), "tm"),
        P(("grp", "user"), "tm", None),
        P(),
        P(),
    )
    out_specs = (P(("grp", "user"), "tm", None), P(("grp", "user"), "tm"), P("grp", None), P("grp"))
    return jax.shard_map(body, mesh=mesh, in_specs=in_specs, out_specs=out_specs, check_vma=False)
```

```python
import functools

import jax
import jax.numpy as jnp
from jax import lax
from jax.experimental import pallas as pl
from jax.experimental.pallas import tpu as pltpu
from jax.sharding import PartitionSpec as P

F32 = jnp.float32
BF16 = jnp.bfloat16
LANES = 128
ALIGN = 16
CHUNKS = 4
VMEM = pl.BlockSpec(memory_space=pltpu.VMEM)
SMEM = pl.BlockSpec(memory_space=pltpu.SMEM)
HBM = pl.BlockSpec(memory_space=pltpu.HBM)


def dot(a, b):
    return jnp.dot(a, b, preferred_element_type=F32)


def dot_nt(a, b):
    return lax.dot_general(a, b, (((1,), (1,)), ((), ())), preferred_element_type=F32)


def dot_tn(a, b):
    return lax.dot_general(a, b, (((0,), (0,)), ((), ())), preferred_element_type=F32)


def logistic(v):
    return 0.5 + 0.5 * jnp.tanh(0.5 * v)


def split3(v):
    high = v.astype(BF16)
    rest = v - high.astype(F32)
    mid = rest.astype(BF16)
    low = (rest - mid.astype(F32)).astype(BF16)
    return high, mid, low


def spread(cols, first_head, head_size, rows):
    lane = lax.broadcasted_iota(jnp.int32, (rows, LANES), 1)
    out = jnp.broadcast_to(cols[:, first_head : first_head + 1], (rows, LANES))
    for k in range(1, LANES // head_size):
        nxt = cols[:, first_head + k : first_head + k + 1]
        out = jnp.where(lane >= k * head_size, nxt, out)
    return out


def convolve(raw, bias, taps, cols, first, count):
    start = cols.start // LANES
    stop = cols.stop // LANES
    acc = jnp.concatenate(
        [jnp.broadcast_to(bias[k : k + 1, :], (count, LANES)) for k in range(start, stop)], axis=1
    )
    n = taps.shape[0]
    for k in range(n):
        acc = acc + taps[k : k + 1, cols] * raw[pl.ds(first - (n - 1) + k, count), cols]
    return (acc * logistic(acc)).astype(BF16)


def scan_kernel(heads, take, xbc, cum_o, dt_t, cum_t, weight_o, last_o, head_o, sum_o, raw, carried):
    hist = take(0)
    dtw, dtb, alog = take(1), take(2), take(3)
    length, width = xbc.shape
    inner = carried.shape[1]
    state = (width - inner) // 2
    head_size = inner // heads
    per = LANES // head_size

    v = dot_nt(hist[...], dtw[...]) + dtb[...]
    dt = jnp.maximum(v, 0.0) + jnp.log1p(jnp.exp(-jnp.abs(v)))
    decay = -jnp.exp(alog[...]) * dt
    ri = lax.broadcasted_iota(jnp.int32, (length, length), 0)
    ci = lax.broadcasted_iota(jnp.int32, (length, length), 1)
    tri = jnp.where(ci <= ri, 1.0, 0.0).astype(BF16)
    parts = split3(decay)
    cum = dot(tri, parts[0]) + (dot(tri, parts[1]) + dot(tri, parts[2]))
    cum_o[...] = cum
    dt_t[...] = dt.T
    cum_t[...] = cum.T
    last = cum[length - 1 : length, :]
    weight = jnp.exp(last - cum) * dt
    weight_o[...] = weight[:ALIGN]
    last_o[...] = jnp.broadcast_to(jnp.exp(last), last_o.shape)

    step = 2 * LANES
    cw, cb, w = take(4), take(5), take(6)
    raw[:ALIGN, :] = jnp.zeros((ALIGN, width), F32)
    for start in list(range(inner, width, step)) + list(range(0, inner, step)):
        cols = slice(start, start + step)
        raw[ALIGN:, cols] = dot(hist[...], w[:, cols]).astype(BF16).astype(F32)
        xbc[:, cols] = convolve(raw, cb, cw, cols, ALIGN, length)
    head_o[...] = raw[ALIGN : 2 * ALIGN, :]
    for start in range(0, inner, LANES):
        cols = slice(start, start + LANES)
        x = xbc[:, cols].astype(F32)
        carried[:, cols] = (
            spread(weight, start // LANES * per, head_size, length) * x
        ).astype(BF16)
    b = xbc[ALIGN:, inner : inner + state]
    sum_o[...] = dot_tn(b, carried[ALIGN:, :])


def edge_kernel(heads, take, halo, w, cw, cb, weight, last, head, later, old, xbc, pay, raw):
    width = xbc.shape[1]
    state, inner = later.shape
    head_size = inner // heads
    per = LANES // head_size
    before = jnp.where(lax.axis_index("tm") == 0, 0.0, halo[...].astype(F32)).astype(BF16)
    raw[:ALIGN, :] = dot(before, w[...]).astype(BF16).astype(F32)
    raw[ALIGN:, :] = head[...]
    top = convolve(raw, cb, cw, slice(0, width), ALIGN, ALIGN)
    xbc[:ALIGN, :] = top
    gain = last[...]
    pick = lax.broadcasted_iota(jnp.int32, (ALIGN, LANES), 0)
    b = top[:, inner : inner + state]
    for start in range(0, inner, LANES):
        cols = slice(start, start + LANES)
        h = start // LANES * per
        carried = (spread(weight[...], h, head_size, ALIGN) * top[:, cols].astype(F32)).astype(BF16)
        pay[:state, cols] = (later[:, cols] + dot_tn(b, carried)).astype(BF16)
        g = spread(gain, h, head_size, ALIGN)
        high = g.astype(BF16).astype(F32)
        pay[state:, cols] = jnp.where(
            pick == 0, high, jnp.where(pick == 1, g - high, 0.0)
        ).astype(BF16)


def gain_row(pay, state):
    tail = pay[state:, :].astype(F32)
    return tail[0:1, :] + tail[1:2, :]


def chip_kernel(take, mine, other, out, gain_out):
    state = out.shape[0]
    odd = lax.rem(lax.axis_index("tm"), 2) == 1
    m = mine[:state, :].astype(F32)
    o = other[:state, :].astype(F32)
    gm = gain_row(mine, state)
    go = gain_row(other, state)
    out[...] = jnp.where(odd, o * gm + m, m * go + o).astype(BF16)
    gain_out[...] = jnp.broadcast_to(gm * go, gain_out.shape)


def within_kernel(
    heads, take, d_skip, xbc, cum, dt_t, cum_t, own, across, pre, hot_o, hot_t_o, item_t_o, part
):
    length, inner = part.shape
    slots = hot_o.shape[0]
    state = (xbc.shape[1] - inner) // 2
    head_size = inner // heads
    per = LANES // head_size
    b = xbc[:, inner : inner + state]
    c = xbc[:, inner + state :]
    scores = dot_nt(c, b)
    half = length // 2
    tops = lax.broadcasted_iota(jnp.int32, (half, half), 0)
    lefts = lax.broadcasted_iota(jnp.int32, (half, half), 1)
    low_tri = lefts <= tops
    lane = lax.broadcasted_iota(jnp.int32, (length, LANES), 1)
    for start in range(0, inner, LANES):
        cols = slice(start, start + LANES)
        x = xbc[:, cols]
        out = None
        for k in range(per):
            h = start // LANES * per + k
            row = cum_t[h : h + 1, :]
            col = cum[:, h : h + 1]
            dts = dt_t[h : h + 1, :]

            def block(r, s, masked):
                gap = col[r : r + half] - row[:, s : s + half]
                if masked:
                    gap = jnp.where(low_tri, gap, 0.0)
                d = jnp.exp(gap)
                if masked:
                    d = jnp.where(low_tri, d, 0.0)
                return (d * dts[:, s : s + half] * scores[r : r + half, s : s + half]).astype(BF16)

            upper = dot(block(0, 0, True), x[:half])
            lower = dot(block(half, 0, False), x[:half]) + dot(block(half, half, True), x[half:])
            got = jnp.concatenate([upper, lower], axis=0)
            skip = d_skip[h]
            got = got + skip * x.astype(F32)
            out = got if out is None else jnp.where(lane >= k * head_size, got, out)
        part[:, cols] = out
    step = 2 * LANES
    grow = jnp.exp(cum[...])
    hist, zw = take(0), take(1)
    for start in range(0, inner, step):
        cols = slice(start, start + step)
        z = dot(hist[...], zw[:, cols]).astype(BF16).astype(F32)
        gate = z * logistic(z)
        own[:, cols] = part[:, cols] * gate
        for k in range(0, step, LANES):
            first_head = (start + k) // LANES * per
            across[:, start + k : start + k + LANES] = (
                spread(grow, first_head, head_size, length) * gate[:, k : k + LANES]
            )
    item, first = take(2), take(3)
    for start in range(0, pre.shape[1], step):
        cols = slice(start, start + step)
        pre[:, cols] = dot(item[...], first[:, cols])
    item_t_o[...] = item[...].T
    place = take(4)[...] - lax.axis_index("tm") * length
    hot = jnp.where(lax.broadcasted_iota(jnp.int32, (length, slots), 0) == place, 1.0, 0.0)
    hot_t_o[...] = hot.astype(BF16)
    hot_o[...] = hot.T.astype(BF16)


def rank_kernel(
    take,
    count,
    incoming,
    other,
    xbc,
    own,
    across,
    pre,
    hot,
    hot_t,
    item_t,
    enc_o,
    logit_o,
    gp_s,
    rank_o,
    *rest,
):
    send_o = rest[:CHUNKS]
    gated_s, rank_s, slope_s, hid_s, enc_s, enc_sem = rest[CHUNKS:]
    length, inner = own.shape
    state = incoming.shape[0]
    slots = pre.shape[0]
    tm = lax.axis_index("tm")
    odd = lax.rem(tm, 2) == 1
    arrived = jnp.where(tm < 2, 0.0, incoming[...].astype(F32))
    enter = jnp.where(
        odd, arrived * gain_row(other, state) + other[:state, :].astype(F32), arrived
    )
    entering = enter.astype(BF16)
    c = xbc[:, inner + state :]
    total = jnp.zeros((length, LANES), F32)
    for start in range(0, inner, LANES):
        cols = slice(start, start + LANES)
        read = dot(c, entering[:, cols])
        y = own[:, cols] + across[:, cols] * read
        gated_s[:, cols] = y
        total = total + y * y
    mean = jnp.sum(total, axis=1, keepdims=True) * (1.0 / inner)
    scale = lax.rsqrt(mean + 1e-05)
    gain, ow = take(0), take(1)
    normed = (gated_s[...] * scale * gain[...]).astype(BF16)
    enc = dot(normed, ow[...]).astype(BF16)
    enc_s[...] = enc
    leaving = pltpu.make_async_copy(enc_s, enc_o, enc_sem)
    leaving.start()
    width = enc.shape[1]
    rank_s[...] = dot(hot[...], enc).astype(BF16)
    rank_t = dot(enc.T, hot_t[...]).astype(BF16)

    hidden_width = pre.shape[1]
    step = 2 * LANES
    logit = jnp.zeros((slots, LANES), F32)
    first, second = take(2), take(3)
    weights2 = second[...].astype(F32)
    for start in range(0, hidden_width, step):
        cols = slice(start, start + step)
        v = pre[:, cols] + dot(rank_s[...], first[:, cols])
        sig = logistic(v)
        silu = v * sig
        hid = silu.astype(BF16)
        hid_s[:, cols] = hid
        k = start // LANES
        w2 = jnp.concatenate([weights2[k : k + 1], weights2[k + 1 : k + 2]], axis=1)
        prod = hid.astype(F32) * w2
        for k in range(0, step, LANES):
            logit = logit + prod[:, k : k + LANES]
        slope_s[:, cols] = w2 * (sig + silu * (1.0 - sig))
    ones = jnp.ones((8, LANES), BF16)
    p = split3(logit)
    logit8 = dot_nt(ones, p[0]) + (dot_nt(ones, p[1]) + dot_nt(ones, p[2]))
    slot = lax.broadcasted_iota(jnp.int32, (8, slots), 1)
    live = jnp.where(slot < count[0, 0], 1.0, 0.0)
    logit_o[...] = (live * logit8)[0:1, :]
    value = take(4)
    target = value[...].astype(F32)
    dl = live * (1.0 / (1.0 + jnp.exp(-logit8)) - target)
    d0, d1, d2 = split3(dl)
    which = lax.broadcasted_iota(jnp.int32, (8, slots), 0)
    dl3 = jnp.where(
        which == 0,
        d0.astype(F32),
        jnp.where(which == 1, d1.astype(F32), jnp.where(which == 2, d2.astype(F32), 0.0)),
    ).astype(BF16)
    grad2 = jnp.sum(dot(dl3, hid_s[...]), axis=0, keepdims=True)
    dcol = dot_tn(dl3, jnp.ones((8, LANES), BF16))
    for start in range(0, hidden_width, LANES):
        cols = slice(start, start + LANES)
        gp_s[:, cols] = (dcol * slope_s[:, cols]).astype(BF16)
    rows = width
    pick = lax.broadcasted_iota(jnp.int32, (8, hidden_width), 0)
    extra = jnp.where(pick == 0, grad2, 0.0).astype(BF16)
    away = jnp.where(odd, rank_t, item_t[...])
    rank_o[...] = rank_t
    size = rows // CHUNKS
    for k in range(CHUNKS):
        part = away[k * size : (k + 1) * size]
        send_o[k][:size, :] = dot(part, gp_s[...]).astype(BF16)
    send_o[CHUNKS - 1][size:, :] = extra
    leaving.wait()


def home_kernel(take, rank_t, item_t, slope, last_sent, *keep_o):
    size = rank_t.shape[0] // CHUNKS
    odd = lax.rem(lax.axis_index("tm"), 2) == 1
    for k in range(CHUNKS):
        part = slice(k * size, (k + 1) * size)
        home = jnp.where(odd, item_t[part, :], rank_t[part, :])
        keep_o[k][:size, :] = dot(home, slope[...]).astype(BF16)
    keep_o[CHUNKS - 1][size:, :] = last_sent[size:, :]


def chunk_shapes(rows, columns):
    size = rows // CHUNKS
    last = size + 8
    return tuple(shape((last if k == CHUNKS - 1 else size, columns), BF16) for k in range(CHUNKS))


def loading(kernel, n_loaded, n_given, n_out, windows, kept):
    def wrapped(*refs):
        sources = refs[:n_loaded]
        given = refs[n_loaded : n_loaded + n_given + n_out]
        first_kept = n_loaded + n_given + n_out
        results = list(refs[first_kept : first_kept + len(kept)])
        rest = list(refs[first_kept + len(kept) :])
        places = [results.pop(0) if i in kept else rest.pop(0) for i in range(n_loaded)]
        sems, scratch = rest[0], rest[1:]
        copies = []
        for i, source in enumerate(sources):
            window = windows.get(i)
            view = source if window is None else source.at[pl.ds(*window)]
            copies.append(pltpu.make_async_copy(view, places[i], sems.at[i]))
            copies[i].start()

        def take(i):
            copies[i].wait()
            return places[i]

        kernel(take, *given, *scratch)

    return wrapped


def call(
    kernel,
    loaded,
    given,
    out_shape,
    scratch,
    flops,
    moved,
    mib,
    windows=None,
    smem=0,
    kept=(),
    aliases=None,
    outside=(),
):
    windows = windows or {}
    places = []
    for i, value in enumerate(loaded):
        dims = value.shape if i not in windows else (windows[i][1],) + value.shape[1:]
        if i not in kept:
            places.append(pltpu.VMEM(dims, value.dtype))
    outs = tuple(out_shape) + tuple(shape(loaded[i].shape, loaded[i].dtype) for i in kept)
    return pl.pallas_call(
        loading(kernel, len(loaded), len(given), len(out_shape), windows, kept),
        out_shape=outs,
        in_specs=[HBM] * len(loaded) + [SMEM] * smem + [VMEM] * (len(given) - smem),
        out_specs=[HBM if i in outside else VMEM for i in range(len(outs))],
        scratch_shapes=places + [pltpu.SemaphoreType.DMA((max(len(loaded), 1),))] + scratch,
        compiler_params=pltpu.CompilerParams(vmem_limit_bytes=mib * 1024 * 1024),
        cost_estimate=pl.CostEstimate(flops=flops, bytes_accessed=moved, transcendentals=0),
        input_output_aliases=aliases or {},
    )(*[pltpu.with_memory_space_constraint(value, pltpu.HBM) for value in loaded], *given)


def shape(dims, dtype):
    return jax.ShapeDtypeStruct(dims, dtype)


def bits_of(n):
    return max(n.bit_length() - 1, 0)


def body(
    history,
    z_weight,
    xbc_weight,
    dt_weight,
    dt_bias,
    a_log,
    conv_weight,
    conv_bias,
    d_skip,
    norm_gain,
    out_weight,
    label_pos,
    label_count,
    label_value,
    item_feat,
    first_weight,
    second_weight,
):
    hist = history[0]
    item = item_feat[0]
    length, width = hist.shape
    inner = z_weight.shape[1]
    heads = a_log.shape[0]
    channels = xbc_weight.shape[1]
    state = (channels - inner) // 2
    slots = label_pos.shape[1]
    hidden = first_weight.shape[1]
    n_tm = lax.axis_size("tm")
    n_user = lax.axis_size("user")
    chips = n_tm // 2
    tm = lax.axis_index("tm")
    user = lax.axis_index("user")

    halo = lax.ppermute(hist[length - ALIGN :], "tm", [(i, (i + 1) % n_tm) for i in range(n_tm)])
    early, cum, dt_t, cum_t, weight, last, head, later, taps, bias, w = call(
        functools.partial(scan_kernel, heads),
        (
            hist,
            dt_weight.T,
            dt_bias.reshape(1, heads),
            a_log.reshape(1, heads),
            conv_weight,
            conv_bias.reshape(channels // LANES, LANES),
            xbc_weight,
        ),
        (),
        (
            shape((length, channels), BF16),
            shape((length, heads), F32),
            shape((heads, length), F32),
            shape((heads, length), F32),
            shape((ALIGN, heads), F32),
            shape((ALIGN, heads), F32),
            shape((ALIGN, channels), F32),
            shape((state, inner), F32),
        ),
        [pltpu.VMEM((length + ALIGN, channels), F32), pltpu.VMEM((length, inner), BF16)],
        2 * length * width * channels,
        4 * width * channels,
        16,
        kept=(4, 5, 6),
    )
    xbc, pay = call(
        functools.partial(edge_kernel, heads),
        (),
        (halo, w, taps, bias, weight, last, head, later, early),
        (shape((length, channels), BF16), shape((state + ALIGN, inner), BF16)),
        [pltpu.VMEM((2 * ALIGN, channels), F32)],
        2 * ALIGN * width * channels,
        2 * width * channels,
        10,
        aliases={8: 0},
    )
    other = lax.ppermute(pay, "tm", [(i, i ^ 1) for i in range(n_tm)])
    chip_state, chip_gain = call(
        chip_kernel,
        (),
        (pay, other),
        (shape((state, inner), BF16), shape((8, inner), F32)),
        [],
        state * inner,
        6 * state * inner,
        6,
    )
    onward = [(i, (i + 2) % n_tm) for i in range(n_tm)]
    incoming = lax.ppermute(chip_state, "tm", onward)
    for _ in range(chips - 2):
        incoming = jnp.where(tm < 2, 0.0, incoming.astype(F32))
        passed = chip_gain[0:1] * incoming + chip_state.astype(F32)
        incoming = lax.ppermute(passed.astype(BF16), "tm", onward)
    own, across, pre, hot, hot_t, item_t = call(
        functools.partial(within_kernel, heads),
        (hist, z_weight, item, first_weight, label_pos),
        (d_skip, xbc, cum, dt_t, cum_t),
        (
            shape((length, inner), F32),
            shape((length, inner), F32),
            shape((slots, hidden), F32),
            shape((slots, length), BF16),
            shape((length, slots), BF16),
            shape((width, slots), BF16),
        ),
        [pltpu.VMEM((length, inner), F32)],
        2 * length * width * inner + 2 * slots * width * hidden + 4 * length * length * inner,
        16 * length * inner * 4,
        24,
        {3: (width, width)},
        1,
    )
    enc, row_logit, slope, rank_t, *send = call(
        rank_kernel,
        (
            norm_gain.reshape(1, inner),
            out_weight,
            first_weight,
            second_weight.reshape(hidden // LANES, LANES),
            label_value,
        ),
        (label_count, incoming, other, xbc, own, across, pre, hot, hot_t, item_t),
        (
            shape((length, width), BF16),
            shape((1, slots), F32),
            shape((slots, hidden), BF16),
            shape((width, slots), BF16),
        )
        + chunk_shapes(width, hidden),
        [
            pltpu.VMEM((length, inner), F32),
            pltpu.VMEM((slots, width), BF16),
            pltpu.VMEM((slots, hidden), F32),
            pltpu.VMEM((slots, hidden), BF16),
            pltpu.VMEM((length, width), BF16),
            pltpu.SemaphoreType.DMA,
        ],
        4 * slots * width * hidden,
        8 * slots * hidden,
        24,
        {2: (0, width)},
        1,
        outside=(0,),
    )
    keep = call(
        home_kernel,
        (),
        (rank_t, item_t, slope, send[-1]),
        chunk_shapes(width, hidden),
        [],
        2 * slots * width * hidden,
        4 * slots * hidden,
        8,
    )
    grad_first, grad_second = total_sum(send, keep, n_user, n_tm, user, tm)
    return (enc[None], row_logit, grad_first, grad_second)


def total_sum(send, keep, n_user, n_tm, user, tm):
    rows = sum(part.shape[0] for part in keep) - 8
    odd = tm % 2
    axes = ("user", "tm")
    every = [(u, t) for u in range(n_user) for t in range(n_tm)]
    chunks = CHUNKS

    def swap(value, partner):
        pairs = [(u * n_tm + t, partner(u, t)) for u, t in every]
        return lax.ppermute(value, axes, pairs)

    def across(u, t):
        return u * n_tm + (t ^ 1)

    chip_bits = [("tm", k) for k in range(bits_of(n_tm // 2))]
    user_bits = [("user", k) for k in range(bits_of(n_user))]
    order_even = chip_bits + user_bits
    order_odd = user_bits + chip_bits

    def partner_of(level):
        def partner(u, t):
            axis, k = (order_even if t % 2 == 0 else order_odd)[level]
            if axis == "tm":
                return u * n_tm + (t ^ (2 << k))
            return (u ^ (1 << k)) * n_tm + t

        return partner

    def bit_of(level):
        def one(entry):
            axis, k = entry
            return (tm >> (k + 1)) & 1 if axis == "tm" else (user >> k) & 1

        return jnp.where(odd == 0, one(order_even[level]), one(order_odd[level])) == 1

    levels = len(order_even)
    bits = [bit_of(level) for level in range(levels)]
    size = rows // chunks
    state = []
    for leave, stay in zip(send, keep):
        got = swap(leave, across)
        extra = None
        if stay.shape[0] > size:
            extra = (stay[size:].astype(F32) + got[size:].astype(F32)).astype(BF16)
        state.append((stay[:size], got[:size], extra))
    for level in range(levels - 1):
        after = []
        for a, b, extra in state:
            size = a.shape[0] // 2
            low = a[:size].astype(F32) + b[:size].astype(F32)
            high = a[size:].astype(F32) + b[size:].astype(F32)
            leave = jnp.where(bits[level], low, high).astype(BF16)
            stay = jnp.where(bits[level], high, low).astype(BF16)
            if extra is not None:
                leave = jnp.concatenate([leave, extra], axis=0)
            got = swap(leave, partner_of(level))
            if extra is not None:
                extra = (extra.astype(F32) + got[size:].astype(F32)).astype(BF16)
            after.append((stay, got[:size], extra))
        state = after
    wholes = []
    for a, b, extra in state:
        size = a.shape[0]
        whole = (a.astype(F32) + b.astype(F32)).astype(BF16)
        if levels:
            leave = whole if extra is None else jnp.concatenate([whole, extra], axis=0)
            got = swap(leave, partner_of(levels - 1))
            whole = (whole.astype(F32) + got[:size].astype(F32)).astype(BF16)
            if extra is not None:
                extra = (extra.astype(F32) + got[size:].astype(F32)).astype(BF16)
        wholes.append((whole, extra))
    for level in reversed(range(levels - 1)):
        after = []
        for whole, extra in wholes:
            got = swap(whole, partner_of(level))
            first = jnp.where(bits[level], got, whole)
            second = jnp.where(bits[level], whole, got)
            after.append((jnp.concatenate([first, second], axis=0), extra))
        wholes = after
    arrived = []
    for whole, extra in wholes:
        arrived.append(
            swap(whole if extra is None else jnp.concatenate([whole, extra], axis=0), across)
        )
    own_extra = wholes[-1][1]
    mine = [whole for whole, _ in wholes]
    total = (2 * rows,) + mine[0].shape[1:]
    last = chunks - 1
    own = [(w, 0, k) for k, w in enumerate(mine)]
    other = [(w, 1, k) for k, w in enumerate(arrived)]
    grad_first = written(None, own + other[:last], rows, total)
    grad_first, grad_second = written(grad_first, other[last:], rows, total, own_extra)
    return grad_first, grad_second.reshape(total[1:])


def written(so_far, blocks, half_rows, total, own_extra=None):
    size = blocks[0][0].shape[0]
    size -= size % LANES
    given = [value for value, _, _ in blocks]
    n = len(given)
    wide = given[-1].shape[0] > size
    aliased = so_far is not None

    def kernel(*refs):
        refs = list(refs)
        if aliased:
            refs.pop(0)
        values = [refs.pop(0) for _ in range(n)]
        mine = refs.pop(0) if wide else None
        out = refs.pop(0)
        second = refs.pop(0) if wide else None
        buf, sems = refs
        odd = lax.rem(lax.axis_index("tm"), 2)
        copies = []
        for i, (_, other, k) in enumerate(blocks):
            buf[i] = values[i][:size, :].astype(F32)
            side = 1 - odd if other else odd
            at = pl.multiple_of(side * half_rows + k * size, 8)
            copies.append(pltpu.make_async_copy(buf.at[i], out.at[pl.ds(at, size)], sems.at[i]))
            copies[i].start()
        if wide:
            own = mine[...].astype(F32)[0:1]
            got = values[-1][size:, :].astype(F32)[0:1]
            second[...] = jnp.where(odd == 1, got, own)
        for copy in copies:
            copy.wait()

    outs = [jax.ShapeDtypeStruct(total, F32)]
    if wide:
        outs.append(jax.ShapeDtypeStruct((1, total[1]), F32))
        given = given + [own_extra]
    operands = given
    if aliased:
        operands = [pltpu.with_memory_space_constraint(so_far, pltpu.HBM)] + given
    result = pl.pallas_call(
        kernel,
        out_shape=tuple(outs),
        in_specs=[HBM] * aliased + [VMEM] * len(given),
        out_specs=tuple([HBM] + [VMEM] * wide),
        scratch_shapes=[pltpu.VMEM((n, size, total[1]), F32), pltpu.SemaphoreType.DMA((n,))],
        input_output_aliases={0: 0} if aliased else {},
        compiler_params=pltpu.CompilerParams(vmem_limit_bytes=12 * 1024 * 1024),
        cost_estimate=pl.CostEstimate(
            flops=n * size * total[1], bytes_accessed=6 * n * size * total[1], transcendentals=0
        ),
    )(*operands)
    return result if wide else result[0]


def solution(mesh):
    in_specs = (
        P(("grp", "user"), "tm", None),
        P(),
        P(),
        P(),
        P(),
        P(),
        P(),
        P(),
        P(),
        P(),
        P(),
        P(("grp", "user"), "tm"),
        P(("grp", "user"), "tm"),
        P(("grp", "user"), "tm"),
        P(("grp", "user"), "tm", None),
        P(),
        P(),
    )
    out_specs = (P(("grp", "user"), "tm", None), P(("grp", "user"), "tm"), P("grp", None), P("grp"))
    return jax.shard_map(body, mesh=mesh, in_specs=in_specs, out_specs=out_specs, check_vma=False)
```

```python
import functools

import jax
import jax.numpy as jnp
from jax import lax
from jax.experimental import pallas as pl
from jax.experimental.pallas import tpu as pltpu
from jax.sharding import PartitionSpec as P

F32 = jnp.float32
BF16 = jnp.bfloat16
LANES = 128
ALIGN = 16
CHUNKS = 4
VMEM = pl.BlockSpec(memory_space=pltpu.VMEM)
SMEM = pl.BlockSpec(memory_space=pltpu.SMEM)
HBM = pl.BlockSpec(memory_space=pltpu.HBM)


def dot(a, b):
    return jnp.dot(a, b, preferred_element_type=F32)


def dot_nt(a, b):
    return lax.dot_general(a, b, (((1,), (1,)), ((), ())), preferred_element_type=F32)


def dot_tn(a, b):
    return lax.dot_general(a, b, (((0,), (0,)), ((), ())), preferred_element_type=F32)


def logistic(v):
    return 0.5 + 0.5 * jnp.tanh(0.5 * v)


def split3(v):
    high = v.astype(BF16)
    rest = v - high.astype(F32)
    mid = rest.astype(BF16)
    low = (rest - mid.astype(F32)).astype(BF16)
    return high, mid, low


def spread(cols, first_head, head_size, rows):
    lane = lax.broadcasted_iota(jnp.int32, (rows, LANES), 1)
    out = jnp.broadcast_to(cols[:, first_head : first_head + 1], (rows, LANES))
    for k in range(1, LANES // head_size):
        nxt = cols[:, first_head + k : first_head + k + 1]
        out = jnp.where(lane >= k * head_size, nxt, out)
    return out


def convolve(raw, bias, taps, cols, first, count):
    start = cols.start // LANES
    stop = cols.stop // LANES
    acc = jnp.concatenate(
        [jnp.broadcast_to(bias[k : k + 1, :], (count, LANES)) for k in range(start, stop)], axis=1
    )
    n = taps.shape[0]
    for k in range(n):
        acc = acc + taps[k : k + 1, cols] * raw[pl.ds(first - (n - 1) + k, count), cols]
    return (acc * logistic(acc)).astype(BF16)


def scan_kernel(heads, take, xbc, cum_o, dt_t, cum_t, weight_o, last_o, head_o, sum_o, raw, carried):
    hist = take(0)
    dtw, dtb, alog = take(1), take(2), take(3)
    length, width = xbc.shape
    inner = carried.shape[1]
    state = (width - inner) // 2
    head_size = inner // heads
    per = LANES // head_size

    v = dot_nt(hist[...], dtw[...]) + dtb[...]
    dt = jnp.maximum(v, 0.0) + jnp.log1p(jnp.exp(-jnp.abs(v)))
    decay = -jnp.exp(alog[...]) * dt
    ri = lax.broadcasted_iota(jnp.int32, (length, length), 0)
    ci = lax.broadcasted_iota(jnp.int32, (length, length), 1)
    tri = jnp.where(ci <= ri, 1.0, 0.0).astype(BF16)
    parts = split3(decay)
    cum = dot(tri, parts[0]) + (dot(tri, parts[1]) + dot(tri, parts[2]))
    cum_o[...] = cum
    dt_t[...] = dt.T
    cum_t[...] = cum.T
    last = cum[length - 1 : length, :]
    weight = jnp.exp(last - cum) * dt
    weight_o[...] = weight[:ALIGN]
    last_o[...] = jnp.broadcast_to(jnp.exp(last), last_o.shape)

    step = 2 * LANES
    cw, cb, w = take(4), take(5), take(6)
    raw[:ALIGN, :] = jnp.zeros((ALIGN, width), F32)
    for start in list(range(inner, width, step)) + list(range(0, inner, step)):
        cols = slice(start, start + step)
        raw[ALIGN:, cols] = dot(hist[...], w[:, cols]).astype(BF16).astype(F32)
        xbc[:, cols] = convolve(raw, cb, cw, cols, ALIGN, length)
    head_o[...] = raw[ALIGN : 2 * ALIGN, :]
    for start in range(0, inner, LANES):
        cols = slice(start, start + LANES)
        x = xbc[:, cols].astype(F32)
        carried[:, cols] = (
            spread(weight, start // LANES * per, head_size, length) * x
        ).astype(BF16)
    b = xbc[ALIGN:, inner : inner + state]
    sum_o[...] = dot_tn(b, carried[ALIGN:, :])


def edge_kernel(heads, take, halo, w, cw, cb, weight, last, head, later, old, xbc, pay, raw):
    width = xbc.shape[1]
    state, inner = later.shape
    head_size = inner // heads
    per = LANES // head_size
    before = jnp.where(lax.axis_index("tm") == 0, 0.0, halo[...].astype(F32)).astype(BF16)
    raw[:ALIGN, :] = dot(before, w[...]).astype(BF16).astype(F32)
    raw[ALIGN:, :] = head[...]
    top = convolve(raw, cb, cw, slice(0, width), ALIGN, ALIGN)
    xbc[:ALIGN, :] = top
    gain = last[...]
    pick = lax.broadcasted_iota(jnp.int32, (ALIGN, LANES), 0)
    b = top[:, inner : inner + state]
    for start in range(0, inner, LANES):
        cols = slice(start, start + LANES)
        h = start // LANES * per
        carried = (spread(weight[...], h, head_size, ALIGN) * top[:, cols].astype(F32)).astype(BF16)
        pay[:state, cols] = (later[:, cols] + dot_tn(b, carried)).astype(BF16)
        g = spread(gain, h, head_size, ALIGN)
        high = g.astype(BF16).astype(F32)
        pay[state:, cols] = jnp.where(
            pick == 0, high, jnp.where(pick == 1, g - high, 0.0)
        ).astype(BF16)


def gain_row(pay, state):
    tail = pay[state:, :].astype(F32)
    return tail[0:1, :] + tail[1:2, :]


def chip_kernel(take, mine, other, out, gain_out):
    state = out.shape[0]
    odd = lax.rem(lax.axis_index("tm"), 2) == 1
    m = mine[:state, :].astype(F32)
    o = other[:state, :].astype(F32)
    gm = gain_row(mine, state)
    go = gain_row(other, state)
    out[...] = jnp.where(odd, o * gm + m, m * go + o).astype(BF16)
    gain_out[...] = jnp.broadcast_to(gm * go, gain_out.shape)


def within_kernel(
    heads, take, d_skip, xbc, cum, dt_t, cum_t, own, across, pre, hot_o, hot_t_o, item_t_o, part
):
    length, inner = part.shape
    slots = hot_o.shape[0]
    state = (xbc.shape[1] - inner) // 2
    head_size = inner // heads
    per = LANES // head_size
    b = xbc[:, inner : inner + state]
    c = xbc[:, inner + state :]
    scores = dot_nt(c, b)
    half = length // 2
    tops = lax.broadcasted_iota(jnp.int32, (half, half), 0)
    lefts = lax.broadcasted_iota(jnp.int32, (half, half), 1)
    low_tri = lefts <= tops
    lane = lax.broadcasted_iota(jnp.int32, (length, LANES), 1)
    for start in range(0, inner, LANES):
        cols = slice(start, start + LANES)
        x = xbc[:, cols]
        out = None
        for k in range(per):
            h = start // LANES * per + k
            row = cum_t[h : h + 1, :]
            col = cum[:, h : h + 1]
            dts = dt_t[h : h + 1, :]

            def block(r, s, masked):
                gap = col[r : r + half] - row[:, s : s + half]
                if masked:
                    gap = jnp.where(low_tri, gap, 0.0)
                d = jnp.exp(gap)
                if masked:
                    d = jnp.where(low_tri, d, 0.0)
                return (d * dts[:, s : s + half] * scores[r : r + half, s : s + half]).astype(BF16)

            upper = dot(block(0, 0, True), x[:half])
            lower = dot(block(half, 0, False), x[:half]) + dot(block(half, half, True), x[half:])
            got = jnp.concatenate([upper, lower], axis=0)
            skip = d_skip[h]
            got = got + skip * x.astype(F32)
            out = got if out is None else jnp.where(lane >= k * head_size, got, out)
        part[:, cols] = out
    step = 2 * LANES
    grow = jnp.exp(cum[...])
    hist, zw = take(0), take(1)
    for start in range(0, inner, step):
        cols = slice(start, start + step)
        z = dot(hist[...], zw[:, cols]).astype(BF16).astype(F32)
        gate = z * logistic(z)
        own[:, cols] = part[:, cols] * gate
        for k in range(0, step, LANES):
            first_head = (start + k) // LANES * per
            across[:, start + k : start + k + LANES] = (
                spread(grow, first_head, head_size, length) * gate[:, k : k + LANES]
            )
    item, first = take(2), take(3)
    for start in range(0, pre.shape[1], step):
        cols = slice(start, start + step)
        pre[:, cols] = dot(item[...], first[:, cols])
    item_t_o[...] = item[...].T
    place = take(4)[...] - lax.axis_index("tm") * length
    hot = jnp.where(lax.broadcasted_iota(jnp.int32, (length, slots), 0) == place, 1.0, 0.0)
    hot_t_o[...] = hot.astype(BF16)
    hot_o[...] = hot.T.astype(BF16)


def rank_kernel(
    take,
    count,
    incoming,
    other,
    xbc,
    own,
    across,
    pre,
    hot,
    hot_t,
    item_t,
    enc_o,
    logit_o,
    gp_s,
    rank_o,
    *rest,
):
    send_o = rest[:CHUNKS]
    gated_s, rank_s, slope_s, hid_s, enc_s, enc_sem = rest[CHUNKS:]
    length, inner = own.shape
    state = incoming.shape[0]
    slots = pre.shape[0]
    tm = lax.axis_index("tm")
    odd = lax.rem(tm, 2) == 1
    arrived = jnp.where(tm < 2, 0.0, incoming[...].astype(F32))
    enter = jnp.where(
        odd, arrived * gain_row(other, state) + other[:state, :].astype(F32), arrived
    )
    entering = enter.astype(BF16)
    c = xbc[:, inner + state :]
    total = jnp.zeros((length, LANES), F32)
    for start in range(0, inner, LANES):
        cols = slice(start, start + LANES)
        read = dot(c, entering[:, cols])
        y = own[:, cols] + across[:, cols] * read
        gated_s[:, cols] = y
        total = total + y * y
    mean = jnp.sum(total, axis=1, keepdims=True) * (1.0 / inner)
    scale = lax.rsqrt(mean + 1e-05)
    gain, ow = take(0), take(1)
    normed = (gated_s[...] * scale * gain[...]).astype(BF16)
    enc = dot(normed, ow[...]).astype(BF16)
    enc_s[...] = enc
    leaving = pltpu.make_async_copy(enc_s, enc_o, enc_sem)
    leaving.start()
    width = enc.shape[1]
    rank_s[...] = dot(hot[...], enc).astype(BF16)
    rank_t = dot(enc.T, hot_t[...]).astype(BF16)

    hidden_width = pre.shape[1]
    step = 2 * LANES
    logit = jnp.zeros((slots, LANES), F32)
    first, second = take(2), take(3)
    weights2 = second[...].astype(F32)
    for start in range(0, hidden_width, step):
        cols = slice(start, start + step)
        v = pre[:, cols] + dot(rank_s[...], first[:, cols])
        sig = logistic(v)
        silu = v * sig
        hid = silu.astype(BF16)
        hid_s[:, cols] = hid
        k = start // LANES
        w2 = jnp.concatenate([weights2[k : k + 1], weights2[k + 1 : k + 2]], axis=1)
        prod = hid.astype(F32) * w2
        for k in range(0, step, LANES):
            logit = logit + prod[:, k : k + LANES]
        slope_s[:, cols] = w2 * (sig + silu * (1.0 - sig))
    ones = jnp.ones((8, LANES), BF16)
    p = split3(logit)
    logit8 = dot_nt(ones, p[0]) + (dot_nt(ones, p[1]) + dot_nt(ones, p[2]))
    slot = lax.broadcasted_iota(jnp.int32, (8, slots), 1)
    live = jnp.where(slot < count[0, 0], 1.0, 0.0)
    logit_o[...] = (live * logit8)[0:1, :]
    value = take(4)
    target = value[...].astype(F32)
    dl = live * (1.0 / (1.0 + jnp.exp(-logit8)) - target)
    d0, d1, d2 = split3(dl)
    which = lax.broadcasted_iota(jnp.int32, (8, slots), 0)
    dl3 = jnp.where(
        which == 0,
        d0.astype(F32),
        jnp.where(which == 1, d1.astype(F32), jnp.where(which == 2, d2.astype(F32), 0.0)),
    ).astype(BF16)
    grad2 = jnp.sum(dot(dl3, hid_s[...]), axis=0, keepdims=True)
    dcol = dot_tn(dl3, jnp.ones((8, LANES), BF16))
    for start in range(0, hidden_width, LANES):
        cols = slice(start, start + LANES)
        gp_s[:, cols] = (dcol * slope_s[:, cols]).astype(BF16)
    rows = width
    pick = lax.broadcasted_iota(jnp.int32, (8, hidden_width), 0)
    extra = jnp.where(pick == 0, grad2, 0.0).astype(BF16)
    away = jnp.where(odd, rank_t, item_t[...])
    rank_o[...] = rank_t
    size = rows // CHUNKS
    for k in range(CHUNKS):
        part = away[k * size : (k + 1) * size]
        send_o[k][:size, :] = dot(part, gp_s[...]).astype(BF16)
    send_o[CHUNKS - 1][size:, :] = extra
    leaving.wait()


def home_kernel(take, rank_t, item_t, slope, last_sent, *keep_o):
    size = rank_t.shape[0] // CHUNKS
    odd = lax.rem(lax.axis_index("tm"), 2) == 1
    for k in range(CHUNKS):
        part = slice(k * size, (k + 1) * size)
        home = jnp.where(odd, item_t[part, :], rank_t[part, :])
        keep_o[k][:size, :] = dot(home, slope[...]).astype(BF16)
    keep_o[CHUNKS - 1][size:, :] = last_sent[size:, :]


def chunk_shapes(rows, columns):
    size = rows // CHUNKS
    last = size + 8
    return tuple(shape((last if k == CHUNKS - 1 else size, columns), BF16) for k in range(CHUNKS))


def loading(kernel, n_loaded, n_given, n_out, windows, kept):
    def wrapped(*refs):
        sources = refs[:n_loaded]
        given = refs[n_loaded : n_loaded + n_given + n_out]
        first_kept = n_loaded + n_given + n_out
        results = list(refs[first_kept : first_kept + len(kept)])
        rest = list(refs[first_kept + len(kept) :])
        places = [results.pop(0) if i in kept else rest.pop(0) for i in range(n_loaded)]
        sems, scratch = rest[0], rest[1:]
        copies = []
        for i, source in enumerate(sources):
            window = windows.get(i)
            view = source if window is None else source.at[pl.ds(*window)]
            copies.append(pltpu.make_async_copy(view, places[i], sems.at[i]))
            copies[i].start()

        def take(i):
            copies[i].wait()
            return places[i]

        kernel(take, *given, *scratch)

    return wrapped


def call(
    kernel,
    loaded,
    given,
    out_shape,
    scratch,
    flops,
    moved,
    mib,
    windows=None,
    smem=0,
    kept=(),
    aliases=None,
    outside=(),
):
    windows = windows or {}
    places = []
    for i, value in enumerate(loaded):
        dims = value.shape if i not in windows else (windows[i][1],) + value.shape[1:]
        if i not in kept:
            places.append(pltpu.VMEM(dims, value.dtype))
    outs = tuple(out_shape) + tuple(shape(loaded[i].shape, loaded[i].dtype) for i in kept)
    return pl.pallas_call(
        loading(kernel, len(loaded), len(given), len(out_shape), windows, kept),
        out_shape=outs,
        in_specs=[HBM] * len(loaded) + [SMEM] * smem + [VMEM] * (len(given) - smem),
        out_specs=[HBM if i in outside else VMEM for i in range(len(outs))],
        scratch_shapes=places + [pltpu.SemaphoreType.DMA((max(len(loaded), 1),))] + scratch,
        compiler_params=pltpu.CompilerParams(vmem_limit_bytes=mib * 1024 * 1024),
        cost_estimate=pl.CostEstimate(flops=flops, bytes_accessed=moved, transcendentals=0),
        input_output_aliases=aliases or {},
    )(*[pltpu.with_memory_space_constraint(value, pltpu.HBM) for value in loaded], *given)


def shape(dims, dtype):
    return jax.ShapeDtypeStruct(dims, dtype)


def bits_of(n):
    return max(n.bit_length() - 1, 0)


def body(
    history,
    z_weight,
    xbc_weight,
    dt_weight,
    dt_bias,
    a_log,
    conv_weight,
    conv_bias,
    d_skip,
    norm_gain,
    out_weight,
    label_pos,
    label_count,
    label_value,
    item_feat,
    first_weight,
    second_weight,
):
    hist = history[0]
    item = item_feat[0]
    length, width = hist.shape
    inner = z_weight.shape[1]
    heads = a_log.shape[0]
    channels = xbc_weight.shape[1]
    state = (channels - inner) // 2
    slots = label_pos.shape[1]
    hidden = first_weight.shape[1]
    n_tm = lax.axis_size("tm")
    n_user = lax.axis_size("user")
    chips = n_tm // 2
    tm = lax.axis_index("tm")
    user = lax.axis_index("user")

    halo = lax.ppermute(hist[length - ALIGN :], "tm", [(i, (i + 1) % n_tm) for i in range(n_tm)])
    early, cum, dt_t, cum_t, weight, last, head, later, taps, bias, w = call(
        functools.partial(scan_kernel, heads),
        (
            hist,
            dt_weight.T,
            dt_bias.reshape(1, heads),
            a_log.reshape(1, heads),
            conv_weight,
            conv_bias.reshape(channels // LANES, LANES),
            xbc_weight,
        ),
        (),
        (
            shape((length, channels), BF16),
            shape((length, heads), F32),
            shape((heads, length), F32),
            shape((heads, length), F32),
            shape((ALIGN, heads), F32),
            shape((ALIGN, heads), F32),
            shape((ALIGN, channels), F32),
            shape((state, inner), F32),
        ),
        [pltpu.VMEM((length + ALIGN, channels), F32), pltpu.VMEM((length, inner), BF16)],
        2 * length * width * channels,
        4 * width * channels,
        16,
        kept=(4, 5, 6),
    )
    xbc, pay = call(
        functools.partial(edge_kernel, heads),
        (),
        (halo, w, taps, bias, weight, last, head, later, early),
        (shape((length, channels), BF16), shape((state + ALIGN, inner), BF16)),
        [pltpu.VMEM((2 * ALIGN, channels), F32)],
        2 * ALIGN * width * channels,
        2 * width * channels,
        10,
        aliases={8: 0},
    )
    other = lax.ppermute(pay, "tm", [(i, i ^ 1) for i in range(n_tm)])
    chip_state, chip_gain = call(
        chip_kernel,
        (),
        (pay, other),
        (shape((state, inner), BF16), shape((8, inner), F32)),
        [],
        state * inner,
        6 * state * inner,
        6,
    )
    onward = [(i, (i + 2) % n_tm) for i in range(n_tm)]
    incoming = lax.ppermute(chip_state, "tm", onward)
    for _ in range(chips - 2):
        incoming = jnp.where(tm < 2, 0.0, incoming.astype(F32))
        passed = chip_gain[0:1] * incoming + chip_state.astype(F32)
        incoming = lax.ppermute(passed.astype(BF16), "tm", onward)
    own, across, pre, hot, hot_t, item_t = call(
        functools.partial(within_kernel, heads),
        (hist, z_weight, item, first_weight, label_pos),
        (d_skip, xbc, cum, dt_t, cum_t),
        (
            shape((length, inner), F32),
            shape((length, inner), F32),
            shape((slots, hidden), F32),
            shape((slots, length), BF16),
            shape((length, slots), BF16),
            shape((width, slots), BF16),
        ),
        [pltpu.VMEM((length, inner), F32)],
        2 * length * width * inner + 2 * slots * width * hidden + 4 * length * length * inner,
        16 * length * inner * 4,
        24,
        {3: (width, width)},
        1,
    )
    enc, row_logit, slope, rank_t, *send = call(
        rank_kernel,
        (
            norm_gain.reshape(1, inner),
            out_weight,
            first_weight,
            second_weight.reshape(hidden // LANES, LANES),
            label_value,
        ),
        (label_count, incoming, other, xbc, own, across, pre, hot, hot_t, item_t),
        (
            shape((length, width), BF16),
            shape((1, slots), F32),
            shape((slots, hidden), BF16),
            shape((width, slots), BF16),
        )
        + chunk_shapes(width, hidden),
        [
            pltpu.VMEM((length, inner), F32),
            pltpu.VMEM((slots, width), BF16),
            pltpu.VMEM((slots, hidden), F32),
            pltpu.VMEM((slots, hidden), BF16),
            pltpu.VMEM((length, width), BF16),
            pltpu.SemaphoreType.DMA,
        ],
        4 * slots * width * hidden,
        8 * slots * hidden,
        24,
        {2: (0, width)},
        1,
        outside=(0,),
    )
    keep = call(
        home_kernel,
        (),
        (rank_t, item_t, slope, send[-1]),
        chunk_shapes(width, hidden),
        [],
        2 * slots * width * hidden,
        4 * slots * hidden,
        8,
    )
    grad_first, grad_second = total_sum(send, keep, n_user, n_tm, user, tm)
    return (enc[None], row_logit, grad_first, grad_second)


def total_sum(send, keep, n_user, n_tm, user, tm):
    rows = sum(part.shape[0] for part in keep) - 8
    odd = tm % 2
    axes = ("user", "tm")
    every = [(u, t) for u in range(n_user) for t in range(n_tm)]
    chunks = CHUNKS

    def swap(value, partner):
        pairs = [(u * n_tm + t, partner(u, t)) for u, t in every]
        return lax.ppermute(value, axes, pairs)

    def across(u, t):
        return u * n_tm + (t ^ 1)

    chip_bits = [("tm", k) for k in range(bits_of(n_tm // 2))]
    user_bits = [("user", k) for k in range(bits_of(n_user))]
    order_even = chip_bits + user_bits
    order_odd = user_bits + chip_bits

    def partner_of(level):
        def partner(u, t):
            axis, k = (order_even if t % 2 == 0 else order_odd)[level]
            if axis == "tm":
                return u * n_tm + (t ^ (2 << k))
            return (u ^ (1 << k)) * n_tm + t

        return partner

    def bit_of(level):
        def one(entry):
            axis, k = entry
            return (tm >> (k + 1)) & 1 if axis == "tm" else (user >> k) & 1

        return jnp.where(odd == 0, one(order_even[level]), one(order_odd[level])) == 1

    levels = len(order_even)
    bits = [bit_of(level) for level in range(levels)]
    size = rows // chunks
    state = []
    for leave, stay in zip(send, keep):
        got = swap(leave, across)
        extra = None
        if stay.shape[0] > size:
            extra = (stay[size:].astype(F32) + got[size:].astype(F32)).astype(BF16)
        state.append((stay[:size], got[:size], extra))
    for level in range(levels - 1):
        after = []
        for a, b, extra in state:
            size = a.shape[0] // 2
            low = a[:size].astype(F32) + b[:size].astype(F32)
            high = a[size:].astype(F32) + b[size:].astype(F32)
            leave = jnp.where(bits[level], low, high).astype(BF16)
            stay = jnp.where(bits[level], high, low).astype(BF16)
            if extra is not None:
                leave = jnp.concatenate([leave, extra], axis=0)
            got = swap(leave, partner_of(level))
            if extra is not None:
                extra = (extra.astype(F32) + got[size:].astype(F32)).astype(BF16)
            after.append((stay, got[:size], extra))
        state = after
    wholes = []
    for a, b, extra in state:
        size = a.shape[0]
        whole = (a.astype(F32) + b.astype(F32)).astype(BF16)
        if levels:
            leave = whole if extra is None else jnp.concatenate([whole, extra], axis=0)
            got = swap(leave, partner_of(levels - 1))
            whole = (whole.astype(F32) + got[:size].astype(F32)).astype(BF16)
            if extra is not None:
                extra = (extra.astype(F32) + got[size:].astype(F32)).astype(BF16)
        wholes.append((whole, extra))
    for level in reversed(range(levels - 1)):
        after = []
        for whole, extra in wholes:
            got = swap(whole, partner_of(level))
            first = jnp.where(bits[level], got, whole)
            second = jnp.where(bits[level], whole, got)
            after.append((jnp.concatenate([first, second], axis=0), extra))
        wholes = after
    arrived = []
    for whole, extra in wholes:
        arrived.append(
            swap(whole if extra is None else jnp.concatenate([whole, extra], axis=0), across)
        )
    own_extra = wholes[-1][1]
    mine = [whole for whole, _ in wholes]
    total = (2 * rows,) + mine[0].shape[1:]
    last = chunks - 1
    own = [(w, 0, k) for k, w in enumerate(mine)]
    other = [(w, 1, k) for k, w in enumerate(arrived)]
    grad_first, grad_second = written(None, own + other, rows, total, own_extra)
    return grad_first, grad_second.reshape(total[1:])


def written(so_far, blocks, half_rows, total, own_extra=None):
    size = blocks[0][0].shape[0]
    size -= size % LANES
    given = [value for value, _, _ in blocks]
    n = len(given)
    wide = given[-1].shape[0] > size
    aliased = so_far is not None

    def kernel(*refs):
        refs = list(refs)
        if aliased:
            refs.pop(0)
        values = [refs.pop(0) for _ in range(n)]
        mine = refs.pop(0) if wide else None
        out = refs.pop(0)
        second = refs.pop(0) if wide else None
        buf, sems = refs
        odd = lax.rem(lax.axis_index("tm"), 2)
        copies = []
        for i, (_, other, k) in enumerate(blocks):
            buf[i] = values[i][:size, :].astype(F32)
            side = 1 - odd if other else odd
            at = pl.multiple_of(side * half_rows + k * size, 8)
            copies.append(pltpu.make_async_copy(buf.at[i], out.at[pl.ds(at, size)], sems.at[i]))
            copies[i].start()
        if wide:
            own = mine[...].astype(F32)[0:1]
            got = values[-1][size:, :].astype(F32)[0:1]
            second[...] = jnp.where(odd == 1, got, own)
        for copy in copies:
            copy.wait()

    outs = [jax.ShapeDtypeStruct(total, F32)]
    if wide:
        outs.append(jax.ShapeDtypeStruct((1, total[1]), F32))
        given = given + [own_extra]
    operands = given
    if aliased:
        operands = [pltpu.with_memory_space_constraint(so_far, pltpu.HBM)] + given
    result = pl.pallas_call(
        kernel,
        out_shape=tuple(outs),
        in_specs=[HBM] * aliased + [VMEM] * len(given),
        out_specs=tuple([HBM] + [VMEM] * wide),
        scratch_shapes=[pltpu.VMEM((n, size, total[1]), F32), pltpu.SemaphoreType.DMA((n,))],
        input_output_aliases={0: 0} if aliased else {},
        compiler_params=pltpu.CompilerParams(vmem_limit_bytes=12 * 1024 * 1024),
        cost_estimate=pl.CostEstimate(
            flops=n * size * total[1], bytes_accessed=6 * n * size * total[1], transcendentals=0
        ),
    )(*operands)
    return result if wide else result[0]


def solution(mesh):
    in_specs = (
        P(("grp", "user"), "tm", None),
        P(),
        P(),
        P(),
        P(),
        P(),
        P(),
        P(),
        P(),
        P(),
        P(),
        P(("grp", "user"), "tm"),
        P(("grp", "user"), "tm"),
        P(("grp", "user"), "tm"),
        P(("grp", "user"), "tm", None),
        P(),
        P(),
    )
    out_specs = (P(("grp", "user"), "tm", None), P(("grp", "user"), "tm"), P("grp", None), P("grp"))
    return jax.shard_map(body, mesh=mesh, in_specs=in_specs, out_specs=out_specs, check_vma=False)
```

```python
import functools

import jax
import jax.numpy as jnp
from jax import lax
from jax.experimental import pallas as pl
from jax.experimental.pallas import tpu as pltpu
from jax.sharding import PartitionSpec as P


F32 = jnp.float32
BF16 = jnp.bfloat16
LANES = 128
ALIGN = 16
CHUNKS = 4
VMEM = pl.BlockSpec(memory_space=pltpu.VMEM)
SMEM = pl.BlockSpec(memory_space=pltpu.SMEM)
HBM = pl.BlockSpec(memory_space=pltpu.HBM)


def dot(a, b):
    return jnp.dot(a, b, preferred_element_type=F32)


def dot_nt(a, b):
    return lax.dot_general(a, b, (((1,), (1,)), ((), ())), preferred_element_type=F32)


def dot_tn(a, b):
    return lax.dot_general(a, b, (((0,), (0,)), ((), ())), preferred_element_type=F32)


def logistic(v):
    return 0.5 + 0.5 * jnp.tanh(0.5 * v)


def split3(v):
    high = v.astype(BF16)
    rest = v - high.astype(F32)
    mid = rest.astype(BF16)
    low = (rest - mid.astype(F32)).astype(BF16)
    return high, mid, low


def spread(cols, first_head, head_size, rows):
    lane = lax.broadcasted_iota(jnp.int32, (rows, LANES), 1)
    out = jnp.broadcast_to(cols[:, first_head : first_head + 1], (rows, LANES))
    for k in range(1, LANES // head_size):
        nxt = cols[:, first_head + k : first_head + k + 1]
        out = jnp.where(lane >= k * head_size, nxt, out)
    return out


def convolve(raw, bias, taps, cols, first, count):
    start = cols.start // LANES
    stop = cols.stop // LANES
    acc = jnp.concatenate(
        [jnp.broadcast_to(bias[k : k + 1, :], (count, LANES)) for k in range(start, stop)], axis=1
    )
    n = taps.shape[0]
    for k in range(n):
        acc = acc + taps[k : k + 1, cols] * raw[pl.ds(first - (n - 1) + k, count), cols]
    return (acc * logistic(acc)).astype(BF16)


def scan_kernel(heads, take, xbc, cum_o, dt_t, cum_t, weight_o, last_o, head_o, sum_o, raw, carried):
    hist = take(0)
    dtw, dtb, alog = take(1), take(2), take(3)
    length, width = xbc.shape
    inner = carried.shape[1]
    state = (width - inner) // 2
    head_size = inner // heads
    per = LANES // head_size

    v = dot_nt(hist[...], dtw[...]) + dtb[...]
    dt = jnp.maximum(v, 0.0) + jnp.log1p(jnp.exp(-jnp.abs(v)))
    decay = -jnp.exp(alog[...]) * dt
    ri = lax.broadcasted_iota(jnp.int32, (length, length), 0)
    ci = lax.broadcasted_iota(jnp.int32, (length, length), 1)
    tri = jnp.where(ci <= ri, 1.0, 0.0).astype(BF16)
    parts = split3(decay)
    cum = dot(tri, parts[0]) + (dot(tri, parts[1]) + dot(tri, parts[2]))
    cum_o[...] = cum
    dt_t[...] = dt.T
    cum_t[...] = cum.T
    last = cum[length - 1 : length, :]
    weight = jnp.exp(last - cum) * dt
    weight_o[...] = weight[:ALIGN]
    last_o[...] = jnp.broadcast_to(jnp.exp(last), last_o.shape)

    step = 2 * LANES
    cw, cb, w = take(4), take(5), take(6)
    raw[:ALIGN, :] = jnp.zeros((ALIGN, width), F32)
    for start in list(range(inner, width, step)) + list(range(0, inner, step)):
        cols = slice(start, start + step)
        raw[ALIGN:, cols] = dot(hist[...], w[:, cols]).astype(BF16).astype(F32)
        xbc[:, cols] = convolve(raw, cb, cw, cols, ALIGN, length)
    head_o[...] = raw[ALIGN : 2 * ALIGN, :]
    for start in range(0, inner, LANES):
        cols = slice(start, start + LANES)
        x = xbc[:, cols].astype(F32)
        carried[:, cols] = (
            spread(weight, start // LANES * per, head_size, length) * x
        ).astype(BF16)
    b = xbc[ALIGN:, inner : inner + state]
    sum_o[...] = dot_tn(b, carried[ALIGN:, :])


def edge_kernel(heads, take, halo, w, cw, cb, weight, last, head, later, old, xbc, pay, raw):
    width = xbc.shape[1]
    state, inner = later.shape
    head_size = inner // heads
    per = LANES // head_size
    before = jnp.where(lax.axis_index("tm") == 0, 0.0, halo[...].astype(F32)).astype(BF16)
    raw[:ALIGN, :] = dot(before, w[...]).astype(BF16).astype(F32)
    raw[ALIGN:, :] = head[...]
    top = convolve(raw, cb, cw, slice(0, width), ALIGN, ALIGN)
    xbc[:ALIGN, :] = top
    gain = last[...]
    pick = lax.broadcasted_iota(jnp.int32, (ALIGN, LANES), 0)
    b = top[:, inner : inner + state]
    for start in range(0, inner, LANES):
        cols = slice(start, start + LANES)
        h = start // LANES * per
        carried = (spread(weight[...], h, head_size, ALIGN) * top[:, cols].astype(F32)).astype(BF16)
        pay[:state, cols] = (later[:, cols] + dot_tn(b, carried)).astype(BF16)
        g = spread(gain, h, head_size, ALIGN)
        high = g.astype(BF16).astype(F32)
        pay[state:, cols] = jnp.where(
            pick == 0, high, jnp.where(pick == 1, g - high, 0.0)
        ).astype(BF16)


def gain_row(pay, state):
    tail = pay[state:, :].astype(F32)
    return tail[0:1, :] + tail[1:2, :]


def chip_kernel(take, mine, other, out, gain_out):
    state, half = out.shape
    odd = lax.rem(lax.axis_index("tm"), 2) == 1

    def part(ref, rows):
        return jnp.where(odd, ref[rows, half:].astype(F32), ref[rows, :half].astype(F32))

    def gain_of(ref):
        tail = part(ref, slice(state, state + ALIGN))
        return tail[0:1, :] + tail[1:2, :]

    m = part(mine, slice(0, state))
    o = part(other, slice(0, state))
    gm = gain_of(mine)
    go = gain_of(other)
    out[...] = jnp.where(odd, o * gm + m, m * go + o).astype(BF16)
    gain_out[...] = jnp.broadcast_to(gm * go, gain_out.shape)


def within_kernel(
    heads, take, d_skip, xbc, cum, dt_t, cum_t, own, across, pre, hot_o, hot_t_o, item_t_o, part
):
    length, inner = part.shape
    slots = hot_o.shape[0]
    state = (xbc.shape[1] - inner) // 2
    head_size = inner // heads
    per = LANES // head_size
    b = xbc[:, inner : inner + state]
    c = xbc[:, inner + state :]
    scores = dot_nt(c, b)
    half = length // 2
    tops = lax.broadcasted_iota(jnp.int32, (half, half), 0)
    lefts = lax.broadcasted_iota(jnp.int32, (half, half), 1)
    low_tri = lefts <= tops
    lane = lax.broadcasted_iota(jnp.int32, (length, LANES), 1)
    for start in range(0, inner, LANES):
        cols = slice(start, start + LANES)
        x = xbc[:, cols]
        out = None
        for k in range(per):
            h = start // LANES * per + k
            row = cum_t[h : h + 1, :]
            col = cum[:, h : h + 1]
            dts = dt_t[h : h + 1, :]

            def block(r, s, masked):
                gap = col[r : r + half] - row[:, s : s + half]
                if masked:
                    gap = jnp.where(low_tri, gap, 0.0)
                d = jnp.exp(gap)
                if masked:
                    d = jnp.where(low_tri, d, 0.0)
                return (d * dts[:, s : s + half] * scores[r : r + half, s : s + half]).astype(BF16)

            upper = dot(block(0, 0, True), x[:half])
            lower = dot(block(half, 0, False), x[:half]) + dot(block(half, half, True), x[half:])
            got = jnp.concatenate([upper, lower], axis=0)
            skip = d_skip[h]
            got = got + skip * x.astype(F32)
            out = got if out is None else jnp.where(lane >= k * head_size, got, out)
        part[:, cols] = out
    step = 2 * LANES
    grow = jnp.exp(cum[...])
    hist, zw = take(0), take(1)
    for start in range(0, inner, step):
        cols = slice(start, start + step)
        z = dot(hist[...], zw[:, cols]).astype(BF16).astype(F32)
        gate = z * logistic(z)
        own[:, cols] = part[:, cols] * gate
        for k in range(0, step, LANES):
            first_head = (start + k) // LANES * per
            across[:, start + k : start + k + LANES] = (
                spread(grow, first_head, head_size, length) * gate[:, k : k + LANES]
            )
    item, first = take(2), take(3)
    for start in range(0, pre.shape[1], step):
        cols = slice(start, start + step)
        pre[:, cols] = dot(item[...], first[:, cols])
    item_t_o[...] = item[...].T
    place = take(4)[...] - lax.axis_index("tm") * length
    hot = jnp.where(lax.broadcasted_iota(jnp.int32, (length, slots), 0) == place, 1.0, 0.0)
    hot_t_o[...] = hot.astype(BF16)
    hot_o[...] = hot.T.astype(BF16)


def rank_kernel(
    take,
    count,
    incoming,
    incoming_other,
    other,
    xbc,
    own,
    across,
    pre,
    hot,
    hot_t,
    item_t,
    enc_o,
    logit_o,
    gp_s,
    rank_o,
    *rest,
):
    send_o = rest[:CHUNKS]
    gated_s, rank_s, slope_s, hid_s, enc_s, enc_sem = rest[CHUNKS:]
    length, inner = own.shape
    state = incoming.shape[0]
    slots = pre.shape[0]
    tm = lax.axis_index("tm")
    odd = lax.rem(tm, 2) == 1
    half_a, half_b = incoming[...].astype(F32), incoming_other[...].astype(F32)
    arrived = jnp.concatenate(
        [jnp.where(odd, half_b, half_a), jnp.where(odd, half_a, half_b)], axis=1
    )
    arrived = jnp.where(tm < 2, 0.0, arrived)
    enter = jnp.where(
        odd, arrived * gain_row(other, state) + other[:state, :].astype(F32), arrived
    )
    entering = enter.astype(BF16)
    c = xbc[:, inner + state :]
    total = jnp.zeros((length, LANES), F32)
    for start in range(0, inner, LANES):
        cols = slice(start, start + LANES)
        read = dot(c, entering[:, cols])
        y = own[:, cols] + across[:, cols] * read
        gated_s[:, cols] = y
        total = total + y * y
    mean = jnp.sum(total, axis=1, keepdims=True) * (1.0 / inner)
    scale = lax.rsqrt(mean + 1e-05)
    gain, ow = take(0), take(1)
    normed = (gated_s[...] * scale * gain[...]).astype(BF16)
    enc = dot(normed, ow[...]).astype(BF16)
    enc_s[...] = enc
    leaving = pltpu.make_async_copy(enc_s, enc_o, enc_sem)
    leaving.start()
    width = enc.shape[1]
    rank_s[...] = dot(hot[...], enc).astype(BF16)
    rank_t = dot(enc.T, hot_t[...]).astype(BF16)

    hidden_width = pre.shape[1]
    step = 2 * LANES
    logit = jnp.zeros((slots, LANES), F32)
    first, second = take(2), take(3)
    weights2 = second[...].astype(F32)
    for start in range(0, hidden_width, step):
        cols = slice(start, start + step)
        v = pre[:, cols] + dot(rank_s[...], first[:, cols])
        sig = logistic(v)
        silu = v * sig
        hid = silu.astype(BF16)
        hid_s[:, cols] = hid
        k = start // LANES
        w2 = jnp.concatenate([weights2[k : k + 1], weights2[k + 1 : k + 2]], axis=1)
        prod = hid.astype(F32) * w2
        for k in range(0, step, LANES):
            logit = logit + prod[:, k : k + LANES]
        slope_s[:, cols] = w2 * (sig + silu * (1.0 - sig))
    ones = jnp.ones((8, LANES), BF16)
    p = split3(logit)
    logit8 = dot_nt(ones, p[0]) + (dot_nt(ones, p[1]) + dot_nt(ones, p[2]))
    slot = lax.broadcasted_iota(jnp.int32, (8, slots), 1)
    live = jnp.where(slot < count[0, 0], 1.0, 0.0)
    logit_o[...] = (live * logit8)[0:1, :]
    value = take(4)
    target = value[...].astype(F32)
    dl = live * (1.0 / (1.0 + jnp.exp(-logit8)) - target)
    d0, d1, d2 = split3(dl)
    which = lax.broadcasted_iota(jnp.int32, (8, slots), 0)
    dl3 = jnp.where(
        which == 0,
        d0.astype(F32),
        jnp.where(which == 1, d1.astype(F32), jnp.where(which == 2, d2.astype(F32), 0.0)),
    ).astype(BF16)
    grad2 = jnp.sum(dot(dl3, hid_s[...]), axis=0, keepdims=True)
    dcol = dot_tn(dl3, jnp.ones((8, LANES), BF16))
    for start in range(0, hidden_width, LANES):
        cols = slice(start, start + LANES)
        gp_s[:, cols] = (dcol * slope_s[:, cols]).astype(BF16)
    rows = width
    pick = lax.broadcasted_iota(jnp.int32, (8, hidden_width), 0)
    extra = jnp.where(pick == 0, grad2, 0.0).astype(BF16)
    away = jnp.where(odd, rank_t, item_t[...])
    rank_o[...] = rank_t
    size = rows // CHUNKS
    for k in range(CHUNKS):
        part = away[k * size : (k + 1) * size]
        send_o[k][:size, :] = dot(part, gp_s[...]).astype(BF16)
    send_o[CHUNKS - 1][size:, :] = extra
    leaving.wait()


def home_kernel(take, rank_t, item_t, slope, last_sent, *keep_o):
    size = rank_t.shape[0] // CHUNKS
    odd = lax.rem(lax.axis_index("tm"), 2) == 1
    for k in range(CHUNKS):
        part = slice(k * size, (k + 1) * size)
        home = jnp.where(odd, item_t[part, :], rank_t[part, :])
        keep_o[k][:size, :] = dot(home, slope[...]).astype(BF16)
    keep_o[CHUNKS - 1][size:, :] = last_sent[size:, :]


def chunk_shapes(rows, columns):
    size = rows // CHUNKS
    last = size + 8
    return tuple(shape((last if k == CHUNKS - 1 else size, columns), BF16) for k in range(CHUNKS))


def loading(kernel, n_loaded, n_given, n_out, windows, kept):
    def wrapped(*refs):
        sources = refs[:n_loaded]
        given = refs[n_loaded : n_loaded + n_given + n_out]
        first_kept = n_loaded + n_given + n_out
        results = list(refs[first_kept : first_kept + len(kept)])
        rest = list(refs[first_kept + len(kept) :])
        places = [results.pop(0) if i in kept else rest.pop(0) for i in range(n_loaded)]
        sems, scratch = rest[0], rest[1:]
        copies = []
        for i, source in enumerate(sources):
            window = windows.get(i)
            view = source if window is None else source.at[pl.ds(*window)]
            copies.append(pltpu.make_async_copy(view, places[i], sems.at[i]))
            copies[i].start()

        def take(i):
            copies[i].wait()
            return places[i]

        kernel(take, *given, *scratch)

    return wrapped


def call(
    kernel,
    loaded,
    given,
    out_shape,
    scratch,
    flops,
    moved,
    mib,
    windows=None,
    smem=0,
    kept=(),
    aliases=None,
    outside=(),
):
    windows = windows or {}
    places = []
    for i, value in enumerate(loaded):
        dims = value.shape if i not in windows else (windows[i][1],) + value.shape[1:]
        if i not in kept:
            places.append(pltpu.VMEM(dims, value.dtype))
    outs = tuple(out_shape) + tuple(shape(loaded[i].shape, loaded[i].dtype) for i in kept)
    return pl.pallas_call(
        loading(kernel, len(loaded), len(given), len(out_shape), windows, kept),
        out_shape=outs,
        in_specs=[HBM] * len(loaded) + [SMEM] * smem + [VMEM] * (len(given) - smem),
        out_specs=[HBM if i in outside else VMEM for i in range(len(outs))],
        scratch_shapes=places + [pltpu.SemaphoreType.DMA((max(len(loaded), 1),))] + scratch,
        compiler_params=pltpu.CompilerParams(vmem_limit_bytes=mib * 1024 * 1024),
        cost_estimate=pl.CostEstimate(flops=flops, bytes_accessed=moved, transcendentals=0),
        input_output_aliases=aliases or {},
    )(*[pltpu.with_memory_space_constraint(value, pltpu.HBM) for value in loaded], *given)


def shape(dims, dtype):
    return jax.ShapeDtypeStruct(dims, dtype)


def bits_of(n):
    return max(n.bit_length() - 1, 0)


def body(
    history,
    z_weight,
    xbc_weight,
    dt_weight,
    dt_bias,
    a_log,
    conv_weight,
    conv_bias,
    d_skip,
    norm_gain,
    out_weight,
    label_pos,
    label_count,
    label_value,
    item_feat,
    first_weight,
    second_weight,
):
    hist = history[0]
    item = item_feat[0]
    length, width = hist.shape
    inner = z_weight.shape[1]
    heads = a_log.shape[0]
    channels = xbc_weight.shape[1]
    state = (channels - inner) // 2
    slots = label_pos.shape[1]
    hidden = first_weight.shape[1]
    n_tm = lax.axis_size("tm")
    n_user = lax.axis_size("user")
    chips = n_tm // 2
    tm = lax.axis_index("tm")
    user = lax.axis_index("user")

    halo = lax.ppermute(hist[length - ALIGN :], "tm", [(i, (i + 1) % n_tm) for i in range(n_tm)])
    early, cum, dt_t, cum_t, weight, last, head, later, taps, bias, w = call(
        functools.partial(scan_kernel, heads),
        (
            hist,
            dt_weight.T,
            dt_bias.reshape(1, heads),
            a_log.reshape(1, heads),
            conv_weight,
            conv_bias.reshape(channels // LANES, LANES),
            xbc_weight,
        ),
        (),
        (
            shape((length, channels), BF16),
            shape((length, heads), F32),
            shape((heads, length), F32),
            shape((heads, length), F32),
            shape((ALIGN, heads), F32),
            shape((ALIGN, heads), F32),
            shape((ALIGN, channels), F32),
            shape((state, inner), F32),
        ),
        [pltpu.VMEM((length + ALIGN, channels), F32), pltpu.VMEM((length, inner), BF16)],
        2 * length * width * channels,
        4 * width * channels,
        16,
        kept=(4, 5, 6),
    )
    xbc, pay = call(
        functools.partial(edge_kernel, heads),
        (),
        (halo, w, taps, bias, weight, last, head, later, early),
        (shape((length, channels), BF16), shape((state + ALIGN, inner), BF16)),
        [pltpu.VMEM((2 * ALIGN, channels), F32)],
        2 * ALIGN * width * channels,
        2 * width * channels,
        10,
        aliases={8: 0},
    )
    other = lax.ppermute(pay, "tm", [(i, i ^ 1) for i in range(n_tm)])
    chip_state, chip_gain = call(
        chip_kernel,
        (),
        (pay, other),
        (shape((state, inner // 2), BF16), shape((8, inner // 2), F32)),
        [],
        state * inner,
        6 * state * inner,
        6,
    )
    onward = [(i, (i + 2) % n_tm) for i in range(n_tm)]
    incoming = lax.ppermute(chip_state, "tm", onward)
    for _ in range(chips - 2):
        incoming = jnp.where(tm < 2, 0.0, incoming.astype(F32))
        passed = chip_gain[0:1] * incoming + chip_state.astype(F32)
        incoming = lax.ppermute(passed.astype(BF16), "tm", onward)
    incoming_other = lax.ppermute(incoming, "tm", [(i, i ^ 1) for i in range(n_tm)])
    own, across, pre, hot, hot_t, item_t = call(
        functools.partial(within_kernel, heads),
        (hist, z_weight, item, first_weight, label_pos),
        (d_skip, xbc, cum, dt_t, cum_t),
        (
            shape((length, inner), F32),
            shape((length, inner), F32),
            shape((slots, hidden), F32),
            shape((slots, length), BF16),
            shape((length, slots), BF16),
            shape((width, slots), BF16),
        ),
        [pltpu.VMEM((length, inner), F32)],
        2 * length * width * inner + 2 * slots * width * hidden + 4 * length * length * inner,
        16 * length * inner * 4,
        24,
        {3: (width, width)},
        1,
    )
    enc, row_logit, slope, rank_t, *send = call(
        rank_kernel,
        (
            norm_gain.reshape(1, inner),
            out_weight,
            first_weight,
            second_weight.reshape(hidden // LANES, LANES),
            label_value,
        ),
        (label_count, incoming, incoming_other, other, xbc, own, across, pre, hot, hot_t, item_t),
        (
            shape((length, width), BF16),
            shape((1, slots), F32),
            shape((slots, hidden), BF16),
            shape((width, slots), BF16),
        )
        + chunk_shapes(width, hidden),
        [
            pltpu.VMEM((length, inner), F32),
            pltpu.VMEM((slots, width), BF16),
            pltpu.VMEM((slots, hidden), F32),
            pltpu.VMEM((slots, hidden), BF16),
            pltpu.VMEM((length, width), BF16),
            pltpu.SemaphoreType.DMA,
        ],
        4 * slots * width * hidden,
        8 * slots * hidden,
        24,
        {2: (0, width)},
        1,
        outside=(0,),
    )
    keep = call(
        home_kernel,
        (),
        (rank_t, item_t, slope, send[-1]),
        chunk_shapes(width, hidden),
        [],
        2 * slots * width * hidden,
        4 * slots * hidden,
        8,
    )
    grad_first, grad_second = total_sum(send, keep, n_user, n_tm, user, tm)
    return (enc[None], row_logit, grad_first, grad_second)


def total_sum(send, keep, n_user, n_tm, user, tm):
    rows = sum(part.shape[0] for part in keep) - 8
    odd = tm % 2
    axes = ("user", "tm")
    every = [(u, t) for u in range(n_user) for t in range(n_tm)]
    chunks = CHUNKS

    def swap(value, partner):
        pairs = [(u * n_tm + t, partner(u, t)) for u, t in every]
        return lax.ppermute(value, axes, pairs)

    def across(u, t):
        return u * n_tm + (t ^ 1)

    chip_bits = [("tm", k) for k in range(bits_of(n_tm // 2))]
    user_bits = [("user", k) for k in range(bits_of(n_user))]
    order_even = chip_bits + user_bits
    order_odd = user_bits + chip_bits

    def partner_of(level):
        def partner(u, t):
            axis, k = (order_even if t % 2 == 0 else order_odd)[level]
            if axis == "tm":
                return u * n_tm + (t ^ (2 << k))
            return (u ^ (1 << k)) * n_tm + t

        return partner

    def bit_of(level):
        def one(entry):
            axis, k = entry
            return (tm >> (k + 1)) & 1 if axis == "tm" else (user >> k) & 1

        return jnp.where(odd == 0, one(order_even[level]), one(order_odd[level])) == 1

    levels = len(order_even)
    bits = [bit_of(level) for level in range(levels)]
    size = rows // chunks
    state = []
    for leave, stay in zip(send, keep):
        got = swap(leave, across)
        extra = None
        if stay.shape[0] > size:
            extra = (stay[size:].astype(F32) + got[size:].astype(F32)).astype(BF16)
        state.append((stay[:size], got[:size], extra))
    for level in range(levels - 1):
        after = []
        for a, b, extra in state:
            size = a.shape[0] // 2
            low = a[:size].astype(F32) + b[:size].astype(F32)
            high = a[size:].astype(F32) + b[size:].astype(F32)
            leave = jnp.where(bits[level], low, high).astype(BF16)
            stay = jnp.where(bits[level], high, low).astype(BF16)
            if extra is not None:
                leave = jnp.concatenate([leave, extra], axis=0)
            got = swap(leave, partner_of(level))
            if extra is not None:
                extra = (extra.astype(F32) + got[size:].astype(F32)).astype(BF16)
            after.append((stay, got[:size], extra))
        state = after
    wholes = []
    for a, b, extra in state:
        size = a.shape[0]
        whole = (a.astype(F32) + b.astype(F32)).astype(BF16)
        if levels:
            leave = whole if extra is None else jnp.concatenate([whole, extra], axis=0)
            got = swap(leave, partner_of(levels - 1))
            whole = (whole.astype(F32) + got[:size].astype(F32)).astype(BF16)
            if extra is not None:
                extra = (extra.astype(F32) + got[size:].astype(F32)).astype(BF16)
        wholes.append((whole, extra))
    for level in reversed(range(levels - 1)):
        after = []
        for whole, extra in wholes:
            got = swap(whole, partner_of(level))
            first = jnp.where(bits[level], got, whole)
            second = jnp.where(bits[level], whole, got)
            after.append((jnp.concatenate([first, second], axis=0), extra))
        wholes = after
    arrived = []
    for whole, extra in wholes:
        arrived.append(
            swap(whole if extra is None else jnp.concatenate([whole, extra], axis=0), across)
        )
    own_extra = wholes[-1][1]
    mine = [whole for whole, _ in wholes]
    total = (2 * rows,) + mine[0].shape[1:]
    own = [(w, 0, k) for k, w in enumerate(mine)]
    other = [(w, 1, k) for k, w in enumerate(arrived)]
    grad_first, grad_second = written(None, own + other, rows, total, own_extra)
    return grad_first, grad_second.reshape(total[1:])


def written(so_far, blocks, half_rows, total, own_extra=None):
    size = blocks[0][0].shape[0]
    size -= size % LANES
    given = [value for value, _, _ in blocks]
    n = len(given)
    wide = given[-1].shape[0] > size
    aliased = so_far is not None

    def kernel(*refs):
        refs = list(refs)
        if aliased:
            refs.pop(0)
        values = [refs.pop(0) for _ in range(n)]
        mine = refs.pop(0) if wide else None
        out = refs.pop(0)
        second = refs.pop(0) if wide else None
        buf, sems = refs
        odd = lax.rem(lax.axis_index("tm"), 2)
        copies = []
        for i, (_, other, k) in enumerate(blocks):
            buf[i] = values[i][:size, :].astype(F32)
            side = 1 - odd if other else odd
            at = pl.multiple_of(side * half_rows + k * size, 8)
            copies.append(pltpu.make_async_copy(buf.at[i], out.at[pl.ds(at, size)], sems.at[i]))
            copies[i].start()
        if wide:
            own = mine[...].astype(F32)[0:1]
            got = values[-1][size:, :].astype(F32)[0:1]
            second[...] = jnp.where(odd == 1, got, own)
        for copy in copies:
            copy.wait()

    outs = [jax.ShapeDtypeStruct(total, F32)]
    if wide:
        outs.append(jax.ShapeDtypeStruct((1, total[1]), F32))
        given = given + [own_extra]
    operands = given
    if aliased:
        operands = [pltpu.with_memory_space_constraint(so_far, pltpu.HBM)] + given
    result = pl.pallas_call(
        kernel,
        out_shape=tuple(outs),
        in_specs=[HBM] * aliased + [VMEM] * len(given),
        out_specs=tuple([HBM] + [VMEM] * wide),
        scratch_shapes=[pltpu.VMEM((n, size, total[1]), F32), pltpu.SemaphoreType.DMA((n,))],
        input_output_aliases={0: 0} if aliased else {},
        compiler_params=pltpu.CompilerParams(vmem_limit_bytes=12 * 1024 * 1024),
        cost_estimate=pl.CostEstimate(
            flops=n * size * total[1], bytes_accessed=6 * n * size * total[1], transcendentals=0
        ),
    )(*operands)
    return result if wide else result[0]


def solution(mesh):
    in_specs = (
        P(("grp", "user"), "tm", None),
        P(),
        P(),
        P(),
        P(),
        P(),
        P(),
        P(),
        P(),
        P(),
        P(),
        P(("grp", "user"), "tm"),
        P(("grp", "user"), "tm"),
        P(("grp", "user"), "tm"),
        P(("grp", "user"), "tm", None),
        P(),
        P(),
    )
    out_specs = (P(("grp", "user"), "tm", None), P(("grp", "user"), "tm"), P("grp", None), P("grp"))

    return jax.shard_map(body, mesh=mesh, in_specs=in_specs, out_specs=out_specs, check_vma=False)
```

```python
import functools

import jax
import jax.numpy as jnp
from jax import lax
from jax.experimental import pallas as pl
from jax.experimental.pallas import tpu as pltpu
from jax.sharding import PartitionSpec as P


F32 = jnp.float32
BF16 = jnp.bfloat16
LANES = 128
ALIGN = 16
CHUNKS = 4
VMEM = pl.BlockSpec(memory_space=pltpu.VMEM)
SMEM = pl.BlockSpec(memory_space=pltpu.SMEM)
HBM = pl.BlockSpec(memory_space=pltpu.HBM)


def dot(a, b):
    return jnp.dot(a, b, preferred_element_type=F32)


def dot_nt(a, b):
    return lax.dot_general(a, b, (((1,), (1,)), ((), ())), preferred_element_type=F32)


def dot_tn(a, b):
    return lax.dot_general(a, b, (((0,), (0,)), ((), ())), preferred_element_type=F32)


def logistic(v):
    return 0.5 + 0.5 * jnp.tanh(0.5 * v)


def split3(v):
    high = v.astype(BF16)
    rest = v - high.astype(F32)
    mid = rest.astype(BF16)
    low = (rest - mid.astype(F32)).astype(BF16)
    return high, mid, low


def spread(cols, first_head, head_size, rows):
    lane = lax.broadcasted_iota(jnp.int32, (rows, LANES), 1)
    out = jnp.broadcast_to(cols[:, first_head : first_head + 1], (rows, LANES))
    for k in range(1, LANES // head_size):
        nxt = cols[:, first_head + k : first_head + k + 1]
        out = jnp.where(lane >= k * head_size, nxt, out)
    return out


def convolve(raw, bias, taps, cols, first, count):
    start = cols.start // LANES
    stop = cols.stop // LANES
    acc = jnp.concatenate(
        [jnp.broadcast_to(bias[k : k + 1, :], (count, LANES)) for k in range(start, stop)], axis=1
    )
    n = taps.shape[0]
    for k in range(n):
        acc = acc + taps[k : k + 1, cols] * raw[pl.ds(first - (n - 1) + k, count), cols]
    return (acc * logistic(acc)).astype(BF16)


def scan_kernel(heads, take, xbc, cum_o, dt_t, cum_t, weight_o, last_o, head_o, sum_o, raw, carried):
    hist = take(0)
    dtw, dtb, alog = take(1), take(2), take(3)
    length, width = xbc.shape
    inner = carried.shape[1]
    state = (width - inner) // 2
    head_size = inner // heads
    per = LANES // head_size

    v = dot_nt(hist[...], dtw[...]) + dtb[...]
    dt = jnp.maximum(v, 0.0) + jnp.log1p(jnp.exp(-jnp.abs(v)))
    decay = -jnp.exp(alog[...]) * dt
    ri = lax.broadcasted_iota(jnp.int32, (length, length), 0)
    ci = lax.broadcasted_iota(jnp.int32, (length, length), 1)
    tri = jnp.where(ci <= ri, 1.0, 0.0).astype(BF16)
    parts = split3(decay)
    cum = dot(tri, parts[0]) + (dot(tri, parts[1]) + dot(tri, parts[2]))
    cum_o[...] = cum
    dt_t[...] = dt.T
    cum_t[...] = cum.T
    last = cum[length - 1 : length, :]
    weight = jnp.exp(last - cum) * dt
    weight_o[...] = weight[:ALIGN]
    last_o[...] = jnp.broadcast_to(jnp.exp(last), last_o.shape)

    step = 2 * LANES
    cw, cb, w = take(4), take(5), take(6)
    raw[:ALIGN, :] = jnp.zeros((ALIGN, width), F32)
    for start in list(range(inner, width, step)) + list(range(0, inner, step)):
        cols = slice(start, start + step)
        raw[ALIGN:, cols] = dot(hist[...], w[:, cols]).astype(BF16).astype(F32)
        xbc[:, cols] = convolve(raw, cb, cw, cols, ALIGN, length)
    head_o[...] = raw[ALIGN : 2 * ALIGN, :]
    for start in range(0, inner, LANES):
        cols = slice(start, start + LANES)
        x = xbc[:, cols].astype(F32)
        carried[:, cols] = (
            spread(weight, start // LANES * per, head_size, length) * x
        ).astype(BF16)
    b = xbc[ALIGN:, inner : inner + state]
    sum_o[...] = dot_tn(b, carried[ALIGN:, :])


def edge_kernel(heads, take, halo, w, cw, cb, weight, last, head, later, old, xbc, pay, raw):
    width = xbc.shape[1]
    state, inner = later.shape
    head_size = inner // heads
    per = LANES // head_size
    before = jnp.where(lax.axis_index("tm") == 0, 0.0, halo[...].astype(F32)).astype(BF16)
    raw[:ALIGN, :] = dot(before, w[...]).astype(BF16).astype(F32)
    raw[ALIGN:, :] = head[...]
    top = convolve(raw, cb, cw, slice(0, width), ALIGN, ALIGN)
    xbc[:ALIGN, :] = top
    gain = last[...]
    pick = lax.broadcasted_iota(jnp.int32, (ALIGN, LANES), 0)
    b = top[:, inner : inner + state]
    for start in range(0, inner, LANES):
        cols = slice(start, start + LANES)
        h = start // LANES * per
        carried = (spread(weight[...], h, head_size, ALIGN) * top[:, cols].astype(F32)).astype(BF16)
        pay[:state, cols] = (later[:, cols] + dot_tn(b, carried)).astype(BF16)
        g = spread(gain, h, head_size, ALIGN)
        high = g.astype(BF16).astype(F32)
        pay[state:, cols] = jnp.where(
            pick == 0, high, jnp.where(pick == 1, g - high, 0.0)
        ).astype(BF16)


def gain_row(pay, state):
    tail = pay[state:, :].astype(F32)
    return tail[0:1, :] + tail[1:2, :]


def chip_kernel(take, mine, other, out, gain_out):
    state, half = out.shape
    odd = lax.rem(lax.axis_index("tm"), 2) == 1

    def part(ref, rows):
        return jnp.where(odd, ref[rows, half:].astype(F32), ref[rows, :half].astype(F32))

    def gain_of(ref):
        tail = part(ref, slice(state, state + ALIGN))
        return tail[0:1, :] + tail[1:2, :]

    m = part(mine, slice(0, state))
    o = part(other, slice(0, state))
    gm = gain_of(mine)
    go = gain_of(other)
    out[...] = jnp.where(odd, o * gm + m, m * go + o).astype(BF16)
    gain_out[...] = jnp.broadcast_to(gm * go, gain_out.shape)


def within_kernel(
    heads, take, d_skip, xbc, cum, dt_t, cum_t, own, across, pre, hot_o, hot_t_o, item_t_o, part
):
    length, inner = part.shape
    slots = hot_o.shape[0]
    state = (xbc.shape[1] - inner) // 2
    head_size = inner // heads
    per = LANES // head_size
    b = xbc[:, inner : inner + state]
    c = xbc[:, inner + state :]
    scores = dot_nt(c, b)
    half = length // 2
    tops = lax.broadcasted_iota(jnp.int32, (half, half), 0)
    lefts = lax.broadcasted_iota(jnp.int32, (half, half), 1)
    low_tri = lefts <= tops
    lane = lax.broadcasted_iota(jnp.int32, (length, LANES), 1)
    for start in range(0, inner, LANES):
        cols = slice(start, start + LANES)
        x = xbc[:, cols]
        out = None
        for k in range(per):
            h = start // LANES * per + k
            row = cum_t[h : h + 1, :]
            col = cum[:, h : h + 1]
            dts = dt_t[h : h + 1, :]

            def block(r, s, masked):
                gap = col[r : r + half] - row[:, s : s + half]
                if masked:
                    gap = jnp.where(low_tri, gap, 0.0)
                d = jnp.exp(gap)
                if masked:
                    d = jnp.where(low_tri, d, 0.0)
                return (d * dts[:, s : s + half] * scores[r : r + half, s : s + half]).astype(BF16)

            upper = dot(block(0, 0, True), x[:half])
            lower = dot(block(half, 0, False), x[:half]) + dot(block(half, half, True), x[half:])
            got = jnp.concatenate([upper, lower], axis=0)
            skip = d_skip[h]
            got = got + skip * x.astype(F32)
            out = got if out is None else jnp.where(lane >= k * head_size, got, out)
        part[:, cols] = out
    step = 2 * LANES
    grow = jnp.exp(cum[...])
    hist, zw = take(0), take(1)
    for start in range(0, inner, step):
        cols = slice(start, start + step)
        z = dot(hist[...], zw[:, cols]).astype(BF16).astype(F32)
        gate = z * logistic(z)
        own[:, cols] = part[:, cols] * gate
        for k in range(0, step, LANES):
            first_head = (start + k) // LANES * per
            across[:, start + k : start + k + LANES] = (
                spread(grow, first_head, head_size, length) * gate[:, k : k + LANES]
            )
    item, first = take(2), take(3)
    for start in range(0, pre.shape[1], step):
        cols = slice(start, start + step)
        pre[:, cols] = dot(item[...], first[:, cols])
    item_t_o[...] = item[...].T
    place = take(4)[...] - lax.axis_index("tm") * length
    hot = jnp.where(lax.broadcasted_iota(jnp.int32, (length, slots), 0) == place, 1.0, 0.0)
    hot_t_o[...] = hot.astype(BF16)
    hot_o[...] = hot.T.astype(BF16)


def rank_kernel(
    take,
    count,
    incoming,
    incoming_other,
    other,
    xbc,
    own,
    across,
    pre,
    hot,
    hot_t,
    item_t,
    enc_o,
    logit_o,
    gp_s,
    rank_o,
    *rest,
):
    send_o = rest[:CHUNKS]
    gated_s, rank_s, slope_s, hid_s, enc_s, enc_sem = rest[CHUNKS:]
    length, inner = own.shape
    state = incoming.shape[0]
    slots = pre.shape[0]
    tm = lax.axis_index("tm")
    odd = lax.rem(tm, 2) == 1
    half_a, half_b = incoming[...].astype(F32), incoming_other[...].astype(F32)
    arrived = jnp.concatenate(
        [jnp.where(odd, half_b, half_a), jnp.where(odd, half_a, half_b)], axis=1
    )
    arrived = jnp.where(tm < 2, 0.0, arrived)
    enter = jnp.where(
        odd, arrived * gain_row(other, state) + other[:state, :].astype(F32), arrived
    )
    entering = enter.astype(BF16)
    c = xbc[:, inner + state :]
    total = jnp.zeros((length, LANES), F32)
    for start in range(0, inner, LANES):
        cols = slice(start, start + LANES)
        read = dot(c, entering[:, cols])
        y = own[:, cols] + across[:, cols] * read
        gated_s[:, cols] = y
        total = total + y * y
    mean = jnp.sum(total, axis=1, keepdims=True) * (1.0 / inner)
    scale = lax.rsqrt(mean + 1e-05)
    gain, ow = take(0), take(1)
    normed = (gated_s[...] * scale * gain[...]).astype(BF16)
    enc = dot(normed, ow[...]).astype(BF16)
    enc_s[...] = enc
    leaving = pltpu.make_async_copy(enc_s, enc_o, enc_sem)
    leaving.start()
    width = enc.shape[1]
    rank_s[...] = dot(hot[...], enc).astype(BF16)
    rank_t = dot(enc.T, hot_t[...]).astype(BF16)

    hidden_width = pre.shape[1]
    step = 2 * LANES
    logit8 = jnp.zeros((8, slots), F32)
    first, second = take(2), take(3)
    weights2 = second[...].astype(F32)
    for start in range(0, hidden_width, step):
        cols = slice(start, start + step)
        v = pre[:, cols] + dot(rank_s[...], first[:, cols])
        sig = logistic(v)
        silu = v * sig
        hid = silu.astype(BF16)
        hid_s[:, cols] = hid
        k = start // LANES
        w2 = jnp.concatenate([weights2[k : k + 1], weights2[k + 1 : k + 2]], axis=1)
        w8 = jnp.broadcast_to(w2, (8, step)).astype(BF16)
        logit8 = logit8 + dot_nt(w8, hid)
        slope_s[:, cols] = w2 * (sig + silu * (1.0 - sig))
    slot = lax.broadcasted_iota(jnp.int32, (8, slots), 1)
    live = jnp.where(slot < count[0, 0], 1.0, 0.0)
    logit_o[...] = (live * logit8)[0:1, :]
    value = take(4)
    target = value[...].astype(F32)
    dl = live * (1.0 / (1.0 + jnp.exp(-logit8)) - target)
    d0, d1, d2 = split3(dl)
    which = lax.broadcasted_iota(jnp.int32, (8, slots), 0)
    dl3 = jnp.where(
        which == 0,
        d0.astype(F32),
        jnp.where(which == 1, d1.astype(F32), jnp.where(which == 2, d2.astype(F32), 0.0)),
    ).astype(BF16)
    grad2 = jnp.sum(dot(dl3, hid_s[...]), axis=0, keepdims=True)
    dcol = dot_tn(dl3, jnp.ones((8, LANES), BF16))
    for start in range(0, hidden_width, LANES):
        cols = slice(start, start + LANES)
        gp_s[:, cols] = (dcol * slope_s[:, cols]).astype(BF16)
    rows = width
    pick = lax.broadcasted_iota(jnp.int32, (8, hidden_width), 0)
    extra = jnp.where(pick == 0, grad2, 0.0).astype(BF16)
    away = jnp.where(odd, rank_t, item_t[...])
    rank_o[...] = rank_t
    size = rows // CHUNKS
    for k in range(CHUNKS):
        part = away[k * size : (k + 1) * size]
        send_o[k][:size, :] = dot(part, gp_s[...]).astype(BF16)
    send_o[CHUNKS - 1][size:, :] = extra
    leaving.wait()


def home_kernel(take, rank_t, item_t, slope, last_sent, *keep_o):
    size = rank_t.shape[0] // CHUNKS
    odd = lax.rem(lax.axis_index("tm"), 2) == 1
    for k in range(CHUNKS):
        part = slice(k * size, (k + 1) * size)
        home = jnp.where(odd, item_t[part, :], rank_t[part, :])
        keep_o[k][:size, :] = dot(home, slope[...]).astype(BF16)
    keep_o[CHUNKS - 1][size:, :] = last_sent[size:, :]


def chunk_shapes(rows, columns):
    size = rows // CHUNKS
    last = size + 8
    return tuple(shape((last if k == CHUNKS - 1 else size, columns), BF16) for k in range(CHUNKS))


def loading(kernel, n_loaded, n_given, n_out, windows, kept):
    def wrapped(*refs):
        sources = refs[:n_loaded]
        given = refs[n_loaded : n_loaded + n_given + n_out]
        first_kept = n_loaded + n_given + n_out
        results = list(refs[first_kept : first_kept + len(kept)])
        rest = list(refs[first_kept + len(kept) :])
        places = [results.pop(0) if i in kept else rest.pop(0) for i in range(n_loaded)]
        sems, scratch = rest[0], rest[1:]
        copies = []
        for i, source in enumerate(sources):
            window = windows.get(i)
            view = source if window is None else source.at[pl.ds(*window)]
            copies.append(pltpu.make_async_copy(view, places[i], sems.at[i]))
            copies[i].start()

        def take(i):
            copies[i].wait()
            return places[i]

        kernel(take, *given, *scratch)

    return wrapped


def call(
    kernel,
    loaded,
    given,
    out_shape,
    scratch,
    flops,
    moved,
    mib,
    windows=None,
    smem=0,
    kept=(),
    aliases=None,
    outside=(),
):
    windows = windows or {}
    places = []
    for i, value in enumerate(loaded):
        dims = value.shape if i not in windows else (windows[i][1],) + value.shape[1:]
        if i not in kept:
            places.append(pltpu.VMEM(dims, value.dtype))
    outs = tuple(out_shape) + tuple(shape(loaded[i].shape, loaded[i].dtype) for i in kept)
    return pl.pallas_call(
        loading(kernel, len(loaded), len(given), len(out_shape), windows, kept),
        out_shape=outs,
        in_specs=[HBM] * len(loaded) + [SMEM] * smem + [VMEM] * (len(given) - smem),
        out_specs=[HBM if i in outside else VMEM for i in range(len(outs))],
        scratch_shapes=places + [pltpu.SemaphoreType.DMA((max(len(loaded), 1),))] + scratch,
        compiler_params=pltpu.CompilerParams(vmem_limit_bytes=mib * 1024 * 1024),
        cost_estimate=pl.CostEstimate(flops=flops, bytes_accessed=moved, transcendentals=0),
        input_output_aliases=aliases or {},
    )(*[pltpu.with_memory_space_constraint(value, pltpu.HBM) for value in loaded], *given)


def shape(dims, dtype):
    return jax.ShapeDtypeStruct(dims, dtype)


def bits_of(n):
    return max(n.bit_length() - 1, 0)


def body(
    history,
    z_weight,
    xbc_weight,
    dt_weight,
    dt_bias,
    a_log,
    conv_weight,
    conv_bias,
    d_skip,
    norm_gain,
    out_weight,
    label_pos,
    label_count,
    label_value,
    item_feat,
    first_weight,
    second_weight,
):
    hist = history[0]
    item = item_feat[0]
    length, width = hist.shape
    inner = z_weight.shape[1]
    heads = a_log.shape[0]
    channels = xbc_weight.shape[1]
    state = (channels - inner) // 2
    slots = label_pos.shape[1]
    hidden = first_weight.shape[1]
    n_tm = lax.axis_size("tm")
    n_user = lax.axis_size("user")
    chips = n_tm // 2
    tm = lax.axis_index("tm")
    user = lax.axis_index("user")

    halo = lax.ppermute(hist[length - ALIGN :], "tm", [(i, (i + 1) % n_tm) for i in range(n_tm)])
    early, cum, dt_t, cum_t, weight, last, head, later, taps, bias, w = call(
        functools.partial(scan_kernel, heads),
        (
            hist,
            dt_weight.T,
            dt_bias.reshape(1, heads),
            a_log.reshape(1, heads),
            conv_weight,
            conv_bias.reshape(channels // LANES, LANES),
            xbc_weight,
        ),
        (),
        (
            shape((length, channels), BF16),
            shape((length, heads), F32),
            shape((heads, length), F32),
            shape((heads, length), F32),
            shape((ALIGN, heads), F32),
            shape((ALIGN, heads), F32),
            shape((ALIGN, channels), F32),
            shape((state, inner), F32),
        ),
        [pltpu.VMEM((length + ALIGN, channels), F32), pltpu.VMEM((length, inner), BF16)],
        2 * length * width * channels,
        4 * width * channels,
        16,
        kept=(4, 5, 6),
    )
    xbc, pay = call(
        functools.partial(edge_kernel, heads),
        (),
        (halo, w, taps, bias, weight, last, head, later, early),
        (shape((length, channels), BF16), shape((state + ALIGN, inner), BF16)),
        [pltpu.VMEM((2 * ALIGN, channels), F32)],
        2 * ALIGN * width * channels,
        2 * width * channels,
        10,
        aliases={8: 0},
    )
    other = lax.ppermute(pay, "tm", [(i, i ^ 1) for i in range(n_tm)])
    chip_state, chip_gain = call(
        chip_kernel,
        (),
        (pay, other),
        (shape((state, inner // 2), BF16), shape((8, inner // 2), F32)),
        [],
        state * inner,
        6 * state * inner,
        6,
    )
    onward = [(i, (i + 2) % n_tm) for i in range(n_tm)]
    incoming = lax.ppermute(chip_state, "tm", onward)
    for _ in range(chips - 2):
        incoming = jnp.where(tm < 2, 0.0, incoming.astype(F32))
        passed = chip_gain[0:1] * incoming + chip_state.astype(F32)
        incoming = lax.ppermute(passed.astype(BF16), "tm", onward)
    incoming_other = lax.ppermute(incoming, "tm", [(i, i ^ 1) for i in range(n_tm)])
    own, across, pre, hot, hot_t, item_t = call(
        functools.partial(within_kernel, heads),
        (hist, z_weight, item, first_weight, label_pos),
        (d_skip, xbc, cum, dt_t, cum_t),
        (
            shape((length, inner), F32),
            shape((length, inner), F32),
            shape((slots, hidden), F32),
            shape((slots, length), BF16),
            shape((length, slots), BF16),
            shape((width, slots), BF16),
        ),
        [pltpu.VMEM((length, inner), F32)],
        2 * length * width * inner + 2 * slots * width * hidden + 4 * length * length * inner,
        16 * length * inner * 4,
        24,
        {3: (width, width)},
        1,
    )
    enc, row_logit, slope, rank_t, *send = call(
        rank_kernel,
        (
            norm_gain.reshape(1, inner),
            out_weight,
            first_weight,
            second_weight.reshape(hidden // LANES, LANES),
            label_value,
        ),
        (label_count, incoming, incoming_other, other, xbc, own, across, pre, hot, hot_t, item_t),
        (
            shape((length, width), BF16),
            shape((1, slots), F32),
            shape((slots, hidden), BF16),
            shape((width, slots), BF16),
        )
        + chunk_shapes(width, hidden),
        [
            pltpu.VMEM((length, inner), F32),
            pltpu.VMEM((slots, width), BF16),
            pltpu.VMEM((slots, hidden), F32),
            pltpu.VMEM((slots, hidden), BF16),
            pltpu.VMEM((length, width), BF16),
            pltpu.SemaphoreType.DMA,
        ],
        4 * slots * width * hidden,
        8 * slots * hidden,
        24,
        {2: (0, width)},
        1,
        outside=(0,),
    )
    keep = call(
        home_kernel,
        (),
        (rank_t, item_t, slope, send[-1]),
        chunk_shapes(width, hidden),
        [],
        2 * slots * width * hidden,
        4 * slots * hidden,
        8,
    )
    grad_first, grad_second = total_sum(send, keep, n_user, n_tm, user, tm)
    return (enc[None], row_logit, grad_first, grad_second)


def total_sum(send, keep, n_user, n_tm, user, tm):
    rows = sum(part.shape[0] for part in keep) - 8
    odd = tm % 2
    axes = ("user", "tm")
    every = [(u, t) for u in range(n_user) for t in range(n_tm)]
    chunks = CHUNKS

    def swap(value, partner):
        pairs = [(u * n_tm + t, partner(u, t)) for u, t in every]
        return lax.ppermute(value, axes, pairs)

    def across(u, t):
        return u * n_tm + (t ^ 1)

    chip_bits = [("tm", k) for k in range(bits_of(n_tm // 2))]
    user_bits = [("user", k) for k in range(bits_of(n_user))]
    order_even = chip_bits + user_bits
    order_odd = user_bits + chip_bits

    def partner_of(level):
        def partner(u, t):
            axis, k = (order_even if t % 2 == 0 else order_odd)[level]
            if axis == "tm":
                return u * n_tm + (t ^ (2 << k))
            return (u ^ (1 << k)) * n_tm + t

        return partner

    def bit_of(level):
        def one(entry):
            axis, k = entry
            return (tm >> (k + 1)) & 1 if axis == "tm" else (user >> k) & 1

        return jnp.where(odd == 0, one(order_even[level]), one(order_odd[level])) == 1

    levels = len(order_even)
    bits = [bit_of(level) for level in range(levels)]
    size = rows // chunks
    state = []
    for leave, stay in zip(send, keep):
        got = swap(leave, across)
        extra = None
        if stay.shape[0] > size:
            extra = (stay[size:].astype(F32) + got[size:].astype(F32)).astype(BF16)
        state.append((stay[:size], got[:size], extra))
    for level in range(levels - 1):
        after = []
        for a, b, extra in state:
            size = a.shape[0] // 2
            low = a[:size].astype(F32) + b[:size].astype(F32)
            high = a[size:].astype(F32) + b[size:].astype(F32)
            leave = jnp.where(bits[level], low, high).astype(BF16)
            stay = jnp.where(bits[level], high, low).astype(BF16)
            if extra is not None:
                leave = jnp.concatenate([leave, extra], axis=0)
            got = swap(leave, partner_of(level))
            if extra is not None:
                extra = (extra.astype(F32) + got[size:].astype(F32)).astype(BF16)
            after.append((stay, got[:size], extra))
        state = after
    wholes = []
    for a, b, extra in state:
        size = a.shape[0]
        whole = (a.astype(F32) + b.astype(F32)).astype(BF16)
        if levels:
            leave = whole if extra is None else jnp.concatenate([whole, extra], axis=0)
            got = swap(leave, partner_of(levels - 1))
            whole = (whole.astype(F32) + got[:size].astype(F32)).astype(BF16)
            if extra is not None:
                extra = (extra.astype(F32) + got[size:].astype(F32)).astype(BF16)
        wholes.append((whole, extra))
    for level in reversed(range(levels - 1)):
        after = []
        for whole, extra in wholes:
            got = swap(whole, partner_of(level))
            first = jnp.where(bits[level], got, whole)
            second = jnp.where(bits[level], whole, got)
            after.append((jnp.concatenate([first, second], axis=0), extra))
        wholes = after
    arrived = []
    for whole, extra in wholes:
        leave = whole if extra is None else jnp.concatenate([whole, extra], axis=0)
        arrived.append(swap(leave, across))
    own_extra = wholes[-1][1]
    mine = [whole for whole, _ in wholes]
    total = (2 * rows,) + mine[0].shape[1:]
    last = chunks - 1
    own = [(w, 0, k) for k, w in enumerate(mine)]
    other = [(w, 1, k) for k, w in enumerate(arrived)]
    grad_first = written(None, own[:last] + own[last:] + other[1:last], rows, total)
    grad_first, grad_second = written(grad_first, [other[0], other[last]], rows, total, own_extra)
    return grad_first, grad_second.reshape(total[1:])


def written(so_far, blocks, half_rows, total, own_extra=None):
    size = blocks[0][0].shape[0]
    size -= size % LANES
    given = [value for value, _, _ in blocks]
    n = len(given)
    wide = given[-1].shape[0] > size
    aliased = so_far is not None

    def kernel(*refs):
        refs = list(refs)
        if aliased:
            refs.pop(0)
        values = [refs.pop(0) for _ in range(n)]
        mine = refs.pop(0) if wide else None
        out = refs.pop(0)
        second = refs.pop(0) if wide else None
        buf, sems = refs
        odd = lax.rem(lax.axis_index("tm"), 2)
        copies = []
        for i, (_, other, k) in enumerate(blocks):
            buf[i] = values[i][:size, :].astype(F32)
            side = 1 - odd if other else odd
            at = pl.multiple_of(side * half_rows + k * size, 8)
            copies.append(pltpu.make_async_copy(buf.at[i], out.at[pl.ds(at, size)], sems.at[i]))
            copies[i].start()
        if wide:
            own = mine[...].astype(F32)[0:1]
            got = values[-1][size:, :].astype(F32)[0:1]
            second[...] = jnp.where(odd == 1, got, own)
        for copy in copies:
            copy.wait()

    outs = [jax.ShapeDtypeStruct(total, F32)]
    if wide:
        outs.append(jax.ShapeDtypeStruct((1, total[1]), F32))
        given = given + [own_extra]
    operands = given
    if aliased:
        operands = [pltpu.with_memory_space_constraint(so_far, pltpu.HBM)] + given
    result = pl.pallas_call(
        kernel,
        out_shape=tuple(outs),
        in_specs=[HBM] * aliased + [VMEM] * len(given),
        out_specs=tuple([HBM] + [VMEM] * wide),
        scratch_shapes=[pltpu.VMEM((n, size, total[1]), F32), pltpu.SemaphoreType.DMA((n,))],
        input_output_aliases={0: 0} if aliased else {},
        compiler_params=pltpu.CompilerParams(vmem_limit_bytes=12 * 1024 * 1024),
        cost_estimate=pl.CostEstimate(
            flops=n * size * total[1], bytes_accessed=6 * n * size * total[1], transcendentals=0
        ),
    )(*operands)
    return result if wide else result[0]


def solution(mesh):
    in_specs = (
        P(("grp", "user"), "tm", None),
        P(),
        P(),
        P(),
        P(),
        P(),
        P(),
        P(),
        P(),
        P(),
        P(),
        P(("grp", "user"), "tm"),
        P(("grp", "user"), "tm"),
        P(("grp", "user"), "tm"),
        P(("grp", "user"), "tm", None),
        P(),
        P(),
    )
    out_specs = (P(("grp", "user"), "tm", None), P(("grp", "user"), "tm"), P("grp", None), P("grp"))

    return jax.shard_map(body, mesh=mesh, in_specs=in_specs, out_specs=out_specs, check_vma=False)
```

```python
import functools

import jax
import jax.numpy as jnp
from jax import lax
from jax.experimental import pallas as pl
from jax.experimental.pallas import tpu as pltpu
from jax.sharding import PartitionSpec as P


F32 = jnp.float32
BF16 = jnp.bfloat16
LANES = 128
ALIGN = 16
CHUNKS = 4
VMEM = pl.BlockSpec(memory_space=pltpu.VMEM)
SMEM = pl.BlockSpec(memory_space=pltpu.SMEM)
HBM = pl.BlockSpec(memory_space=pltpu.HBM)


def dot(a, b):
    return jnp.dot(a, b, preferred_element_type=F32)


def dot_nt(a, b):
    return lax.dot_general(a, b, (((1,), (1,)), ((), ())), preferred_element_type=F32)


def dot_tn(a, b):
    return lax.dot_general(a, b, (((0,), (0,)), ((), ())), preferred_element_type=F32)


def logistic(v):
    return 0.5 + 0.5 * jnp.tanh(0.5 * v)


def split3(v):
    high = v.astype(BF16)
    rest = v - high.astype(F32)
    mid = rest.astype(BF16)
    low = (rest - mid.astype(F32)).astype(BF16)
    return high, mid, low


def spread(cols, first_head, head_size, rows):
    lane = lax.broadcasted_iota(jnp.int32, (rows, LANES), 1)
    out = jnp.broadcast_to(cols[:, first_head : first_head + 1], (rows, LANES))
    for k in range(1, LANES // head_size):
        nxt = cols[:, first_head + k : first_head + k + 1]
        out = jnp.where(lane >= k * head_size, nxt, out)
    return out


def convolve(raw, bias, taps, cols, first, count):
    start = cols.start // LANES
    stop = cols.stop // LANES
    acc = jnp.concatenate(
        [jnp.broadcast_to(bias[k : k + 1, :], (count, LANES)) for k in range(start, stop)], axis=1
    )
    n = taps.shape[0]
    for k in range(n):
        acc = acc + taps[k : k + 1, cols] * raw[pl.ds(first - (n - 1) + k, count), cols]
    return (acc * logistic(acc)).astype(BF16)


def scan_kernel(heads, take, xbc, cum_o, dt_t, cum_t, weight_o, last_o, head_o, sum_o, raw, carried):
    hist = take(0)
    dtw, dtb, alog = take(1), take(2), take(3)
    length, width = xbc.shape
    inner = carried.shape[1]
    state = (width - inner) // 2
    head_size = inner // heads
    per = LANES // head_size

    v = dot_nt(hist[...], dtw[...]) + dtb[...]
    dt = jnp.maximum(v, 0.0) + jnp.log1p(jnp.exp(-jnp.abs(v)))
    decay = -jnp.exp(alog[...]) * dt
    ri = lax.broadcasted_iota(jnp.int32, (length, length), 0)
    ci = lax.broadcasted_iota(jnp.int32, (length, length), 1)
    tri = jnp.where(ci <= ri, 1.0, 0.0).astype(BF16)
    parts = split3(decay)
    cum = dot(tri, parts[0]) + (dot(tri, parts[1]) + dot(tri, parts[2]))
    cum_o[...] = cum
    dt_t[...] = dt.T
    cum_t[...] = cum.T
    last = cum[length - 1 : length, :]
    weight = jnp.exp(last - cum) * dt
    weight_o[...] = weight[:ALIGN]
    last_o[...] = jnp.broadcast_to(jnp.exp(last), last_o.shape)

    step = 2 * LANES
    cw, cb, w = take(4), take(5), take(6)
    raw[:ALIGN, :] = jnp.zeros((ALIGN, width), F32)
    for start in list(range(inner, width, step)) + list(range(0, inner, step)):
        cols = slice(start, start + step)
        raw[ALIGN:, cols] = dot(hist[...], w[:, cols]).astype(BF16).astype(F32)
        xbc[:, cols] = convolve(raw, cb, cw, cols, ALIGN, length)
    head_o[...] = raw[ALIGN : 2 * ALIGN, :]
    for start in range(0, inner, LANES):
        cols = slice(start, start + LANES)
        x = xbc[:, cols].astype(F32)
        carried[:, cols] = (
            spread(weight, start // LANES * per, head_size, length) * x
        ).astype(BF16)
    b = xbc[ALIGN:, inner : inner + state]
    sum_o[...] = dot_tn(b, carried[ALIGN:, :])


def edge_kernel(heads, take, halo, w, cw, cb, weight, last, head, later, old, xbc, pay, raw):
    width = xbc.shape[1]
    state, inner = later.shape
    head_size = inner // heads
    per = LANES // head_size
    before = jnp.where(lax.axis_index("tm") == 0, 0.0, halo[...].astype(F32)).astype(BF16)
    raw[:ALIGN, :] = dot(before, w[...]).astype(BF16).astype(F32)
    raw[ALIGN:, :] = head[...]
    top = convolve(raw, cb, cw, slice(0, width), ALIGN, ALIGN)
    xbc[:ALIGN, :] = top
    gain = last[...]
    pick = lax.broadcasted_iota(jnp.int32, (ALIGN, LANES), 0)
    b = top[:, inner : inner + state]
    for start in range(0, inner, LANES):
        cols = slice(start, start + LANES)
        h = start // LANES * per
        carried = (spread(weight[...], h, head_size, ALIGN) * top[:, cols].astype(F32)).astype(BF16)
        pay[:state, cols] = (later[:, cols] + dot_tn(b, carried)).astype(BF16)
        g = spread(gain, h, head_size, ALIGN)
        high = g.astype(BF16).astype(F32)
        pay[state:, cols] = jnp.where(
            pick == 0, high, jnp.where(pick == 1, g - high, 0.0)
        ).astype(BF16)


def gain_row(pay, state):
    tail = pay[state:, :].astype(F32)
    return tail[0:1, :] + tail[1:2, :]


def chip_kernel(take, mine, other, out, gain_out):
    state, half = out.shape
    odd = lax.rem(lax.axis_index("tm"), 2) == 1

    def part(ref, rows):
        return jnp.where(odd, ref[rows, half:].astype(F32), ref[rows, :half].astype(F32))

    def gain_of(ref):
        tail = part(ref, slice(state, state + ALIGN))
        return tail[0:1, :] + tail[1:2, :]

    m = part(mine, slice(0, state))
    o = part(other, slice(0, state))
    gm = gain_of(mine)
    go = gain_of(other)
    out[...] = jnp.where(odd, o * gm + m, m * go + o).astype(BF16)
    gain_out[...] = jnp.broadcast_to(gm * go, gain_out.shape)


def within_kernel(
    heads, take, d_skip, xbc, cum, dt_t, cum_t, own, across, pre, hot_o, hot_t_o, item_t_o, part
):
    length, inner = part.shape
    slots = hot_o.shape[0]
    state = (xbc.shape[1] - inner) // 2
    head_size = inner // heads
    per = LANES // head_size
    b = xbc[:, inner : inner + state]
    c = xbc[:, inner + state :]
    scores = dot_nt(c, b)
    half = length // 2
    tops = lax.broadcasted_iota(jnp.int32, (half, half), 0)
    lefts = lax.broadcasted_iota(jnp.int32, (half, half), 1)
    low_tri = lefts <= tops
    lane = lax.broadcasted_iota(jnp.int32, (length, LANES), 1)
    for start in range(0, inner, LANES):
        cols = slice(start, start + LANES)
        x = xbc[:, cols]
        out = None
        for k in range(per):
            h = start // LANES * per + k
            row = cum_t[h : h + 1, :]
            col = cum[:, h : h + 1]
            dts = dt_t[h : h + 1, :]

            def block(r, s, masked):
                gap = col[r : r + half] - row[:, s : s + half]
                if masked:
                    gap = jnp.where(low_tri, gap, 0.0)
                d = jnp.exp(gap)
                if masked:
                    d = jnp.where(low_tri, d, 0.0)
                return (d * dts[:, s : s + half] * scores[r : r + half, s : s + half]).astype(BF16)

            upper = dot(block(0, 0, True), x[:half])
            lower = dot(block(half, 0, False), x[:half]) + dot(block(half, half, True), x[half:])
            got = jnp.concatenate([upper, lower], axis=0)
            skip = d_skip[h]
            got = got + skip * x.astype(F32)
            out = got if out is None else jnp.where(lane >= k * head_size, got, out)
        part[:, cols] = out
    step = 2 * LANES
    grow = jnp.exp(cum[...])
    hist, zw = take(0), take(1)
    for start in range(0, inner, step):
        cols = slice(start, start + step)
        z = dot(hist[...], zw[:, cols]).astype(BF16).astype(F32)
        gate = z * logistic(z)
        own[:, cols] = part[:, cols] * gate
        for k in range(0, step, LANES):
            first_head = (start + k) // LANES * per
            across[:, start + k : start + k + LANES] = (
                spread(grow, first_head, head_size, length) * gate[:, k : k + LANES]
            )
    item, first = take(2), take(3)
    for start in range(0, pre.shape[1], step):
        cols = slice(start, start + step)
        pre[:, cols] = dot(item[...], first[:, cols])
    item_t_o[...] = item[...].T
    place = take(4)[...] - lax.axis_index("tm") * length
    hot = jnp.where(lax.broadcasted_iota(jnp.int32, (length, slots), 0) == place, 1.0, 0.0)
    hot_t_o[...] = hot.astype(BF16)
    hot_o[...] = hot.T.astype(BF16)


def rank_kernel(
    take,
    count,
    incoming,
    incoming_other,
    other,
    xbc,
    own,
    across,
    pre,
    hot,
    hot_t,
    item_t,
    enc_o,
    logit_o,
    gp_s,
    rank_o,
    *rest,
):
    send_o = rest[:CHUNKS]
    gated_s, rank_s, slope_s, hid_s, enc_s, enc_sem = rest[CHUNKS:]
    length, inner = own.shape
    state = incoming.shape[0]
    slots = pre.shape[0]
    tm = lax.axis_index("tm")
    odd = lax.rem(tm, 2) == 1
    half_a, half_b = incoming[...].astype(F32), incoming_other[...].astype(F32)
    arrived = jnp.concatenate(
        [jnp.where(odd, half_b, half_a), jnp.where(odd, half_a, half_b)], axis=1
    )
    arrived = jnp.where(tm < 2, 0.0, arrived)
    enter = jnp.where(
        odd, arrived * gain_row(other, state) + other[:state, :].astype(F32), arrived
    )
    entering = enter.astype(BF16)
    c = xbc[:, inner + state :]
    total = jnp.zeros((length, LANES), F32)
    for start in range(0, inner, LANES):
        cols = slice(start, start + LANES)
        read = dot(c, entering[:, cols])
        y = own[:, cols] + across[:, cols] * read
        gated_s[:, cols] = y
        total = total + y * y
    mean = jnp.sum(total, axis=1, keepdims=True) * (1.0 / inner)
    scale = lax.rsqrt(mean + 1e-05)
    gain, ow = take(0), take(1)
    normed = (gated_s[...] * scale * gain[...]).astype(BF16)
    enc = dot(normed, ow[...]).astype(BF16)
    enc_s[...] = enc
    leaving = pltpu.make_async_copy(enc_s, enc_o, enc_sem)
    leaving.start()
    width = enc.shape[1]
    rank_s[...] = dot(hot[...], enc).astype(BF16)
    rank_t = dot(enc.T, hot_t[...]).astype(BF16)

    hidden_width = pre.shape[1]
    step = 2 * LANES
    logit = jnp.zeros((slots, LANES), F32)
    first, second = take(2), take(3)
    weights2 = second[...].astype(F32)
    for start in range(0, hidden_width, step):
        cols = slice(start, start + step)
        v = pre[:, cols] + dot(rank_s[...], first[:, cols])
        sig = logistic(v)
        silu = v * sig
        hid = silu.astype(BF16)
        hid_s[:, cols] = hid
        k = start // LANES
        w2 = jnp.concatenate([weights2[k : k + 1], weights2[k + 1 : k + 2]], axis=1)
        prod = hid.astype(F32) * w2
        for k in range(0, step, LANES):
            logit = logit + prod[:, k : k + LANES]
        slope_s[:, cols] = w2 * (sig + silu * (1.0 - sig))
    ones = jnp.ones((8, LANES), BF16)
    p = split3(logit)
    logit8 = dot_nt(ones, p[0]) + (dot_nt(ones, p[1]) + dot_nt(ones, p[2]))
    slot = lax.broadcasted_iota(jnp.int32, (8, slots), 1)
    live = jnp.where(slot < count[0, 0], 1.0, 0.0)
    logit_o[...] = (live * logit8)[0:1, :]
    value = take(4)
    target = value[...].astype(F32)
    dl = live * (1.0 / (1.0 + jnp.exp(-logit8)) - target)
    d0, d1, d2 = split3(dl)
    which = lax.broadcasted_iota(jnp.int32, (8, slots), 0)
    dl3 = jnp.where(
        which == 0,
        d0.astype(F32),
        jnp.where(which == 1, d1.astype(F32), jnp.where(which == 2, d2.astype(F32), 0.0)),
    ).astype(BF16)
    grad2 = jnp.sum(dot(dl3, hid_s[...]), axis=0, keepdims=True)
    dcol = dot_tn(dl3, jnp.ones((8, LANES), BF16))
    for start in range(0, hidden_width, LANES):
        cols = slice(start, start + LANES)
        gp_s[:, cols] = (dcol * slope_s[:, cols]).astype(BF16)
    rows = width
    pick = lax.broadcasted_iota(jnp.int32, (8, hidden_width), 0)
    extra = jnp.where(pick == 0, grad2, 0.0).astype(BF16)
    away = jnp.where(odd, rank_t, item_t[...])
    rank_o[...] = rank_t
    size = rows // CHUNKS
    for k in range(CHUNKS):
        part = away[k * size : (k + 1) * size]
        send_o[k][:size, :] = dot(part, gp_s[...]).astype(BF16)
    send_o[CHUNKS - 1][size:, :] = extra
    leaving.wait()


def home_kernel(take, rank_t, item_t, slope, last_sent, *keep_o):
    size = rank_t.shape[0] // CHUNKS
    odd = lax.rem(lax.axis_index("tm"), 2) == 1
    for k in range(CHUNKS):
        part = slice(k * size, (k + 1) * size)
        home = jnp.where(odd, item_t[part, :], rank_t[part, :])
        keep_o[k][:size, :] = dot(home, slope[...]).astype(BF16)
    keep_o[CHUNKS - 1][size:, :] = last_sent[size:, :]


def chunk_shapes(rows, columns):
    size = rows // CHUNKS
    last = size + 8
    return tuple(shape((last if k == CHUNKS - 1 else size, columns), BF16) for k in range(CHUNKS))


def loading(kernel, n_loaded, n_given, n_out, windows, kept):
    def wrapped(*refs):
        sources = refs[:n_loaded]
        given = refs[n_loaded : n_loaded + n_given + n_out]
        first_kept = n_loaded + n_given + n_out
        results = list(refs[first_kept : first_kept + len(kept)])
        rest = list(refs[first_kept + len(kept) :])
        places = [results.pop(0) if i in kept else rest.pop(0) for i in range(n_loaded)]
        sems, scratch = rest[0], rest[1:]
        copies = []
        for i, source in enumerate(sources):
            window = windows.get(i)
            view = source if window is None else source.at[pl.ds(*window)]
            copies.append(pltpu.make_async_copy(view, places[i], sems.at[i]))
            copies[i].start()

        def take(i):
            copies[i].wait()
            return places[i]

        kernel(take, *given, *scratch)

    return wrapped


def call(
    kernel,
    loaded,
    given,
    out_shape,
    scratch,
    flops,
    moved,
    mib,
    windows=None,
    smem=0,
    kept=(),
    aliases=None,
    outside=(),
):
    windows = windows or {}
    places = []
    for i, value in enumerate(loaded):
        dims = value.shape if i not in windows else (windows[i][1],) + value.shape[1:]
        if i not in kept:
            places.append(pltpu.VMEM(dims, value.dtype))
    outs = tuple(out_shape) + tuple(shape(loaded[i].shape, loaded[i].dtype) for i in kept)
    return pl.pallas_call(
        loading(kernel, len(loaded), len(given), len(out_shape), windows, kept),
        out_shape=outs,
        in_specs=[HBM] * len(loaded) + [SMEM] * smem + [VMEM] * (len(given) - smem),
        out_specs=[HBM if i in outside else VMEM for i in range(len(outs))],
        scratch_shapes=places + [pltpu.SemaphoreType.DMA((max(len(loaded), 1),))] + scratch,
        compiler_params=pltpu.CompilerParams(vmem_limit_bytes=mib * 1024 * 1024),
        cost_estimate=pl.CostEstimate(flops=flops, bytes_accessed=moved, transcendentals=0),
        input_output_aliases=aliases or {},
    )(*[pltpu.with_memory_space_constraint(value, pltpu.HBM) for value in loaded], *given)


def shape(dims, dtype):
    return jax.ShapeDtypeStruct(dims, dtype)


def bits_of(n):
    return max(n.bit_length() - 1, 0)


def body(
    history,
    z_weight,
    xbc_weight,
    dt_weight,
    dt_bias,
    a_log,
    conv_weight,
    conv_bias,
    d_skip,
    norm_gain,
    out_weight,
    label_pos,
    label_count,
    label_value,
    item_feat,
    first_weight,
    second_weight,
):
    hist = history[0]
    item = item_feat[0]
    length, width = hist.shape
    inner = z_weight.shape[1]
    heads = a_log.shape[0]
    channels = xbc_weight.shape[1]
    state = (channels - inner) // 2
    slots = label_pos.shape[1]
    hidden = first_weight.shape[1]
    n_tm = lax.axis_size("tm")
    n_user = lax.axis_size("user")
    chips = n_tm // 2
    tm = lax.axis_index("tm")
    user = lax.axis_index("user")

    halo = lax.ppermute(hist[length - ALIGN :], "tm", [(i, (i + 1) % n_tm) for i in range(n_tm)])
    early, cum, dt_t, cum_t, weight, last, head, later, taps, bias, w = call(
        functools.partial(scan_kernel, heads),
        (
            hist,
            dt_weight.T,
            dt_bias.reshape(1, heads),
            a_log.reshape(1, heads),
            conv_weight,
            conv_bias.reshape(channels // LANES, LANES),
            xbc_weight,
        ),
        (),
        (
            shape((length, channels), BF16),
            shape((length, heads), F32),
            shape((heads, length), F32),
            shape((heads, length), F32),
            shape((ALIGN, heads), F32),
            shape((ALIGN, heads), F32),
            shape((ALIGN, channels), F32),
            shape((state, inner), F32),
        ),
        [pltpu.VMEM((length + ALIGN, channels), F32), pltpu.VMEM((length, inner), BF16)],
        2 * length * width * channels,
        4 * width * channels,
        16,
        kept=(4, 5, 6),
    )
    xbc, pay = call(
        functools.partial(edge_kernel, heads),
        (),
        (halo, w, taps, bias, weight, last, head, later, early),
        (shape((length, channels), BF16), shape((state + ALIGN, inner), BF16)),
        [pltpu.VMEM((2 * ALIGN, channels), F32)],
        2 * ALIGN * width * channels,
        2 * width * channels,
        10,
        aliases={8: 0},
    )
    other = lax.ppermute(pay, "tm", [(i, i ^ 1) for i in range(n_tm)])
    chip_state, chip_gain = call(
        chip_kernel,
        (),
        (pay, other),
        (shape((state, inner // 2), BF16), shape((8, inner // 2), F32)),
        [],
        state * inner,
        6 * state * inner,
        6,
    )
    onward = [(i, (i + 2) % n_tm) for i in range(n_tm)]
    incoming = lax.ppermute(chip_state, "tm", onward)
    for _ in range(chips - 2):
        incoming = jnp.where(tm < 2, 0.0, incoming.astype(F32))
        passed = chip_gain[0:1] * incoming + chip_state.astype(F32)
        incoming = lax.ppermute(passed.astype(BF16), "tm", onward)
    incoming_other = lax.ppermute(incoming, "tm", [(i, i ^ 1) for i in range(n_tm)])
    own, across, pre, hot, hot_t, item_t = call(
        functools.partial(within_kernel, heads),
        (hist, z_weight, item, first_weight, label_pos),
        (d_skip, xbc, cum, dt_t, cum_t),
        (
            shape((length, inner), F32),
            shape((length, inner), F32),
            shape((slots, hidden), F32),
            shape((slots, length), BF16),
            shape((length, slots), BF16),
            shape((width, slots), BF16),
        ),
        [pltpu.VMEM((length, inner), F32)],
        2 * length * width * inner + 2 * slots * width * hidden + 4 * length * length * inner,
        16 * length * inner * 4,
        24,
        {3: (width, width)},
        1,
    )
    enc, row_logit, slope, rank_t, *send = call(
        rank_kernel,
        (
            norm_gain.reshape(1, inner),
            out_weight,
            first_weight,
            second_weight.reshape(hidden // LANES, LANES),
            label_value,
        ),
        (label_count, incoming, incoming_other, other, xbc, own, across, pre, hot, hot_t, item_t),
        (
            shape((length, width), BF16),
            shape((1, slots), F32),
            shape((slots, hidden), BF16),
            shape((width, slots), BF16),
        )
        + chunk_shapes(width, hidden),
        [
            pltpu.VMEM((length, inner), F32),
            pltpu.VMEM((slots, width), BF16),
            pltpu.VMEM((slots, hidden), F32),
            pltpu.VMEM((slots, hidden), BF16),
            pltpu.VMEM((length, width), BF16),
            pltpu.SemaphoreType.DMA,
        ],
        4 * slots * width * hidden,
        8 * slots * hidden,
        24,
        {2: (0, width)},
        1,
        outside=(0,),
    )
    keep = call(
        home_kernel,
        (),
        (rank_t, item_t, slope, send[-1]),
        chunk_shapes(width, hidden),
        [],
        2 * slots * width * hidden,
        4 * slots * hidden,
        8,
    )
    grad_first, grad_second = total_sum(send, keep, n_user, n_tm, user, tm)
    return (enc[None], row_logit, grad_first, grad_second)


def total_sum(send, keep, n_user, n_tm, user, tm):
    rows = sum(part.shape[0] for part in keep) - 8
    odd = tm % 2
    axes = ("user", "tm")
    every = [(u, t) for u in range(n_user) for t in range(n_tm)]
    chunks = CHUNKS

    def swap(value, partner):
        pairs = [(u * n_tm + t, partner(u, t)) for u, t in every]
        return lax.ppermute(value, axes, pairs)

    def across(u, t):
        return u * n_tm + (t ^ 1)

    chip_bits = [("tm", k) for k in range(bits_of(n_tm // 2))]
    user_bits = [("user", k) for k in range(bits_of(n_user))]
    chip_first = chip_bits + user_bits
    user_first = user_bits + chip_bits
    mixed = (chip_first, user_first)
    alike = (chip_first, chip_first)
    orders = [mixed, mixed, alike, mixed]

    def partner_of(level, chunk):
        def partner(u, t):
            axis, k = orders[chunk][t % 2][level]
            if axis == "tm":
                return u * n_tm + (t ^ (2 << k))
            return (u ^ (1 << k)) * n_tm + t

        return partner

    def bit_of(level, chunk):
        def one(entry):
            axis, k = entry
            return (tm >> (k + 1)) & 1 if axis == "tm" else (user >> k) & 1

        even_one, odd_one = (one(order[level]) for order in orders[chunk])
        return jnp.where(odd == 0, even_one, odd_one) == 1

    levels = len(chip_first)
    bits = [[bit_of(level, chunk) for chunk in range(chunks)] for level in range(levels)]
    size = rows // chunks
    state = []
    for leave, stay in zip(send, keep):
        got = swap(leave, across)
        extra = None
        if stay.shape[0] > size:
            extra = (stay[size:].astype(F32) + got[size:].astype(F32)).astype(BF16)
        state.append((stay[:size], got[:size], extra))
    for level in range(levels - 1):
        after = []
        for chunk, (a, b, extra) in enumerate(state):
            size = a.shape[0] // 2
            low = a[:size].astype(F32) + b[:size].astype(F32)
            high = a[size:].astype(F32) + b[size:].astype(F32)
            leave = jnp.where(bits[level][chunk], low, high).astype(BF16)
            stay = jnp.where(bits[level][chunk], high, low).astype(BF16)
            if extra is not None:
                leave = jnp.concatenate([leave, extra], axis=0)
            got = swap(leave, partner_of(level, chunk))
            if extra is not None:
                extra = (extra.astype(F32) + got[size:].astype(F32)).astype(BF16)
            after.append((stay, got[:size], extra))
        state = after
    wholes = []
    for chunk, (a, b, extra) in enumerate(state):
        size = a.shape[0]
        whole = (a.astype(F32) + b.astype(F32)).astype(BF16)
        if levels:
            leave = whole if extra is None else jnp.concatenate([whole, extra], axis=0)
            got = swap(leave, partner_of(levels - 1, chunk))
            whole = (whole.astype(F32) + got[:size].astype(F32)).astype(BF16)
            if extra is not None:
                extra = (extra.astype(F32) + got[size:].astype(F32)).astype(BF16)
        wholes.append((whole, extra))
    for level in reversed(range(levels - 1)):
        after = []
        for chunk, (whole, extra) in enumerate(wholes):
            got = swap(whole, partner_of(level, chunk))
            first = jnp.where(bits[level][chunk], got, whole)
            second = jnp.where(bits[level][chunk], whole, got)
            after.append((jnp.concatenate([first, second], axis=0), extra))
        wholes = after
    arrived = []
    for whole, extra in wholes:
        leave = whole if extra is None else jnp.concatenate([whole, extra], axis=0)
        arrived.append(swap(leave, across))
    own_extra = wholes[-1][1]
    mine = [whole for whole, _ in wholes]
    total = (2 * rows,) + mine[0].shape[1:]
    last = chunks - 1
    own = [(w, 0, k) for k, w in enumerate(mine)]
    other = [(w, 1, k) for k, w in enumerate(arrived)]
    grad_first = written(None, own[:last] + own[last:] + other[1:last], rows, total)
    grad_first, grad_second = written(grad_first, [other[0], other[last]], rows, total, own_extra)
    return grad_first, grad_second.reshape(total[1:])


def written(so_far, blocks, half_rows, total, own_extra=None):
    size = blocks[0][0].shape[0]
    size -= size % LANES
    given = [value for value, _, _ in blocks]
    n = len(given)
    wide = given[-1].shape[0] > size
    aliased = so_far is not None

    def kernel(*refs):
        refs = list(refs)
        if aliased:
            refs.pop(0)
        values = [refs.pop(0) for _ in range(n)]
        mine = refs.pop(0) if wide else None
        out = refs.pop(0)
        second = refs.pop(0) if wide else None
        buf, sems = refs
        odd = lax.rem(lax.axis_index("tm"), 2)
        copies = []
        for i, (_, other, k) in enumerate(blocks):
            buf[i] = values[i][:size, :].astype(F32)
            side = 1 - odd if other else odd
            at = pl.multiple_of(side * half_rows + k * size, 8)
            copies.append(pltpu.make_async_copy(buf.at[i], out.at[pl.ds(at, size)], sems.at[i]))
            copies[i].start()
        if wide:
            own = mine[...].astype(F32)[0:1]
            got = values[-1][size:, :].astype(F32)[0:1]
            second[...] = jnp.where(odd == 1, got, own)
        for copy in copies:
            copy.wait()

    outs = [jax.ShapeDtypeStruct(total, F32)]
    if wide:
        outs.append(jax.ShapeDtypeStruct((1, total[1]), F32))
        given = given + [own_extra]
    operands = given
    if aliased:
        operands = [pltpu.with_memory_space_constraint(so_far, pltpu.HBM)] + given
    result = pl.pallas_call(
        kernel,
        out_shape=tuple(outs),
        in_specs=[HBM] * aliased + [VMEM] * len(given),
        out_specs=tuple([HBM] + [VMEM] * wide),
        scratch_shapes=[pltpu.VMEM((n, size, total[1]), F32), pltpu.SemaphoreType.DMA((n,))],
        input_output_aliases={0: 0} if aliased else {},
        compiler_params=pltpu.CompilerParams(vmem_limit_bytes=12 * 1024 * 1024),
        cost_estimate=pl.CostEstimate(
            flops=n * size * total[1], bytes_accessed=6 * n * size * total[1], transcendentals=0
        ),
    )(*operands)
    return result if wide else result[0]


def solution(mesh):
    in_specs = (
        P(("grp", "user"), "tm", None),
        P(),
        P(),
        P(),
        P(),
        P(),
        P(),
        P(),
        P(),
        P(),
        P(),
        P(("grp", "user"), "tm"),
        P(("grp", "user"), "tm"),
        P(("grp", "user"), "tm"),
        P(("grp", "user"), "tm", None),
        P(),
        P(),
    )
    out_specs = (P(("grp", "user"), "tm", None), P(("grp", "user"), "tm"), P("grp", None), P("grp"))

    return jax.shard_map(body, mesh=mesh, in_specs=in_specs, out_specs=out_specs, check_vma=False)
```
